128 devices in a mesh: bx: 8 (over y, core), by: 16 (over z, x).
Axes of the slice: x: 4, y: 4, z: 4, core: 2. Of those that a mesh axis runs over, the one named last changes fastest.
Arguments:
- point_box: int32 [262144, 1], P(('bx', 'by')), may hold values from 0 to 127; in each aligned block of 2048 rows (0 to 2047, 2048 to 4095, ...) at most 32 rows name the same one
- point_offset: int32 [2, 262144], P(None, ('bx', 'by')), may hold values from 0 to 1023
- point_value: float32 [2, 262144], P(None, ('bx', 'by')), may hold values from -0.0625 to 0.0625
- coef: int32 [4], replicated, may hold values from 0 to 31
Outputs:
- weights: float32 [2, 64, 131072], P(None, None, ('bx', 'by'))
The draws below stay inside these ranges and needn't reach their ends.
Inputs may be any that keep to these rules, and one draw needn't show every extreme that they name: `point_box`: the 2048 points of one device name any one box at most 32 times, a bound that some block reaches.
All inputs are finite; a program needn't handle non-finite values.
Results may differ from the reference program's by a relative error of at most 0.0012.
Values sent between devices are 32-bit elements; how exact they have to be, the bound alone decides.
No kernel may reach another device: no remote copies, remote signals or barrier semaphores. Data moves between devices by JAX's collectives and lax.ppermute only.
A program may use at most 64 MiB of HBM per device.

```python
import math
import jax
import jax.numpy as jnp
import numpy as np
from jax import lax

N = 16384
ORDER = 8
PTS_DEV = 2048
TGT1 = 32
TGT2 = 32
CAP = 32
POINTS = 262144
N_BX = 8
N_BY = 16
DEVICES = 128


def touch_ends(result, stream_key, smallest, top_value):
    extent = result.shape
    index_at = [jax.random.randint(jax.random.fold_in(stream_key, axis), (), 0, extent[axis]) for axis in range(len(extent))]
    result = result.at[tuple(index_at)].set(smallest)
    longest = extent.index(max(extent))
    index_at[longest] = (index_at[longest] + 1) % extent[longest]
    return result.at[tuple(index_at)].set(top_value)


def level_of(own_key, extent, shards, least, largest):
    loudness, own = 1.0, jax.random.fold_in(own_key, 6)
    for position, shards_of in shards:
        heights = jnp.exp(jax.random.uniform(jax.random.fold_in(own, position), (shards_of,), jnp.float32, least / len(shards), largest / len(shards)))
        loudness = loudness * jnp.repeat(heights, extent[position] // shards_of).reshape([-1 if axis == position else 1 for axis in range(len(extent))])
    return loudness


def deal_out(rng, own, number, rows, number_of, top, bound, skew):
    order = jax.random.permutation(rng, number_of)
    heavy_load, ordinary = load_shares(number_of, rows * top, bound, skew, True), load_shares(number_of, rows * top, bound, skew, False)
    places = jnp.arange(number_of)

    def named(tallies, turn):
        used = int((tallies > 0).sum())
        fixed = max(1, used // 4)
        shifted = fixed + (places - fixed + turn * (used - fixed)) % max(1, number_of - fixed)
        return jnp.zeros((number_of,), jnp.int32).at[order[jnp.where(places < fixed, places, shifted)]].set(jnp.asarray(tallies, jnp.int32))

    tallies = jnp.where(number % 4 == 0, named(heavy_load, number // 4), named(ordinary, number - number // 4 - 1))
    mixed = jax.random.permutation(jax.random.fold_in(own, 3), number_of)
    source_of, sink = mixed[0:number_of // 2 * 2:2], mixed[1:number_of // 2 * 2:2]
    margin = jnp.minimum(tallies[source_of] - 1, bound - tallies[sink]) // 2
    margin = jnp.where((source_of == order[0]) | (sink == order[0]) | (tallies[sink] == 0), 0, jnp.maximum(margin, 0))
    shifted = jax.random.randint(jax.random.fold_in(own, 4), (number_of // 2,), 0, 1 << 20) % (margin + 1)
    tallies = tallies.at[source_of].add(-shifted).at[sink].add(shifted)
    members = jnp.searchsorted(jnp.cumsum(tallies), jnp.arange(rows * top), side="right").astype(jnp.int32)
    listing = members.reshape(top, rows).T
    listing = listing[jax.random.permutation(jax.random.fold_in(own, 1), rows)]
    turn = jax.random.randint(jax.random.fold_in(own, 2), (rows, 1), 0, top)
    return jnp.take_along_axis(listing, (jnp.arange(top)[None, :] + turn) % top, axis=1)


def load_shares(number_of, total, bound, slope, full):
    weights = [(1 << 20) // math.isqrt(rank ** slope) + 1 for rank in range(1, number_of + 1)]
    largest = bound if full else min(bound, max(-(-total // number_of), total * weights[0] // sum(weights)))
    least = 1 if total - largest >= number_of - 1 else 0
    given, spare = [largest] + [least] * (number_of - 1), total - largest - least * (number_of - 1)
    while spare > 0:
        movable = [i for i in range(1, number_of) if given[i] < largest] or [i for i in range(1, number_of) if given[i] < bound]
        whole, left = sum([weights[i] for i in movable]), spare
        for i in movable:
            addition = min(bound - given[i], max(1, left * weights[i] // whole), spare)
            given[i] = given[i] + addition
            spare = spare - addition
    return np.array(given)


def gaussian(rng, extent, scale, limit, pieces=(), held_as=jnp.bfloat16):
    entries = scale * jax.random.normal(rng, extent, jnp.float32)
    if pieces:
        entries = entries * level_of(rng, extent, pieces, -0.22, 0.18)
    return jnp.clip(entries, -limit, limit).astype(held_as)


def setup_inputs(seed: int = 0) -> dict:
    arg_keys = jax.random.split(jax.random.key(seed), 5)
    point_box_keys = jax.random.split(jax.random.fold_in(arg_keys[0], 1), POINTS // PTS_DEV)
    point_box_turns = jax.random.permutation(jax.random.fold_in(arg_keys[0], 3), POINTS // PTS_DEV)
    point_box = jax.vmap(lambda own, number: deal_out(jax.random.fold_in(arg_keys[0], 2), own, number, PTS_DEV, DEVICES, 1, CAP, 2))(point_box_keys, point_box_turns).reshape((POINTS, 1))
    point_offset = touch_ends(jax.random.randint(arg_keys[1], (2, POINTS), 0, N // N_BY), jax.random.fold_in(arg_keys[1], 1), 0, (N // N_BY) - 1).astype(jnp.int32)
    point_value = gaussian(arg_keys[2], (2, POINTS), 0.01, 0.0625, ((1, 128),), jnp.float32)
    coef = touch_ends(jax.random.randint(arg_keys[3], (4,), 0, 32), jax.random.fold_in(arg_keys[3], 1), 0, 31).astype(jnp.int32)
    return {"point_box": point_box, "point_offset": point_offset, "point_value": point_value, "coef": coef}


def node_table():
    counting = np.arange(ORDER) * 1.0
    return 0.5 - 0.5 * np.cos(np.pi * (2.0 * counting + 1.0) / (2.0 * ORDER))

def lagrange(coords):
    nodes = node_table()
    columns = []
    for target in range(ORDER):
        factor = jnp.ones_like(coords)
        for source in range(ORDER):
            if source != target:
                factor = factor * ((coords - float(nodes[source])) * float(1.0 / (nodes[target] - nodes[source])))
        columns.append(factor)
    return jnp.stack(columns, axis=-1)

def child_matrix(side):
    nodes = node_table()
    points = 0.5 * (side + nodes)
    rows_all = []
    for target in range(ORDER):
        factor = np.ones(ORDER)
        for source in range(ORDER):
            if source != target:
                factor = factor * (points - nodes[source]) / (nodes[target] - nodes[source])
        rows_all.append(factor)
    return jnp.asarray(np.stack(rows_all), dtype=jnp.float32)

def phases(tgt_first, tgt_second, freq_first, freq_second, coef):
    scaled = coef.astype(jnp.float32)
    wave = jnp.sin(128.0 * jnp.pi * (tgt_first + tgt_second))
    speed_first = (32.0 + scaled[0] + scaled[1] * wave) / 4096.0
    speed_second = (32.0 + scaled[2] + scaled[3] * wave) / 4096.0
    kfirst = freq_first[:, None]
    ksecond = freq_second[:, None]
    total = tgt_first * kfirst + tgt_second * ksecond + jnp.sqrt(1.0 + (speed_first * kfirst) ** 2 + (speed_second * ksecond) ** 2)
    fraction = total - jnp.floor(total)
    return (jnp.cos(2.0 * jnp.pi * fraction), jnp.sin(2.0 * jnp.pi * fraction))

def grid_nodes(corner_first, width_first, corner_second, width_second):
    nodes = jnp.asarray(node_table(), dtype=jnp.float32)
    along_first = corner_first + width_first * nodes
    along_second = corner_second + width_second * nodes
    return (jnp.broadcast_to(along_first[:, None], (ORDER, ORDER)).reshape(-1), jnp.broadcast_to(along_second[None, :], (ORDER, ORDER)).reshape(-1))

def tgt_axis(index, merged, count, boxes):
    code = jnp.zeros((), jnp.int32)
    for bit in range(merged):
        code = code + (index >> bit & 1) * 2 ** (merged - 1 - bit)
    place = jnp.arange(count, dtype=jnp.int32) * 2 ** merged + code
    return (place.astype(jnp.float32) + 0.5) * (boxes / (N * 2.0 ** merged))

def centers(index_x, index_y, merged_x, merged_y, boxes_x, boxes_y):
    first = tgt_axis(index_x, merged_x, TGT1, boxes_x)
    second = tgt_axis(index_y, merged_y, TGT2, boxes_y)
    return (jnp.broadcast_to(first[:, None], (TGT1, TGT2)).reshape(-1), jnp.broadcast_to(second[None, :], (TGT1, TGT2)).reshape(-1))

def leaf_terms(columns, corner_first, width_first, corner_second, width_second, tgt_first, tgt_second, coef):
    cosine, sine = phases(tgt_first, tgt_second, columns[0], columns[1], coef)
    real_in = columns[2][:, None]
    imag_in = columns[3][:, None]
    real_part = cosine * real_in - sine * imag_in
    imag_part = cosine * imag_in + sine * real_in
    basis_first = lagrange((columns[0] - corner_first) / width_first)
    basis_second = lagrange((columns[1] - corner_second) / width_second)
    basis = (basis_first[:, :, None] * basis_second[:, None, :]).reshape(columns.shape[1], ORDER * ORDER)
    dims = (((0,), (0,)), ((), ()))
    real_sum = lax.dot_general(basis, real_part, dims, precision=lax.Precision.HIGHEST, preferred_element_type=jnp.float32)
    imag_sum = lax.dot_general(basis, imag_part, dims, precision=lax.Precision.HIGHEST, preferred_element_type=jnp.float32)
    return (real_sum, imag_sum)

def shift_back(real_sum, imag_sum, node_first, node_second, tgt_first, tgt_second, coef):
    cosine, sine = phases(tgt_first, tgt_second, node_first, node_second, coef)
    return jnp.stack([cosine * real_sum + sine * imag_sum, cosine * imag_sum - sine * real_sum])

def merge_box(first_w, second_w, tgt_first, tgt_second, along, corner_d, width_d, corner_o, width_o, coef):
    spreads = []
    for side, child in ((0, first_w), (1, second_w)):
        start = corner_d + side * width_d
        if along == 1:
            node_first, node_second = grid_nodes(start, width_d, corner_o, width_o)
        else:
            node_first, node_second = grid_nodes(corner_o, width_o, start, width_d)
        cosine, sine = phases(tgt_first, tgt_second, node_first, node_second, coef)
        lifted = jnp.stack([cosine * child[0] - sine * child[1], cosine * child[1] + sine * child[0]])
        lifted = lifted.reshape(2, ORDER, ORDER, -1)
        table = child_matrix(side)
        if along == 1:
            spreads.append(jnp.einsum('ts,rsuk->rtuk', table, lifted, precision=lax.Precision.HIGHEST))
        else:
            spreads.append(jnp.einsum('us,rtsk->rtuk', table, lifted, precision=lax.Precision.HIGHEST))
    total = (spreads[0] + spreads[1]).reshape(2, ORDER * ORDER, -1)
    if along == 1:
        node_first, node_second = grid_nodes(corner_d, 2.0 * width_d, corner_o, width_o)
    else:
        node_first, node_second = grid_nodes(corner_o, width_o, corner_d, 2.0 * width_d)
    return shift_back(total[0], total[1], node_first, node_second, tgt_first, tgt_second, coef)

def merge_first(holding, partner, index_x, row_y, level, boxes_x, boxes_y, coef):
    width_first = N // boxes_x
    width_second = N // boxes_y
    flag = index_x >> level & 1 == 0
    first_w = jnp.where(flag, holding, partner)
    second_w = jnp.where(flag, partner, holding)
    tgt_first, tgt_second = centers(index_x, row_y, level + 1, level, boxes_x, boxes_y)
    corner_d = ((index_x >> level + 1) * (width_first * 2 ** (level + 1))).astype(jnp.float32)
    corner_o = ((row_y >> level) * (width_second * 2 ** level)).astype(jnp.float32)
    return merge_box(first_w, second_w, tgt_first, tgt_second, 1, corner_d, float(width_first * 2 ** level), corner_o, float(width_second * 2 ** level), coef)

def merge_second(holding, partner, index_x, index_y, level, boxes_x, boxes_y, coef):
    width_first = N // boxes_x
    width_second = N // boxes_y
    flag = index_y >> level & 1 == 0
    first_w = jnp.where(flag, holding, partner)
    second_w = jnp.where(flag, partner, holding)
    tgt_first, tgt_second = centers(index_x, index_y, level + 1, level + 1, boxes_x, boxes_y)
    corner_d = ((index_y >> level + 1) * (width_second * 2 ** (level + 1))).astype(jnp.float32)
    corner_o = ((index_x >> level + 1) * (width_first * 2 ** (level + 1))).astype(jnp.float32)
    return merge_box(first_w, second_w, tgt_first, tgt_second, 2, corner_d, float(width_second * 2 ** level), corner_o, float(width_first * 2 ** (level + 1)), coef)

def pack_slots(box_ids, offsets, values, boxes_y, width_first, width_second, owners, slot_cap):
    ids = box_ids[:, 0]
    onehot = (ids[:, None] == jnp.arange(owners, dtype=jnp.int32)[None, :]).astype(jnp.int32)
    ranks = lax.optimization_barrier(jnp.sum((jnp.cumsum(onehot, axis=0) - 1) * onehot, axis=1))
    freq_first = (ids // boxes_y * width_first + offsets[0]).astype(jnp.float32)
    freq_second = (ids % boxes_y * width_second + offsets[1]).astype(jnp.float32)
    stacked = jnp.stack([freq_first, freq_second, values[0], values[1]], axis=0)
    slot_of = ids * slot_cap + ranks
    blank = jnp.concatenate([jnp.full((2, owners * slot_cap), -1.0, jnp.float32), jnp.zeros((2, owners * slot_cap), jnp.float32)], axis=0)
    filled = blank.at[:, slot_of].set(stacked)
    return filled.reshape(4, owners, slot_cap).transpose(1, 0, 2).reshape(owners, 4 * slot_cap)

def spread_columns(arrived):
    owners = arrived.shape[0]
    return arrived.reshape(owners, 4, -1).transpose(1, 0, 2).reshape(4, -1)

def reference(point_box, point_offset, point_value, coef):
    owners = N_BX * N_BY
    width_first = N // N_BX
    width_second = N // N_BY
    box_rows = point_box.reshape(owners, PTS_DEV, 1)
    offset_rows = point_offset.reshape(2, owners, PTS_DEV).transpose(1, 0, 2)
    value_rows = point_value.reshape(2, owners, PTS_DEV).transpose(1, 0, 2)
    sent = lax.map(lambda group: pack_slots(group[0], group[1], group[2], N_BY, width_first, width_second, owners, CAP), (box_rows, offset_rows, value_rows))
    arrived = sent.transpose(1, 0, 2)

    def leaf_of(group):
        received, owner = group
        index_x = owner // N_BY
        index_y = owner % N_BY
        columns = spread_columns(received)
        corner_first = (index_x * width_first).astype(jnp.float32)
        corner_second = (index_y * width_second).astype(jnp.float32)
        tgt_first, tgt_second = centers(index_x, index_y, 0, 0, N_BX, N_BY)
        real_sum, imag_sum = leaf_terms(columns, corner_first, float(width_first), corner_second, float(width_second), tgt_first, tgt_second, coef)
        node_first, node_second = grid_nodes(corner_first, float(width_first), corner_second, float(width_second))
        return shift_back(real_sum, imag_sum, node_first, node_second, tgt_first, tgt_second, coef)
    weights = lax.map(leaf_of, (arrived, jnp.arange(owners, dtype=jnp.int32)))
    weights = weights.reshape(N_BX, N_BY, 2, ORDER * ORDER, TGT1 * TGT2)
    grid_x = jnp.broadcast_to(jnp.arange(N_BX, dtype=jnp.int32)[:, None], (N_BX, N_BY))
    grid_y = jnp.broadcast_to(jnp.arange(N_BY, dtype=jnp.int32)[None, :], (N_BX, N_BY))
    for level in range(2):
        partner = weights[jnp.arange(N_BX, dtype=jnp.int32) ^ 1 << level]
        step_first = jax.vmap(jax.vmap(lambda hold, other, ix, iy: merge_first(hold, other, ix, iy, level, N_BX, N_BY, coef)))
        weights = step_first(weights, partner, grid_x, grid_y)
        partner = weights[:, jnp.arange(N_BY, dtype=jnp.int32) ^ 1 << level]
        step_second = jax.vmap(jax.vmap(lambda hold, other, ix, iy: merge_second(hold, other, ix, iy, level, N_BX, N_BY, coef)))
        weights = step_second(weights, partner, grid_x, grid_y)
    weights = weights.reshape(owners, 2, ORDER * ORDER, TGT1 * TGT2)
    return weights.transpose(1, 2, 0, 3).reshape(2, ORDER * ORDER, owners * TGT1 * TGT2)
```

```python
import functools
import math

import jax
import jax.numpy as jnp
import numpy as np
from jax import lax
from jax.experimental import pallas as pl
from jax.experimental.pallas import tpu as pltpu
from jax.sharding import PartitionSpec as P

N = 16384
ORDER = 8
TGT = 32
CAP = 32
NODES = ORDER * ORDER
TARGETS = TGT * TGT
F32 = jnp.float32
BF16 = jnp.bfloat16

SIN_C = (3.1415925798055824, -5.167706866167939, 2.550031193519312, -0.5980441939121666, 0.07721838615746283)
COS_C = (0.9999999532476086, -4.934792830619651, 4.058411352862725, -1.3318765680816773, 0.21968961109948903)


def node_table():
    counting = np.arange(ORDER) * 1.0
    return 0.5 - 0.5 * np.cos(np.pi * (2.0 * counting + 1.0) / (2.0 * ORDER))


def child_matrix(side):
    nodes = node_table()
    points = 0.5 * (side + nodes)
    rows = []
    for target in range(ORDER):
        factor = np.ones(ORDER)
        for source in range(ORDER):
            if source != target:
                factor = factor * (points - nodes[source]) / (nodes[target] - nodes[source])
        rows.append(factor)
    return np.stack(rows)


def merge_tables(along):
    eye = np.eye(ORDER)
    both = []
    for bit in range(2):
        parts = []
        for side in (bit, 1 - bit):
            matrix = child_matrix(side)
            parts.append(np.kron(matrix, eye) if along == 1 else np.kron(eye, matrix))
        full = np.concatenate(parts, axis=1)
        high = full.astype(np.float32).astype(BF16)
        low = (full - high.astype(np.float64)).astype(np.float32).astype(BF16)
        top = np.concatenate([high, high], axis=1)
        bottom = np.concatenate([low, np.zeros_like(low)], axis=1)
        both.append(np.concatenate([top, bottom], axis=0))
    return np.stack(both)


def horner(coefs, x):
    total = coefs[-1]
    for c in coefs[-2::-1]:
        total = total * x + c
    return total


def turn(phase):
    r = phase - jnp.floor(phase + 0.5)
    x = r * r
    sine = horner(SIN_C, x) * r
    cosine = horner(COS_C, x)
    twice = sine + sine
    return 1.0 - twice * sine, twice * cosine


def split(x):
    high = x.astype(BF16)
    return high, (x - high.astype(F32)).astype(BF16)


def iota(shape, axis):
    return lax.broadcasted_iota(jnp.int32, shape, axis)


def nt(a, b):
    return lax.dot_general(a, b, (((1,), (1,)), ((), ())), preferred_element_type=F32)


def pack_body(box_ref, off_ref, val_ref, out_ref):
    blocks = box_ref.shape[0]
    row = iota((128, 128), 0)
    row2 = iota((128, 256), 0)
    col2 = iota((128, 256), 1)
    prefix = jnp.where((row2 < col2) | (col2 >= 128), 1.0, 0.0).astype(BF16)
    same = [row == box_ref[b : b + 1, :] for b in range(blocks)]
    ones = [jnp.where(m, 1.0, 0.0).astype(BF16) for m in same]
    counts = jnp.dot(jnp.concatenate(ones, axis=0), prefix, preferred_element_type=F32)
    slots = iota((CAP, 128), 0).astype(F32)
    carry = jnp.zeros((128, 128), F32)
    wide = []
    for b in range(blocks):
        part = counts[b * 128 : (b + 1) * 128]
        rank = jnp.sum(jnp.where(same[b], part[:, :128] + carry, 0.0), axis=0, keepdims=True)
        carry = carry + part[:, 128:]
        hit = slots == rank
        cols = slice(b * 128, (b + 1) * 128)
        values = [off_ref[0:1, cols].astype(F32), off_ref[1:2, cols].astype(F32), val_ref[0:1, cols], val_ref[1:2, cols]]
        pieces = [[], [], []]
        for v in values:
            rest = v
            for piece in pieces:
                top = rest.astype(BF16).astype(F32)
                rest = rest - top
                piece.append(jnp.where(hit, top, 0.0).astype(BF16))
        wide.append(jnp.concatenate([x for piece in pieces for x in piece], axis=0))
    total = nt(jnp.concatenate(ones, axis=1), jnp.concatenate(wide, axis=1))
    out_ref[...] = total[:, :128] + total[:, 128:256] + total[:, 256:]


def pack(box, offsets, values):
    return pl.pallas_call(
        pack_body,
        out_shape=jax.ShapeDtypeStruct((128, 4 * CAP), F32),
        in_specs=[pl.BlockSpec(memory_space=pltpu.VMEM)] * 3,
        out_specs=pl.BlockSpec(memory_space=pltpu.VMEM),
        name="pack",
    )(box, offsets, values)


def basis_rows(tau):
    nodes = node_table()
    which = iota((ORDER, 128), 0)
    total = None
    for step in range(1, ORDER):
        other = jnp.zeros((ORDER, 128), F32)
        scale = jnp.zeros((ORDER, 128), F32)
        for t in range(ORDER):
            s = (t + step) % ORDER
            other = jnp.where(which == t, float(nodes[s]), other)
            scale = jnp.where(which == t, float(1.0 / (nodes[t] - nodes[s])), scale)
        factor = (tau - other) * scale
        total = factor if total is None else total * factor
    return total


def leaf_body(info_ref, rx_ref, out_ref, xt_ref, q_ref, r_ref, l_ref, acc_ref):
    width_first, width_second = float(N // 8), float(N // 16)
    corner_first = info_ref[4].astype(F32) * width_first
    corner_second = info_ref[5].astype(F32) * width_second
    xt_ref[...] = rx_ref[...].T
    acc_ref[...] = jnp.zeros_like(acc_ref)

    order = iota((TGT, 128), 0)
    klass = (order % 16) * 2 + order // 16
    _, wave = turn((klass.astype(F32) + 1.5) * (1.0 / 32.0))
    speed_first = (32.0 + info_ref[0].astype(F32) + info_ref[1].astype(F32) * wave) * (1.0 / 4096.0)
    speed_second = (32.0 + info_ref[2].astype(F32) + info_ref[3].astype(F32) * wave) * (1.0 / 4096.0)
    lin_second = (iota((TGT, 128), 0) * 4 + 34).astype(F32)
    power = iota((16, 128), 0).astype(F32)

    def slot(s, lane):
        off_first = xt_ref[pl.ds(s, 1), :]
        off_second = xt_ref[pl.ds(CAP + s, 1), :]
        real_in = xt_ref[pl.ds(2 * CAP + s, 1), :]
        imag_in = xt_ref[pl.ds(3 * CAP + s, 1), :]
        first = off_first + corner_first
        second = off_second + corner_second
        a = speed_first * first
        b = speed_second * second
        root = jnp.sqrt(1.0 + a * a + b * b)
        root = root - jnp.floor(root)
        along = lin_second * second
        for eps in range(2):
            part = root[eps * 16 : eps * 16 + 16]
            lin = (along + first * (2.0 * eps + 1.0)) * (1.0 / 4096.0)
            lin = lin - jnp.floor(lin)
            cosine, sine = turn(lin + jnp.concatenate([part, part], axis=0))
            q_ref[2 * eps] = cosine
            q_ref[2 * eps + 1] = sine
        cosine, sine = turn(power * ((first - second) * (1.0 / 1024.0)))
        z_real = cosine * real_in - sine * imag_in
        z_imag = cosine * imag_in + sine * real_in
        cols = slice(lane * 128, lane * 128 + 128)
        low_cols = slice(256 + lane * 128, 256 + lane * 128 + 128)
        for up in range(16):
            zr = z_real[up : up + 1]
            zi = z_imag[up : up + 1]
            for eps in range(2):
                qr = q_ref[2 * eps, up : up + 16, :]
                qi = q_ref[2 * eps + 1, up : up + 16, :]
                for part, value in enumerate((qr * zr - qi * zi, qr * zi + qi * zr)):
                    high, low = split(value)
                    base = part * 512 + (2 * up + eps) * 16
                    r_ref[base : base + 16, cols] = high
                    r_ref[base : base + 16, low_cols] = low
        first_rows = basis_rows(off_first * (1.0 / width_first))
        second_rows = basis_rows(off_second * (1.0 / width_second))
        for part, value in enumerate(turn(second * (1.0 / 128.0))):
            scaled = second_rows * value
            for t in range(0, ORDER, 2):
                pair = jnp.concatenate([first_rows[t : t + 1] * scaled, first_rows[t + 1 : t + 2] * scaled], axis=0)
                high, low = split(pair)
                base = part * NODES + t * ORDER
                l_ref[base : base + 16, cols] = high
                l_ref[128 + base : 128 + base + 16, cols] = low

    def step(i, carry):
        slot(2 * i, 0)
        slot(2 * i + 1, 1)
        right = l_ref[...]
        for m in range(4):
            rows = slice(m * 256, m * 256 + 256)
            acc_ref[rows, :] += nt(r_ref[rows, :256], right) + nt(r_ref[rows, 256:], right)
        return carry

    lax.fori_loop(0, CAP // 2, step, 0)

    for m in range(4):
        blocks = []
        for part in range(2):
            rows = slice(part * 512 + m * 128, part * 512 + m * 128 + 128)
            blocks.append((acc_ref[rows, :128] + acc_ref[rows, 128:]).T)
        (cr, sr), (ci, si) = [(x[:NODES], x[NODES:]) for x in blocks]
        low_cols = slice(m * 128, m * 128 + 128)
        high_cols = slice(512 + m * 128, 512 + m * 128 + 128)
        out_ref[:NODES, low_cols] = cr + si
        out_ref[NODES:, low_cols] = ci - sr
        out_ref[:NODES, high_cols] = cr - si
        out_ref[NODES:, high_cols] = ci + sr


def leaf(info, arrived):
    return pl.pallas_call(
        leaf_body,
        out_shape=jax.ShapeDtypeStruct((2 * NODES, TARGETS), F32),
        in_specs=[pl.BlockSpec(memory_space=pltpu.SMEM), pl.BlockSpec(memory_space=pltpu.VMEM)],
        out_specs=pl.BlockSpec(memory_space=pltpu.VMEM),
        scratch_shapes=[
            pltpu.VMEM((128, 128), F32),
            pltpu.VMEM((4, TGT, 128), F32),
            pltpu.VMEM((1024, 512), BF16),
            pltpu.VMEM((256, 256), BF16),
            pltpu.VMEM((1024, 256), F32),
        ],
        name="leaf",
    )(info, arrived)


def place(index, merged):
    code = jnp.int32(0)
    for bit in range(merged):
        code = code + ((index >> bit) & 1) * 2 ** (merged - 1 - bit)
    return (code.astype(F32) + 0.5) * (1.0 / 2.0**merged)


def node_columns(shape):
    nodes = node_table()
    row = iota(shape, 0)
    first = jnp.zeros(shape, F32)
    second = jnp.zeros(shape, F32)
    for t in range(ORDER):
        first = jnp.where(row // ORDER == t, float(nodes[t]), first)
        second = jnp.where(row % ORDER == t, float(nodes[t]), second)
    return first, second


def speeds(info_ref, klass, place_first, place_second):
    _, wave = turn((klass + (place_first + 2.0 * place_second)) * (1.0 / 32.0))
    one = (32.0 + info_ref[0].astype(F32) + info_ref[1].astype(F32) * wave) * (1.0 / 4096.0)
    two = (32.0 + info_ref[2].astype(F32) + info_ref[3].astype(F32) * wave) * (1.0 / 4096.0)
    return one, two


def root_of(speed, first, second):
    a = speed[0] * first
    b = speed[1] * second
    return jnp.sqrt(1.0 + a * a + b * b)


LEVELS = ((1, 0), (2, 0), (1, 1), (2, 1))


def tables_body(info_ref, gamma_ref, last_ref):
    index_x = info_ref[4]
    index_y = info_ref[5]
    z_first, z_second = node_columns((NODES, 128))
    for tile in range(4):
        lane = iota((1, 128), 1)
        u = tile * 8 + lane // 16
        v = lane % 16
        klass = ((u + 2 * v) % TGT).astype(F32)
        cols = slice(tile * 128, tile * 128 + 128)
        merged = [0, 0]
        for number, (along, level) in enumerate(LEVELS):
            before = list(merged)
            merged[along - 1] += 1
            old = [place(index_x, before[0]), place(index_y, before[1])]
            new = [place(index_x, merged[0]), place(index_y, merged[1])]
            speed_old = speeds(info_ref, klass, *old)
            speed_new = speeds(info_ref, klass, *new)
            index_d = index_x if along == 1 else index_y
            bit = (index_d >> level) & 1
            for who in range(2):
                side = bit if who == 0 else 1 - bit
                child_first = index_x >> before[0]
                child_second = index_y >> before[1]
                if along == 1:
                    child_first = (index_x >> merged[0]) * 2 + side
                else:
                    child_second = (index_y >> merged[1]) * 2 + side
                width_first = float(N // 8 * 2 ** before[0])
                width_second = float(N // 16 * 2 ** before[1])
                first = child_first.astype(F32) * width_first + width_first * z_first
                second = child_second.astype(F32) * width_second + width_second * z_second
                if along == 1:
                    moved = first * ((new[0] - old[0]) * (1.0 / 2048.0))
                else:
                    moved = second * ((new[1] - old[1]) * (1.0 / 1024.0))
                phase = root_of(speed_new, first, second) - root_of(speed_old, first, second) + moved
                cosine, sine = turn(phase)
                gamma_ref[number, who, :NODES, cols] = cosine
                gamma_ref[number, who, NODES:, cols] = sine
        width_first = float(N // 8 * 4)
        width_second = float(N // 16 * 4)
        first = (index_x >> 2).astype(F32) * width_first + width_first * z_first
        second = (index_y >> 2).astype(F32) * width_second + width_second * z_second
        new = [place(index_x, 2), place(index_y, 2)]
        root = root_of(speeds(info_ref, klass, *new), first, second)
        root = root - jnp.floor(root)
        at_first = first * ((u.astype(F32) + new[0]) * (1.0 / 2048.0))
        at_first = at_first - jnp.floor(at_first) + root
        for half in range(2):
            at_second = second * ((v.astype(F32) + (16.0 * half + new[1])) * (1.0 / 1024.0))
            cosine, sine = turn(at_first + at_second)
            wide = slice(half * 512 + tile * 128, half * 512 + tile * 128 + 128)
            last_ref[:NODES, wide] = cosine
            last_ref[NODES:, wide] = sine


def tables(info):
    return pl.pallas_call(
        tables_body,
        out_shape=(
            jax.ShapeDtypeStruct((4, 2, 2 * NODES, 512), F32),
            jax.ShapeDtypeStruct((2 * NODES, TARGETS), F32),
        ),
        in_specs=[pl.BlockSpec(memory_space=pltpu.SMEM)],
        out_specs=[pl.BlockSpec(memory_space=pltpu.VMEM)] * 2,
        name="tables",
    )(info)


def merge_body(number, info_ref, own_ref, other_ref, gamma_ref, mix_ref, *rest):
    along, level = LEVELS[number]
    final = number == 3
    out_ref = rest[-1]
    index_d = info_ref[4] if along == 1 else info_ref[5]
    bit = (index_d >> level) & 1
    left = mix_ref[bit]

    def combined(cols, gcols):
        reals, imags = [], []
        for who, ref in ((0, own_ref), (1, other_ref)):
            gr = gamma_ref[number, who, :NODES, gcols]
            gi = gamma_ref[number, who, NODES:, gcols]
            xr = ref[:NODES, cols]
            xi = ref[NODES:, cols]
            reals.append(split(gr * xr - gi * xi))
            imags.append(split(gr * xi + gi * xr))
        out = []
        for parts in (reals, imags):
            right = jnp.concatenate([parts[0][0], parts[1][0], parts[0][1], parts[1][1]], axis=0)
            both = jnp.dot(left, right, preferred_element_type=F32)
            out.append(both[:NODES] + both[NODES:])
        return out

    if not final:
        for tile in range(4):
            cols = slice(tile * 256, tile * 256 + 256)
            gcols = slice((tile % 2) * 256, (tile % 2) * 256 + 256)
            real, imag = combined(cols, gcols)
            out_ref[:NODES, cols] = real
            out_ref[NODES:, cols] = imag
        return
    last_ref = rest[0]
    source = iota((256, 256), 0)
    target = iota((256, 256), 1)
    wanted = ((target // 16) % 2) * 128 + (target // 32) * 16 + target % 16
    order = jnp.where(source == wanted, 1.0, 0.0).astype(BF16)
    for tile in range(4):
        halves = []
        for half in range(2):
            cols = slice(half * 512 + tile * 128, half * 512 + tile * 128 + 128)
            real, imag = combined(cols, slice(tile * 128, tile * 128 + 128))
            cosine = last_ref[:NODES, cols]
            sine = last_ref[NODES:, cols]
            halves.append(jnp.concatenate([cosine * real + sine * imag, cosine * imag - sine * real], axis=0))
        value = jnp.concatenate(halves, axis=1)
        high = value.astype(BF16)
        value = value - high.astype(F32)
        mid, low = split(value)
        moved = jnp.dot(jnp.concatenate([high, mid, low], axis=0), order, preferred_element_type=F32)
        moved = moved[:128] + moved[128:256] + moved[256:]
        out_ref[0, :, tile * 256 : tile * 256 + 256] = moved[:NODES]
        out_ref[1, :, tile * 256 : tile * 256 + 256] = moved[NODES:]


def merge(number, info, own, other, gamma, last):
    final = number == 3
    args = [info, own, other, gamma, jnp.asarray(merge_tables(LEVELS[number][0]))]
    if final:
        args.append(last)
    shape = (2, NODES, TARGETS) if final else (2 * NODES, TARGETS)
    return pl.pallas_call(
        functools.partial(merge_body, number),
        out_shape=jax.ShapeDtypeStruct(shape, F32),
        in_specs=[pl.BlockSpec(memory_space=pltpu.SMEM)] + [pl.BlockSpec(memory_space=pltpu.VMEM)] * (len(args) - 1),
        out_specs=pl.BlockSpec(memory_space=pltpu.VMEM),
        name="merge_%d" % number,
    )(*args)


def swap(value, along, level):
    axis = "bx" if along == 1 else "by"
    return lax.ppermute(value, axis, [(i, i ^ 1 << level) for i in range(lax.axis_size(axis))])


def on_device(point_box, point_offset, point_value, coef):
    owners = lax.axis_size("bx") * lax.axis_size("by")
    place_on = jnp.stack([lax.axis_index("bx"), lax.axis_index("by")]).astype(jnp.int32)
    info = jnp.concatenate([coef, place_on])
    sent = pack(point_box.reshape(-1, 128), point_offset, point_value)
    arrived = lax.all_to_all(sent.reshape(owners, 1, -1), ("bx", "by"), split_axis=0, concat_axis=0, tiled=True)
    gamma, last = tables(info)
    holding = leaf(info, arrived.reshape(owners, -1))
    for number, (along, level) in enumerate(LEVELS):
        holding = merge(number, info, holding, swap(holding, along, level), gamma, last)
    return holding


def solution(mesh):
    in_specs = (P(("bx", "by"), None), P(None, ("bx", "by")), P(None, ("bx", "by")), P())
    out_specs = P(None, None, ("bx", "by"))
    return jax.shard_map(on_device, mesh=mesh, in_specs=in_specs, out_specs=out_specs, check_vma=False)
```

```python
import functools
import math

import jax
import jax.numpy as jnp
import numpy as np
from jax import lax
from jax.experimental import pallas as pl
from jax.experimental.pallas import tpu as pltpu
from jax.sharding import PartitionSpec as P

N = 16384
ORDER = 8
TGT = 32
CAP = 32
NODES = ORDER * ORDER
TARGETS = TGT * TGT
F32 = jnp.float32
BF16 = jnp.bfloat16

SIN_C = (3.1415925798055824, -5.167706866167939, 2.550031193519312, -0.5980441939121666, 0.07721838615746283)
COS_C = (0.9999999532476086, -4.934792830619651, 4.058411352862725, -1.3318765680816773, 0.21968961109948903)


def node_table():
    counting = np.arange(ORDER) * 1.0
    return 0.5 - 0.5 * np.cos(np.pi * (2.0 * counting + 1.0) / (2.0 * ORDER))


def child_matrix(side):
    nodes = node_table()
    points = 0.5 * (side + nodes)
    rows = []
    for target in range(ORDER):
        factor = np.ones(ORDER)
        for source in range(ORDER):
            if source != target:
                factor = factor * (points - nodes[source]) / (nodes[target] - nodes[source])
        rows.append(factor)
    return np.stack(rows)


def merge_tables(along):
    eye = np.eye(ORDER)
    both = []
    for bit in range(2):
        parts = []
        for side in (bit, 1 - bit):
            matrix = child_matrix(side)
            parts.append(np.kron(matrix, eye) if along == 1 else np.kron(eye, matrix))
        full = np.concatenate(parts, axis=1)
        high = full.astype(np.float32).astype(BF16)
        low = (full - high.astype(np.float64)).astype(np.float32).astype(BF16)
        top = np.concatenate([high, high], axis=1)
        bottom = np.concatenate([low, np.zeros_like(low)], axis=1)
        both.append(np.concatenate([top, bottom], axis=0))
    return np.stack(both)


def horner(coefs, x):
    total = coefs[-1]
    for c in coefs[-2::-1]:
        total = total * x + c
    return total


def turn(phase):
    r = phase - jnp.floor(phase + 0.5)
    x = r * r
    sine = horner(SIN_C, x) * r
    cosine = horner(COS_C, x)
    twice = sine + sine
    return 1.0 - twice * sine, twice * cosine


def split(x):
    high = x.astype(BF16)
    return high, (x - high.astype(F32)).astype(BF16)


def iota(shape, axis):
    return lax.broadcasted_iota(jnp.int32, shape, axis)


def nt(a, b):
    return lax.dot_general(a, b, (((1,), (1,)), ((), ())), preferred_element_type=F32)


def pack_body(box_ref, off_ref, val_ref, out_ref):
    blocks = box_ref.shape[0]
    row = iota((128, 128), 0)
    row2 = iota((128, 256), 0)
    col2 = iota((128, 256), 1)
    prefix = jnp.where((row2 < col2) | (col2 >= 128), 1.0, 0.0).astype(BF16)
    same = [row == box_ref[b : b + 1, :] for b in range(blocks)]
    ones = [jnp.where(m, 1.0, 0.0).astype(BF16) for m in same]
    counts = jnp.dot(jnp.concatenate(ones, axis=0), prefix, preferred_element_type=F32)
    slots = iota((CAP, 128), 0).astype(F32)
    carry = jnp.zeros((128, 128), F32)
    wide = []
    for b in range(blocks):
        part = counts[b * 128 : (b + 1) * 128]
        rank = jnp.sum(jnp.where(same[b], part[:, :128] + carry, 0.0), axis=0, keepdims=True)
        carry = carry + part[:, 128:]
        hit = slots == rank
        cols = slice(b * 128, (b + 1) * 128)
        values = [off_ref[0:1, cols].astype(F32), off_ref[1:2, cols].astype(F32), val_ref[0:1, cols], val_ref[1:2, cols]]
        pieces = [[], [], []]
        for v in values:
            rest = v
            for piece in pieces:
                top = rest.astype(BF16).astype(F32)
                rest = rest - top
                piece.append(jnp.where(hit, top, 0.0).astype(BF16))
        wide.append(jnp.concatenate([x for piece in pieces for x in piece], axis=0))
    total = nt(jnp.concatenate(ones, axis=1), jnp.concatenate(wide, axis=1))
    out_ref[...] = total[:, :128] + total[:, 128:256] + total[:, 256:]


def pack(box, offsets, values):
    return pl.pallas_call(
        pack_body,
        out_shape=jax.ShapeDtypeStruct((128, 4 * CAP), F32),
        in_specs=[pl.BlockSpec(memory_space=pltpu.VMEM)] * 3,
        out_specs=pl.BlockSpec(memory_space=pltpu.VMEM),
        name="pack", compiler_params=pltpu.CompilerParams(vmem_limit_bytes=8 << 20),
    )(box, offsets, values)


def basis_rows(tau):
    nodes = node_table()
    which = iota((ORDER, 128), 0)
    total = None
    for step in range(1, ORDER):
        other = jnp.zeros((ORDER, 128), F32)
        scale = jnp.zeros((ORDER, 128), F32)
        for t in range(ORDER):
            s = (t + step) % ORDER
            other = jnp.where(which == t, float(nodes[s]), other)
            scale = jnp.where(which == t, float(1.0 / (nodes[t] - nodes[s])), scale)
        factor = (tau - other) * scale
        total = factor if total is None else total * factor
    return total


def leaf_body(info_ref, rx_ref, out_ref, xt_ref, q_ref, r_ref, l_ref, acc_ref):
    width_first, width_second = float(N // 8), float(N // 16)
    corner_first = info_ref[4].astype(F32) * width_first
    corner_second = info_ref[5].astype(F32) * width_second
    xt_ref[...] = rx_ref[...].T
    acc_ref[...] = jnp.zeros_like(acc_ref)

    order = iota((TGT, 128), 0)
    klass = (order % 16) * 2 + order // 16
    _, wave = turn((klass.astype(F32) + 1.5) * (1.0 / 32.0))
    speed_first = (32.0 + info_ref[0].astype(F32) + info_ref[1].astype(F32) * wave) * (1.0 / 4096.0)
    speed_second = (32.0 + info_ref[2].astype(F32) + info_ref[3].astype(F32) * wave) * (1.0 / 4096.0)
    lin_second = (iota((TGT, 128), 0) * 4 + 34).astype(F32)
    power = iota((16, 128), 0).astype(F32)

    def slot(s, lane):
        off_first = xt_ref[pl.ds(s, 1), :]
        off_second = xt_ref[pl.ds(CAP + s, 1), :]
        real_in = xt_ref[pl.ds(2 * CAP + s, 1), :]
        imag_in = xt_ref[pl.ds(3 * CAP + s, 1), :]
        first = off_first + corner_first
        second = off_second + corner_second
        a = speed_first * first
        b = speed_second * second
        root = jnp.sqrt(1.0 + a * a + b * b)
        root = root - jnp.floor(root)
        along = lin_second * second
        for eps in range(2):
            part = root[eps * 16 : eps * 16 + 16]
            lin = (along + first * (2.0 * eps + 1.0)) * (1.0 / 4096.0)
            lin = lin - jnp.floor(lin)
            cosine, sine = turn(lin + jnp.concatenate([part, part], axis=0))
            q_ref[2 * eps] = cosine
            q_ref[2 * eps + 1] = sine
        cosine, sine = turn(power * ((first - second) * (1.0 / 1024.0)))
        z_real = cosine * real_in - sine * imag_in
        z_imag = cosine * imag_in + sine * real_in
        cols = slice(lane * 128, lane * 128 + 128)
        low_cols = slice(256 + lane * 128, 256 + lane * 128 + 128)
        for up in range(16):
            zr = z_real[up : up + 1]
            zi = z_imag[up : up + 1]
            for eps in range(2):
                qr = q_ref[2 * eps, up : up + 16, :]
                qi = q_ref[2 * eps + 1, up : up + 16, :]
                for part, value in enumerate((qr * zr - qi * zi, qr * zi + qi * zr)):
                    high, low = split(value)
                    base = part * 512 + (2 * up + eps) * 16
                    r_ref[base : base + 16, cols] = high
                    r_ref[base : base + 16, low_cols] = low
        first_rows = basis_rows(off_first * (1.0 / width_first))
        second_rows = basis_rows(off_second * (1.0 / width_second))
        for part, value in enumerate(turn(second * (1.0 / 128.0))):
            scaled = second_rows * value
            for t in range(0, ORDER, 2):
                pair = jnp.concatenate([first_rows[t : t + 1] * scaled, first_rows[t + 1 : t + 2] * scaled], axis=0)
                high, low = split(pair)
                base = part * NODES + t * ORDER
                l_ref[base : base + 16, cols] = high
                l_ref[128 + base : 128 + base + 16, cols] = low

    def step(i, carry):
        slot(2 * i, 0)
        slot(2 * i + 1, 1)
        right = l_ref[...]
        for m in range(4):
            rows = slice(m * 256, m * 256 + 256)
            acc_ref[rows, :] += nt(r_ref[rows, :256], right) + nt(r_ref[rows, 256:], right)
        return carry

    lax.fori_loop(0, CAP // 2, step, 0)

    for m in range(4):
        blocks = []
        for part in range(2):
            rows = slice(part * 512 + m * 128, part * 512 + m * 128 + 128)
            blocks.append((acc_ref[rows, :128] + acc_ref[rows, 128:]).T)
        (cr, sr), (ci, si) = [(x[:NODES], x[NODES:]) for x in blocks]
        low_cols = slice(m * 128, m * 128 + 128)
        high_cols = slice(512 + m * 128, 512 + m * 128 + 128)
        out_ref[:NODES, low_cols] = cr + si
        out_ref[NODES:, low_cols] = ci - sr
        out_ref[:NODES, high_cols] = cr - si
        out_ref[NODES:, high_cols] = ci + sr


def leaf(info, arrived):
    return pl.pallas_call(
        leaf_body,
        out_shape=jax.ShapeDtypeStruct((2 * NODES, TARGETS), F32),
        in_specs=[pl.BlockSpec(memory_space=pltpu.SMEM), pl.BlockSpec(memory_space=pltpu.VMEM)],
        out_specs=pl.BlockSpec(memory_space=pltpu.VMEM),
        scratch_shapes=[
            pltpu.VMEM((128, 128), F32),
            pltpu.VMEM((4, TGT, 128), F32),
            pltpu.VMEM((1024, 512), BF16),
            pltpu.VMEM((256, 256), BF16),
            pltpu.VMEM((1024, 256), F32),
        ],
        name="leaf", compiler_params=pltpu.CompilerParams(vmem_limit_bytes=16 << 20),
    )(info, arrived)


def place(index, merged):
    code = jnp.int32(0)
    for bit in range(merged):
        code = code + ((index >> bit) & 1) * 2 ** (merged - 1 - bit)
    return (code.astype(F32) + 0.5) * (1.0 / 2.0**merged)


def node_columns(shape):
    nodes = node_table()
    row = iota(shape, 0)
    first = jnp.zeros(shape, F32)
    second = jnp.zeros(shape, F32)
    for t in range(ORDER):
        first = jnp.where(row // ORDER == t, float(nodes[t]), first)
        second = jnp.where(row % ORDER == t, float(nodes[t]), second)
    return first, second


def speeds(info_ref, klass, place_first, place_second):
    _, wave = turn((klass + (place_first + 2.0 * place_second)) * (1.0 / 32.0))
    one = (32.0 + info_ref[0].astype(F32) + info_ref[1].astype(F32) * wave) * (1.0 / 4096.0)
    two = (32.0 + info_ref[2].astype(F32) + info_ref[3].astype(F32) * wave) * (1.0 / 4096.0)
    return one, two


def root_of(speed, first, second):
    a = speed[0] * first
    b = speed[1] * second
    return jnp.sqrt(1.0 + a * a + b * b)


LEVELS = ((1, 0), (2, 0), (1, 1), (2, 1))


def tables_body(info_ref, gamma_ref, last_ref):
    index_x = info_ref[4]
    index_y = info_ref[5]
    z_first, z_second = node_columns((NODES, 128))
    for tile in range(4):
        lane = iota((1, 128), 1)
        u = tile * 8 + lane // 16
        v = lane % 16
        klass = ((u + 2 * v) % TGT).astype(F32)
        cols = slice(tile * 128, tile * 128 + 128)
        merged = [0, 0]
        for number, (along, level) in enumerate(LEVELS):
            before = list(merged)
            merged[along - 1] += 1
            old = [place(index_x, before[0]), place(index_y, before[1])]
            new = [place(index_x, merged[0]), place(index_y, merged[1])]
            speed_old = speeds(info_ref, klass, *old)
            speed_new = speeds(info_ref, klass, *new)
            index_d = index_x if along == 1 else index_y
            bit = (index_d >> level) & 1
            for who in range(2):
                side = bit if who == 0 else 1 - bit
                child_first = index_x >> before[0]
                child_second = index_y >> before[1]
                if along == 1:
                    child_first = (index_x >> merged[0]) * 2 + side
                else:
                    child_second = (index_y >> merged[1]) * 2 + side
                width_first = float(N // 8 * 2 ** before[0])
                width_second = float(N // 16 * 2 ** before[1])
                first = child_first.astype(F32) * width_first + width_first * z_first
                second = child_second.astype(F32) * width_second + width_second * z_second
                if along == 1:
                    moved = first * ((new[0] - old[0]) * (1.0 / 2048.0))
                else:
                    moved = second * ((new[1] - old[1]) * (1.0 / 1024.0))
                phase = root_of(speed_new, first, second) - root_of(speed_old, first, second) + moved
                cosine, sine = turn(phase)
                gamma_ref[number, who, :NODES, cols] = cosine
                gamma_ref[number, who, NODES:, cols] = sine
        width_first = float(N // 8 * 4)
        width_second = float(N // 16 * 4)
        first = (index_x >> 2).astype(F32) * width_first + width_first * z_first
        second = (index_y >> 2).astype(F32) * width_second + width_second * z_second
        new = [place(index_x, 2), place(index_y, 2)]
        root = root_of(speeds(info_ref, klass, *new), first, second)
        root = root - jnp.floor(root)
        at_first = first * ((u.astype(F32) + new[0]) * (1.0 / 2048.0))
        at_first = at_first - jnp.floor(at_first) + root
        for half in range(2):
            at_second = second * ((v.astype(F32) + (16.0 * half + new[1])) * (1.0 / 1024.0))
            cosine, sine = turn(at_first + at_second)
            wide = slice(half * 512 + tile * 128, half * 512 + tile * 128 + 128)
            last_ref[:NODES, wide] = cosine
            last_ref[NODES:, wide] = sine


def tables(info):
    return pl.pallas_call(
        tables_body,
        out_shape=(
            jax.ShapeDtypeStruct((4, 2, 2 * NODES, 512), F32),
            jax.ShapeDtypeStruct((2 * NODES, TARGETS), F32),
        ),
        in_specs=[pl.BlockSpec(memory_space=pltpu.SMEM)],
        out_specs=[pl.BlockSpec(memory_space=pltpu.VMEM)] * 2,
        name="tables", compiler_params=pltpu.CompilerParams(vmem_limit_bytes=16 << 20),
    )(info)


def merge_body(number, info_ref, own_ref, other_ref, gamma_ref, mix_ref, *rest):
    along, level = LEVELS[number]
    final = number == 3
    out_ref = rest[-1]
    index_d = info_ref[4] if along == 1 else info_ref[5]
    bit = (index_d >> level) & 1
    left = mix_ref[bit]

    def combined(cols, gcols):
        reals, imags = [], []
        for who, ref in ((0, own_ref), (1, other_ref)):
            gr = gamma_ref[number, who, :NODES, gcols]
            gi = gamma_ref[number, who, NODES:, gcols]
            xr = ref[:NODES, cols]
            xi = ref[NODES:, cols]
            reals.append(split(gr * xr - gi * xi))
            imags.append(split(gr * xi + gi * xr))
        out = []
        for parts in (reals, imags):
            right = jnp.concatenate([parts[0][0], parts[1][0], parts[0][1], parts[1][1]], axis=0)
            both = jnp.dot(left, right, preferred_element_type=F32)
            out.append(both[:NODES] + both[NODES:])
        return out

    if not final:
        for tile in range(4):
            cols = slice(tile * 256, tile * 256 + 256)
            gcols = slice((tile % 2) * 256, (tile % 2) * 256 + 256)
            real, imag = combined(cols, gcols)
            out_ref[:NODES, cols] = real
            out_ref[NODES:, cols] = imag
        return
    last_ref = rest[0]
    source = iota((256, 256), 0)
    target = iota((256, 256), 1)
    wanted = ((target // 16) % 2) * 128 + (target // 32) * 16 + target % 16
    order = jnp.where(source == wanted, 1.0, 0.0).astype(BF16)
    for tile in range(4):
        halves = []
        for half in range(2):
            cols = slice(half * 512 + tile * 128, half * 512 + tile * 128 + 128)
            real, imag = combined(cols, slice(tile * 128, tile * 128 + 128))
            cosine = last_ref[:NODES, cols]
            sine = last_ref[NODES:, cols]
            halves.append(jnp.concatenate([cosine * real + sine * imag, cosine * imag - sine * real], axis=0))
        value = jnp.concatenate(halves, axis=1)
        high = value.astype(BF16)
        value = value - high.astype(F32)
        mid, low = split(value)
        moved = jnp.dot(jnp.concatenate([high, mid, low], axis=0), order, preferred_element_type=F32)
        moved = moved[:128] + moved[128:256] + moved[256:]
        out_ref[0, :, tile * 256 : tile * 256 + 256] = moved[:NODES]
        out_ref[1, :, tile * 256 : tile * 256 + 256] = moved[NODES:]


def merge(number, info, own, other, gamma, last):
    final = number == 3
    args = [info, own, other, gamma, jnp.asarray(merge_tables(LEVELS[number][0]))]
    if final:
        args.append(last)
    shape = (2, NODES, TARGETS) if final else (2 * NODES, TARGETS)
    return pl.pallas_call(
        functools.partial(merge_body, number),
        out_shape=jax.ShapeDtypeStruct(shape, F32),
        in_specs=[pl.BlockSpec(memory_space=pltpu.SMEM)] + [pl.BlockSpec(memory_space=pltpu.VMEM)] * (len(args) - 1),
        out_specs=pl.BlockSpec(memory_space=pltpu.VMEM),
        name="merge_%d" % number, compiler_params=pltpu.CompilerParams(vmem_limit_bytes=16 << 20),
    )(*args)


def swap(value, along, level):
    axis = "bx" if along == 1 else "by"
    return lax.ppermute(value, axis, [(i, i ^ 1 << level) for i in range(lax.axis_size(axis))])


def on_device(point_box, point_offset, point_value, coef):
    owners = lax.axis_size("bx") * lax.axis_size("by")
    place_on = jnp.stack([lax.axis_index("bx"), lax.axis_index("by")]).astype(jnp.int32)
    info = jnp.concatenate([coef, place_on])
    sent = pack(point_box.reshape(-1, 128), point_offset, point_value)
    arrived = lax.all_to_all(sent.reshape(owners, 1, -1), ("bx", "by"), split_axis=0, concat_axis=0, tiled=True)
    gamma, last = tables(info)
    holding = leaf(info, arrived.reshape(owners, -1))
    for number, (along, level) in enumerate(LEVELS):
        holding = merge(number, info, holding, swap(holding, along, level), gamma, last)
    return holding


def solution(mesh):
    in_specs = (P(("bx", "by"), None), P(None, ("bx", "by")), P(None, ("bx", "by")), P())
    out_specs = P(None, None, ("bx", "by"))
    return jax.shard_map(on_device, mesh=mesh, in_specs=in_specs, out_specs=out_specs, check_vma=False)
```

```python
import functools
import math

import jax
import jax.numpy as jnp
import numpy as np
from jax import lax
from jax.experimental import pallas as pl
from jax.experimental.pallas import tpu as pltpu
from jax.sharding import PartitionSpec as P

N = 16384
ORDER = 8
TGT = 32
CAP = 32
CHUNKS = 4
GROUPS = 4 // CHUNKS
LANES = 256 * GROUPS
STEP = 8
NODES = ORDER * ORDER
TARGETS = TGT * TGT
F32 = jnp.float32
BF16 = jnp.bfloat16

SIN_C = (3.1415925798055824, -5.167706866167939, 2.550031193519312, -0.5980441939121666, 0.07721838615746283)
COS_C = (0.9999999532476086, -4.934792830619651, 4.058411352862725, -1.3318765680816773, 0.21968961109948903)


def node_table():
    counting = np.arange(ORDER) * 1.0
    return 0.5 - 0.5 * np.cos(np.pi * (2.0 * counting + 1.0) / (2.0 * ORDER))


def child_matrix(side):
    nodes = node_table()
    points = 0.5 * (side + nodes)
    rows = []
    for target in range(ORDER):
        factor = np.ones(ORDER)
        for source in range(ORDER):
            if source != target:
                factor = factor * (points - nodes[source]) / (nodes[target] - nodes[source])
        rows.append(factor)
    return np.stack(rows)


def merge_tables(along):
    eye = np.eye(ORDER)
    both = []
    for bit in range(2):
        parts = []
        for side in (bit, 1 - bit):
            matrix = child_matrix(side)
            parts.append(np.kron(matrix, eye) if along == 1 else np.kron(eye, matrix))
        full = np.concatenate(parts, axis=1)
        high = full.astype(np.float32).astype(BF16)
        low = (full - high.astype(np.float64)).astype(np.float32).astype(BF16)
        top = np.concatenate([high, high], axis=1)
        bottom = np.concatenate([low, np.zeros_like(low)], axis=1)
        both.append(np.concatenate([top, bottom], axis=0))
    return np.stack(both)


def horner(coefs, x):
    total = coefs[-1]
    for c in coefs[-2::-1]:
        total = total * x + c
    return total


def turn(phase):
    r = phase - jnp.floor(phase + 0.5)
    x = r * r
    sine = horner(SIN_C, x) * r
    cosine = horner(COS_C, x)
    twice = sine + sine
    return 1.0 - twice * sine, twice * cosine


def split(x):
    high = x.astype(BF16)
    return high, (x - high.astype(F32)).astype(BF16)


def cost(micros):
    return pl.CostEstimate(flops=0, bytes_accessed=int(micros * 3.7e6), transcendentals=0)


def vmem(count):
    return [pl.BlockSpec(memory_space=pltpu.VMEM)] * count


SMALL = pltpu.CompilerParams(vmem_limit_bytes=12 << 20)


def iota(shape, axis):
    return lax.broadcasted_iota(jnp.int32, shape, axis)


def nt(a, b):
    return lax.dot_general(a, b, (((1,), (1,)), ((), ())), preferred_element_type=F32)


def pack_body(box_ref, off_ref, val_ref, out_ref):
    blocks = box_ref.shape[0]
    row = iota((128, 128), 0)
    row2 = iota((128, 256), 0)
    col2 = iota((128, 256), 1)
    prefix = jnp.where((row2 < col2) | (col2 >= 128), 1.0, 0.0).astype(BF16)
    same = [row == box_ref[b : b + 1, :] for b in range(blocks)]
    ones = [jnp.where(m, 1.0, 0.0).astype(BF16) for m in same]
    counts = jnp.dot(jnp.concatenate(ones, axis=0), prefix, preferred_element_type=F32)
    slots = iota((CAP, 128), 0).astype(F32)
    carry = jnp.zeros((128, 128), F32)
    wide = []
    for b in range(blocks):
        part = counts[b * 128 : (b + 1) * 128]
        rank = jnp.sum(jnp.where(same[b], part[:, :128] + carry, 0.0), axis=0, keepdims=True)
        carry = carry + part[:, 128:]
        hit = slots == rank
        cols = slice(b * 128, (b + 1) * 128)
        values = [off_ref[0:1, cols].astype(F32), off_ref[1:2, cols].astype(F32), val_ref[0:1, cols], val_ref[1:2, cols]]
        pieces = [[], [], []]
        for v in values:
            rest = v
            for piece in pieces:
                top = rest.astype(BF16).astype(F32)
                rest = rest - top
                piece.append(jnp.where(hit, top, 0.0).astype(BF16))
        wide.append(jnp.concatenate([x for piece in pieces for x in piece], axis=0))
    total = nt(jnp.concatenate(ones, axis=1), jnp.concatenate(wide, axis=1))
    out_ref[...] = total[:, :128] + total[:, 128:256] + total[:, 256:]


def pack(box, offsets, values):
    return pl.pallas_call(
        pack_body,
        out_shape=jax.ShapeDtypeStruct((128, 4 * CAP), F32),
        in_specs=[pl.BlockSpec(memory_space=pltpu.VMEM)] * 3,
        out_specs=pl.BlockSpec(memory_space=pltpu.VMEM),
        name="pack",
        cost_estimate=cost(2.0),
    )(box, offsets, values)


def basis_rows(tau):
    nodes = node_table()
    which = iota((ORDER, 128), 0)
    total = None
    for step in range(1, ORDER):
        other = jnp.zeros((ORDER, 128), F32)
        scale = jnp.zeros((ORDER, 128), F32)
        for t in range(ORDER):
            s = (t + step) % ORDER
            other = jnp.where(which == t, float(nodes[s]), other)
            scale = jnp.where(which == t, float(1.0 / (nodes[t] - nodes[s])), scale)
        factor = (tau - other) * scale
        total = factor if total is None else total * factor
    return total


def prepare_body(info_ref, rx_ref, l_ref, q_ref, z_ref, xt_ref):
    width_first, width_second = float(N // 8), float(N // 16)
    corner_first = info_ref[4].astype(F32) * width_first
    corner_second = info_ref[5].astype(F32) * width_second
    xt_ref[...] = rx_ref[...].T

    order = iota((TGT, 128), 0)
    klass = (order % 16) * 2 + order // 16
    _, wave = turn((klass.astype(F32) + 1.5) * (1.0 / 32.0))
    speed_first = (32.0 + info_ref[0].astype(F32) + info_ref[1].astype(F32) * wave) * (1.0 / 4096.0)
    speed_second = (32.0 + info_ref[2].astype(F32) + info_ref[3].astype(F32) * wave) * (1.0 / 4096.0)
    lin_second = (iota((TGT, 128), 0) * 4 + 34).astype(F32)
    power = iota((16, 128), 0).astype(F32)

    for s in range(CAP):
        off_first = xt_ref[s : s + 1, :]
        off_second = xt_ref[CAP + s : CAP + s + 1, :]
        real_in = xt_ref[2 * CAP + s : 2 * CAP + s + 1, :]
        imag_in = xt_ref[3 * CAP + s : 3 * CAP + s + 1, :]
        first = off_first + corner_first
        second = off_second + corner_second
        a = speed_first * first
        b = speed_second * second
        root = jnp.sqrt(1.0 + a * a + b * b)
        root = root - jnp.floor(root)
        along = lin_second * second
        for eps in range(2):
            part = root[eps * 16 : eps * 16 + 16]
            lin = (along + first * (2.0 * eps + 1.0)) * (1.0 / 4096.0)
            lin = lin - jnp.floor(lin)
            cosine, sine = turn(lin + jnp.concatenate([part, part], axis=0))
            q_ref[s, 2 * eps] = cosine
            q_ref[s, 2 * eps + 1] = sine
        cosine, sine = turn(power * ((first - second) * (1.0 / 1024.0)))
        z_ref[s, 0] = cosine * real_in - sine * imag_in
        z_ref[s, 1] = cosine * imag_in + sine * real_in
        cols = slice(s * 128, s * 128 + 128)
        first_rows = basis_rows(off_first * (1.0 / width_first))
        second_rows = basis_rows(off_second * (1.0 / width_second))
        for part, value in enumerate(turn(second * (1.0 / 128.0))):
            scaled = second_rows * value
            for t in range(0, ORDER, 2):
                pair = jnp.concatenate([first_rows[t : t + 1] * scaled, first_rows[t + 1 : t + 2] * scaled], axis=0)
                high, low = split(pair)
                base = part * NODES + t * ORDER
                l_ref[base : base + 16, cols] = high
                l_ref[128 + base : 128 + base + 16, cols] = low


def prepare(info, arrived):
    return pl.pallas_call(
        prepare_body,
        out_shape=(
            jax.ShapeDtypeStruct((256, CAP * 128), BF16),
            jax.ShapeDtypeStruct((CAP, 4, TGT, 128), F32),
            jax.ShapeDtypeStruct((CAP, 2, 16, 128), F32),
        ),
        in_specs=[pl.BlockSpec(memory_space=pltpu.SMEM)] + vmem(1),
        out_specs=vmem(3),
        scratch_shapes=[pltpu.VMEM((128, 128), F32)],
        name="prepare",
        compiler_params=SMALL,
        cost_estimate=cost(2.0),
    )(info, arrived)


def leaf_body(chunk, l_ref, q_ref, z_ref, out_ref, ra_ref, rb_ref, acc_ref):
    half = STEP * 128

    def build(step, r_ref):
        for j in range(STEP):
            s = step * STEP + j
            cols = slice(j * 128, j * 128 + 128)
            low_cols = slice(half + j * 128, half + j * 128 + 128)
            for local in range(4 * GROUPS):
                up = chunk * 4 * GROUPS + local
                zr = z_ref[s, 0, up : up + 1, :]
                zi = z_ref[s, 1, up : up + 1, :]
                for eps in range(2):
                    qr = q_ref[s, 2 * eps, up : up + 16, :]
                    qi = q_ref[s, 2 * eps + 1, up : up + 16, :]
                    for part, value in enumerate((qr * zr - qi * zi, qr * zi + qi * zr)):
                        high, low = split(value)
                        base = (local // 4) * 256 + part * 128 + (2 * (local % 4) + eps) * 16
                        r_ref[base : base + 16, cols] = high
                        r_ref[base : base + 16, low_cols] = low

    steps = CAP // STEP
    build(0, ra_ref)
    for step in range(steps):
        now, later = (ra_ref, rb_ref) if step % 2 == 0 else (rb_ref, ra_ref)
        if step + 1 < steps:
            build(step + 1, later)
        right = l_ref[:, step * half : step * half + half]
        product = nt(now[...], jnp.concatenate([right, right], axis=1))
        if step == 0:
            acc_ref[...] = product
        else:
            acc_ref[...] += product

    for g in range(GROUPS):
        blocks = []
        for part in range(2):
            rows = slice(g * 256 + part * 128, g * 256 + part * 128 + 128)
            blocks.append((acc_ref[rows, :128] + acc_ref[rows, 128:]).T)
        (cr, sr), (ci, si) = [(x[:NODES], x[NODES:]) for x in blocks]
        low_cols = slice(g * 256, g * 256 + 128)
        high_cols = slice(g * 256 + 128, g * 256 + 256)
        out_ref[:NODES, low_cols] = cr + si
        out_ref[NODES:, low_cols] = ci - sr
        out_ref[:NODES, high_cols] = cr - si
        out_ref[NODES:, high_cols] = ci + sr


def leaf(chunk, prepared):
    return pl.pallas_call(
        functools.partial(leaf_body, chunk),
        out_shape=jax.ShapeDtypeStruct((2 * NODES, LANES), F32),
        in_specs=vmem(3),
        out_specs=vmem(1)[0],
        scratch_shapes=[
            pltpu.VMEM((LANES, STEP * 256), BF16),
            pltpu.VMEM((LANES, STEP * 256), BF16),
            pltpu.VMEM((LANES, 256), F32),
        ],
        name="leaf_%d" % chunk,
        compiler_params=SMALL,
        cost_estimate=cost(2.5 * GROUPS),
    )(*prepared)


def place(index, merged):
    code = jnp.int32(0)
    for bit in range(merged):
        code = code + ((index >> bit) & 1) * 2 ** (merged - 1 - bit)
    return (code.astype(F32) + 0.5) * (1.0 / 2.0**merged)


def node_columns(shape):
    nodes = node_table()
    row = iota(shape, 0)
    first = jnp.zeros(shape, F32)
    second = jnp.zeros(shape, F32)
    for t in range(ORDER):
        first = jnp.where(row // ORDER == t, float(nodes[t]), first)
        second = jnp.where(row % ORDER == t, float(nodes[t]), second)
    return first, second


def speeds(info_ref, klass, place_first, place_second):
    _, wave = turn((klass + (place_first + 2.0 * place_second)) * (1.0 / 32.0))
    one = (32.0 + info_ref[0].astype(F32) + info_ref[1].astype(F32) * wave) * (1.0 / 4096.0)
    two = (32.0 + info_ref[2].astype(F32) + info_ref[3].astype(F32) * wave) * (1.0 / 4096.0)
    return one, two


def root_of(speed, first, second):
    a = speed[0] * first
    b = speed[1] * second
    return jnp.sqrt(1.0 + a * a + b * b)


LEVELS = ((1, 0), (2, 0), (1, 1), (2, 1))


def tables_body(numbers, with_last, info_ref, *out_refs):
    index_x = info_ref[4]
    index_y = info_ref[5]
    z_first, z_second = node_columns((NODES, 128))
    for tile in range(4):
        lane = iota((1, 128), 1)
        u = tile * 8 + lane // 16
        v = lane % 16
        klass = ((u + 2 * v) % TGT).astype(F32)
        cols = slice(tile * 128, tile * 128 + 128)
        merged = [0, 0]
        for number, (along, level) in enumerate(LEVELS):
            before = list(merged)
            merged[along - 1] += 1
            if number not in numbers:
                continue
            gamma_ref = out_refs[numbers.index(number)]
            old = [place(index_x, before[0]), place(index_y, before[1])]
            new = [place(index_x, merged[0]), place(index_y, merged[1])]
            speed_old = speeds(info_ref, klass, *old)
            speed_new = speeds(info_ref, klass, *new)
            index_d = index_x if along == 1 else index_y
            bit = (index_d >> level) & 1
            for who in range(2):
                side = bit if who == 0 else 1 - bit
                child_first = index_x >> before[0]
                child_second = index_y >> before[1]
                if along == 1:
                    child_first = (index_x >> merged[0]) * 2 + side
                else:
                    child_second = (index_y >> merged[1]) * 2 + side
                width_first = float(N // 8 * 2 ** before[0])
                width_second = float(N // 16 * 2 ** before[1])
                first = child_first.astype(F32) * width_first + width_first * z_first
                second = child_second.astype(F32) * width_second + width_second * z_second
                if along == 1:
                    moved = first * ((new[0] - old[0]) * (1.0 / 2048.0))
                else:
                    moved = second * ((new[1] - old[1]) * (1.0 / 1024.0))
                phase = root_of(speed_new, first, second) - root_of(speed_old, first, second) + moved
                cosine, sine = turn(phase)
                gamma_ref[who, :NODES, cols] = cosine
                gamma_ref[who, NODES:, cols] = sine
        if not with_last:
            continue
        last_ref = out_refs[-1]
        width_first = float(N // 8 * 4)
        width_second = float(N // 16 * 4)
        first = (index_x >> 2).astype(F32) * width_first + width_first * z_first
        second = (index_y >> 2).astype(F32) * width_second + width_second * z_second
        new = [place(index_x, 2), place(index_y, 2)]
        root = root_of(speeds(info_ref, klass, *new), first, second)
        root = root - jnp.floor(root)
        at_first = first * ((u.astype(F32) + new[0]) * (1.0 / 2048.0))
        at_first = at_first - jnp.floor(at_first) + root
        for half in range(2):
            at_second = second * ((v.astype(F32) + (16.0 * half + new[1])) * (1.0 / 1024.0))
            cosine, sine = turn(at_first + at_second)
            wide = slice(tile * 256 + half * 128, tile * 256 + half * 128 + 128)
            last_ref[:NODES, wide] = cosine
            last_ref[NODES:, wide] = sine


def tables(info, numbers, with_last=False):
    shapes = [jax.ShapeDtypeStruct((2, 2 * NODES, 512), F32)] * len(numbers)
    if with_last:
        shapes.append(jax.ShapeDtypeStruct((2 * NODES, TARGETS), F32))
    return pl.pallas_call(
        functools.partial(tables_body, numbers, with_last),
        out_shape=tuple(shapes),
        in_specs=[pl.BlockSpec(memory_space=pltpu.SMEM)],
        out_specs=vmem(len(shapes)),
        name="tables_" + "".join(str(n) for n in numbers),
        compiler_params=SMALL,
        cost_estimate=cost(0.6 * len(numbers) + 0.6 * with_last),
    )(info)


def combined(number, group, left, own_ref, other_ref, gamma_ref, chunk):
    tile = chunk * GROUPS + group
    gcols = slice(tile * 128, tile * 128 + 128)
    sides = [[], []]
    for half in range(2):
        cols = slice(group * 256 + half * 128, group * 256 + half * 128 + 128)
        reals, imags = [], []
        for who, ref in ((0, own_ref), (1, other_ref)):
            gr = gamma_ref[who, :NODES, gcols]
            gi = gamma_ref[who, NODES:, gcols]
            xr = ref[:NODES, cols]
            xi = ref[NODES:, cols]
            reals.append(split(gr * xr - gi * xi))
            imags.append(split(gr * xi + gi * xr))
        for side, parts in zip(sides, (reals, imags)):
            side.append(jnp.concatenate([parts[0][0], parts[1][0], parts[0][1], parts[1][1]], axis=0))
    out = []
    for side in sides:
        both = jnp.dot(left, jnp.concatenate(side, axis=1), preferred_element_type=F32)
        out.append(both[:NODES] + both[NODES:])
    return out


def merge_body(number, chunk, info_ref, own_ref, other_ref, gamma_ref, mix_ref, out_ref):
    along, level = LEVELS[number]
    index_d = info_ref[4] if along == 1 else info_ref[5]
    left = mix_ref[(index_d >> level) & 1]
    for group in range(GROUPS):
        real, imag = combined(number, group, left, own_ref, other_ref, gamma_ref, chunk)
        cols = slice(group * 256, group * 256 + 256)
        out_ref[:NODES, cols] = real
        out_ref[NODES:, cols] = imag


def merge(number, chunk, info, own, other, gamma):
    return pl.pallas_call(
        functools.partial(merge_body, number, chunk),
        out_shape=jax.ShapeDtypeStruct((2 * NODES, LANES), F32),
        in_specs=[pl.BlockSpec(memory_space=pltpu.SMEM)] + vmem(4),
        out_specs=vmem(1)[0],
        name="merge_%d_%d" % (number, chunk),
        compiler_params=SMALL,
        cost_estimate=cost(0.4 * GROUPS),
    )(info, own, other, gamma, jnp.asarray(merge_tables(LEVELS[number][0])))


def finish_body(chunk, info_ref, own_ref, other_ref, gamma_ref, mix_ref, last_ref, *rest):
    number = 3
    out_ref, wide_ref, sem = rest[-3:]
    left = mix_ref[(info_ref[5] >> 1) & 1]
    source = iota((256, 256), 0)
    target = iota((256, 256), 1)
    wanted = ((target // 16) % 2) * 128 + (target // 32) * 16 + target % 16
    order = jnp.where(source == wanted, 1.0, 0.0).astype(BF16)
    for group in range(GROUPS):
        real, imag = combined(number, group, left, own_ref, other_ref, gamma_ref, chunk)
        tile = chunk * GROUPS + group
        cols = slice(tile * 256, tile * 256 + 256)
        cosine = last_ref[:NODES, cols]
        sine = last_ref[NODES:, cols]
        value = jnp.concatenate([cosine * real + sine * imag, cosine * imag - sine * real], axis=0)
        high = value.astype(BF16)
        value = value - high.astype(F32)
        mid, low = split(value)
        moved = jnp.dot(jnp.concatenate([high, mid, low], axis=0), order, preferred_element_type=F32)
        moved = moved[:128] + moved[128:256] + moved[256:]
        wide_ref[0, :, group * 256 : group * 256 + 256] = moved[:NODES]
        wide_ref[1, :, group * 256 : group * 256 + 256] = moved[NODES:]
    copy = pltpu.make_async_copy(wide_ref, out_ref.at[:, :, chunk * LANES : chunk * LANES + LANES], sem)
    copy.start()
    copy.wait()


def finish(chunk, info, own, other, gamma, last, sofar):
    args = [info, own, other, gamma, jnp.asarray(merge_tables(2)), last]
    specs = [pl.BlockSpec(memory_space=pltpu.SMEM)] + vmem(5)
    aliases = {}
    if sofar is not None:
        aliases = {len(args): 0}
        args.append(sofar)
        specs.append(pl.BlockSpec(memory_space=pl.ANY))
    return pl.pallas_call(
        functools.partial(finish_body, chunk),
        out_shape=jax.ShapeDtypeStruct((2, NODES, TARGETS), F32),
        in_specs=specs,
        out_specs=pl.BlockSpec(memory_space=pl.ANY),
        scratch_shapes=[pltpu.VMEM((2, NODES, LANES), F32), pltpu.SemaphoreType.DMA],
        input_output_aliases=aliases,
        name="finish_%d" % chunk,
        compiler_params=SMALL,
        cost_estimate=cost(0.8 * GROUPS),
    )(*args)


def swap(value, along, level):
    axis = "bx" if along == 1 else "by"
    return lax.ppermute(value, axis, [(i, i ^ 1 << level) for i in range(lax.axis_size(axis))])


def on_device(point_box, point_offset, point_value, coef):
    owners = lax.axis_size("bx") * lax.axis_size("by")
    place_on = jnp.stack([lax.axis_index("bx"), lax.axis_index("by")]).astype(jnp.int32)
    info = jnp.concatenate([coef, place_on])
    sent = pack(point_box.reshape(-1, 128), point_offset, point_value)
    arrived = lax.all_to_all(sent.reshape(owners, 1, -1), ("bx", "by"), split_axis=0, concat_axis=0, tiled=True)
    prepared = prepare(info, arrived.reshape(owners, -1))
    gammas = list(tables(info, (0, 1)))
    *late, last = tables(info, (2, 3), True)
    gammas += late
    chunks = range(CHUNKS)
    holding = [leaf(c, prepared) for c in chunks]
    for number in range(3):
        holding = [merge(number, c, info, holding[c], swap(holding[c], *LEVELS[number]), gammas[number]) for c in chunks]
    out = None
    for c in chunks:
        out = finish(c, info, holding[c], swap(holding[c], *LEVELS[3]), gammas[3], last, out)
    return out


def solution(mesh):
    in_specs = (P(("bx", "by"), None), P(None, ("bx", "by")), P(None, ("bx", "by")), P())
    out_specs = P(None, None, ("bx", "by"))
    return jax.shard_map(on_device, mesh=mesh, in_specs=in_specs, out_specs=out_specs, check_vma=False)
```

```python
import functools
import math

import jax
import jax.numpy as jnp
import numpy as np
from jax import lax
from jax.experimental import pallas as pl
from jax.experimental.pallas import tpu as pltpu
from jax.sharding import PartitionSpec as P

N = 16384
ORDER = 8
TGT = 32
CAP = 32
CHUNKS = ((0, 2), (2, 2))
STEP = 8
NODES = ORDER * ORDER
TARGETS = TGT * TGT
F32 = jnp.float32
BF16 = jnp.bfloat16

SIN_C = (3.1415925798055824, -5.167706866167939, 2.550031193519312, -0.5980441939121666, 0.07721838615746283)
COS_C = (0.9999999532476086, -4.934792830619651, 4.058411352862725, -1.3318765680816773, 0.21968961109948903)


def node_table():
    counting = np.arange(ORDER) * 1.0
    return 0.5 - 0.5 * np.cos(np.pi * (2.0 * counting + 1.0) / (2.0 * ORDER))


def child_matrix(side):
    nodes = node_table()
    points = 0.5 * (side + nodes)
    rows = []
    for target in range(ORDER):
        factor = np.ones(ORDER)
        for source in range(ORDER):
            if source != target:
                factor = factor * (points - nodes[source]) / (nodes[target] - nodes[source])
        rows.append(factor)
    return np.stack(rows)


def merge_tables(along):
    eye = np.eye(ORDER)
    both = []
    for bit in range(2):
        parts = []
        for side in (bit, 1 - bit):
            matrix = child_matrix(side)
            parts.append(np.kron(matrix, eye) if along == 1 else np.kron(eye, matrix))
        full = np.concatenate(parts, axis=1)
        high = full.astype(np.float32).astype(BF16)
        low = (full - high.astype(np.float64)).astype(np.float32).astype(BF16)
        top = np.concatenate([high, high], axis=1)
        bottom = np.concatenate([low, np.zeros_like(low)], axis=1)
        both.append(np.concatenate([top, bottom], axis=0))
    return np.stack(both)


def horner(coefs, x):
    total = coefs[-1]
    for c in coefs[-2::-1]:
        total = total * x + c
    return total


def turn(phase):
    r = phase - jnp.floor(phase + 0.5)
    x = r * r
    sine = horner(SIN_C, x) * r
    cosine = horner(COS_C, x)
    twice = sine + sine
    return 1.0 - twice * sine, twice * cosine


def split(x):
    high = x.astype(BF16)
    return high, (x - high.astype(F32)).astype(BF16)


def cost(micros):
    return pl.CostEstimate(flops=0, bytes_accessed=int(micros * 3.7e6), transcendentals=0)


def vmem(count):
    return [pl.BlockSpec(memory_space=pltpu.VMEM)] * count


def anywhere(count):
    return [pl.BlockSpec(memory_space=pl.ANY)] * count


SMALL = pltpu.CompilerParams(vmem_limit_bytes=12 << 20)


def iota(shape, axis):
    return lax.broadcasted_iota(jnp.int32, shape, axis)


def nt(a, b):
    return lax.dot_general(a, b, (((1,), (1,)), ((), ())), preferred_element_type=F32)


def pack_body(box_ref, off_ref, val_ref, out_ref):
    blocks = box_ref.shape[0]
    row = iota((128, 128), 0)
    row2 = iota((128, 256), 0)
    col2 = iota((128, 256), 1)
    prefix = jnp.where((row2 < col2) | (col2 >= 128), 1.0, 0.0).astype(BF16)
    same = [row == box_ref[b : b + 1, :] for b in range(blocks)]
    ones = [jnp.where(m, 1.0, 0.0).astype(BF16) for m in same]
    counts = jnp.dot(jnp.concatenate(ones, axis=0), prefix, preferred_element_type=F32)
    slots = iota((CAP, 128), 0).astype(F32)
    carry = jnp.zeros((128, 128), F32)
    wide = []
    for b in range(blocks):
        part = counts[b * 128 : (b + 1) * 128]
        rank = jnp.sum(jnp.where(same[b], part[:, :128] + carry, 0.0), axis=0, keepdims=True)
        carry = carry + part[:, 128:]
        hit = slots == rank
        cols = slice(b * 128, (b + 1) * 128)
        values = [off_ref[0:1, cols].astype(F32), off_ref[1:2, cols].astype(F32), val_ref[0:1, cols], val_ref[1:2, cols]]
        pieces = [[], [], []]
        for v in values:
            rest = v
            for piece in pieces:
                top = rest.astype(BF16).astype(F32)
                rest = rest - top
                piece.append(jnp.where(hit, top, 0.0).astype(BF16))
        wide.append(jnp.concatenate([x for piece in pieces for x in piece], axis=0))
    total = nt(jnp.concatenate(ones, axis=1), jnp.concatenate(wide, axis=1))
    out_ref[...] = total[:, :128] + total[:, 128:256] + total[:, 256:]


def pack(box, offsets, values):
    return pl.pallas_call(
        pack_body,
        out_shape=jax.ShapeDtypeStruct((128, 4 * CAP), F32),
        in_specs=[pl.BlockSpec(memory_space=pltpu.VMEM)] * 3,
        out_specs=pl.BlockSpec(memory_space=pltpu.VMEM),
        name="pack",
        cost_estimate=cost(2.0),
    )(box, offsets, values)


def basis_rows(tau):
    nodes = node_table()
    which = iota((ORDER, 128), 0)
    total = None
    for step in range(1, ORDER):
        other = jnp.zeros((ORDER, 128), F32)
        scale = jnp.zeros((ORDER, 128), F32)
        for t in range(ORDER):
            s = (t + step) % ORDER
            other = jnp.where(which == t, float(nodes[s]), other)
            scale = jnp.where(which == t, float(1.0 / (nodes[t] - nodes[s])), scale)
        factor = (tau - other) * scale
        total = factor if total is None else total * factor
    return total


def prepare_body(info_ref, rx_ref, *rest):
    l_ref, q_ref, z_ref, xt_ref, trig_ref = rest[-5:]
    width_first, width_second = float(N // 8), float(N // 16)
    corner_first = info_ref[4].astype(F32) * width_first
    corner_second = info_ref[5].astype(F32) * width_second
    xt_ref[...] = rx_ref[...].T

    order = iota((TGT, 128), 0)
    klass = (order % 16) * 2 + order // 16
    _, wave = turn((klass.astype(F32) + 1.5) * (1.0 / 32.0))
    speed_first = (32.0 + info_ref[0].astype(F32) + info_ref[1].astype(F32) * wave) * (1.0 / 4096.0)
    speed_second = (32.0 + info_ref[2].astype(F32) + info_ref[3].astype(F32) * wave) * (1.0 / 4096.0)
    lin_first = (order // 16 * 2 + 1).astype(F32) * (1.0 / 4096.0)
    lin_second = (order % 16 * 4 + 34).astype(F32) * (1.0 / 4096.0)
    power = iota((16, 128), 0).astype(F32) * (1.0 / 1024.0)

    second_all = xt_ref[CAP : 2 * CAP, :] + corner_second
    cosine, sine = turn(second_all * (1.0 / 128.0))
    trig_ref[0] = cosine
    trig_ref[1] = sine
    trig_ref[2] = 1.0 - 2.0 * sine * sine
    trig_ref[3] = 2.0 * cosine * sine

    for s in range(CAP):
        off_first = xt_ref[s : s + 1, :]
        off_second = xt_ref[CAP + s : CAP + s + 1, :]
        real_in = xt_ref[2 * CAP + s : 2 * CAP + s + 1, :]
        imag_in = xt_ref[3 * CAP + s : 3 * CAP + s + 1, :]
        wrap_real = trig_ref[2, s : s + 1, :]
        wrap_imag = trig_ref[3, s : s + 1, :]
        first = off_first + corner_first
        second = off_second + corner_second
        a = speed_first * first
        b = speed_second * second
        root = jnp.sqrt(1.0 + a * a + b * b)
        root = root - jnp.floor(root)
        lin = lin_first * first + lin_second * second
        cosine, sine = turn(root + (lin - jnp.floor(lin)))
        more_cosine = cosine * wrap_real - sine * wrap_imag
        more_sine = cosine * wrap_imag + sine * wrap_real
        for eps in range(2):
            rows = slice(eps * 16, eps * 16 + 16)
            q_ref[s, 2 * eps, :16] = cosine[rows]
            q_ref[s, 2 * eps, 16:] = more_cosine[rows]
            q_ref[s, 2 * eps + 1, :16] = sine[rows]
            q_ref[s, 2 * eps + 1, 16:] = more_sine[rows]
        cosine, sine = turn(power * (first - second))
        z_ref[s, 0] = cosine * real_in - sine * imag_in
        z_ref[s, 1] = cosine * imag_in + sine * real_in
        cols = slice(s * 128, s * 128 + 128)
        first_rows = basis_rows(off_first * (1.0 / width_first))
        second_rows = basis_rows(off_second * (1.0 / width_second))
        for part in range(2):
            scaled = second_rows * trig_ref[part, s : s + 1, :]
            for t in range(0, ORDER, 2):
                pair = jnp.concatenate([first_rows[t : t + 1] * scaled, first_rows[t + 1 : t + 2] * scaled], axis=0)
                high, low = split(pair)
                base = part * NODES + t * ORDER
                l_ref[base : base + 16, cols] = high
                l_ref[128 + base : 128 + base + 16, cols] = low


def prepare(info, arrived, after):
    return pl.pallas_call(
        prepare_body,
        out_shape=(
            jax.ShapeDtypeStruct((256, CAP * 128), BF16),
            jax.ShapeDtypeStruct((CAP, 4, TGT, 128), F32),
            jax.ShapeDtypeStruct((CAP, 2, 16, 128), F32),
        ),
        in_specs=[pl.BlockSpec(memory_space=pltpu.SMEM)] + vmem(1) + anywhere(len(after)),
        out_specs=vmem(3),
        scratch_shapes=[pltpu.VMEM((128, 128), F32), pltpu.VMEM((4, CAP, 128), F32)],
        name="prepare",
        compiler_params=SMALL,
        cost_estimate=cost(2.0),
    )(info, arrived, *after)


def leaf_body(chunk, l_ref, q_ref, z_ref, *rest):
    start, groups = chunk
    out_ref, ra_ref, rb_ref, acc_ref = rest[-4:]
    half = STEP * 128

    def build(step, r_ref):
        for j in range(STEP):
            s = step * STEP + j
            cols = slice(j * 128, j * 128 + 128)
            low_cols = slice(half + j * 128, half + j * 128 + 128)
            for local in range(4 * groups):
                up = start * 4 + local
                zr = z_ref[s, 0, up : up + 1, :]
                zi = z_ref[s, 1, up : up + 1, :]
                for eps in range(2):
                    qr = q_ref[s, 2 * eps, up : up + 16, :]
                    qi = q_ref[s, 2 * eps + 1, up : up + 16, :]
                    for part, value in enumerate((qr * zr - qi * zi, qr * zi + qi * zr)):
                        high, low = split(value)
                        base = (local // 4) * 256 + part * 128 + (2 * (local % 4) + eps) * 16
                        r_ref[base : base + 16, cols] = high
                        r_ref[base : base + 16, low_cols] = low

    steps = CAP // STEP
    build(0, ra_ref)
    for step in range(steps):
        now, later = (ra_ref, rb_ref) if step % 2 == 0 else (rb_ref, ra_ref)
        if step + 1 < steps:
            build(step + 1, later)
        right = l_ref[:, step * half : step * half + half]
        product = nt(now[...], jnp.concatenate([right, right], axis=1))
        if step == 0:
            acc_ref[...] = product
        else:
            acc_ref[...] += product

    for g in range(groups):
        blocks = []
        for part in range(2):
            rows = slice(g * 256 + part * 128, g * 256 + part * 128 + 128)
            blocks.append((acc_ref[rows, :128] + acc_ref[rows, 128:]).T)
        (cr, sr), (ci, si) = [(x[:NODES], x[NODES:]) for x in blocks]
        low_cols = slice(g * 256, g * 256 + 128)
        high_cols = slice(g * 256 + 128, g * 256 + 256)
        out_ref[:NODES, low_cols] = cr + si
        out_ref[NODES:, low_cols] = ci - sr
        out_ref[:NODES, high_cols] = cr - si
        out_ref[NODES:, high_cols] = ci + sr


def leaf(chunk, prepared, after):
    lanes = 256 * chunk[1]
    return pl.pallas_call(
        functools.partial(leaf_body, chunk),
        out_shape=jax.ShapeDtypeStruct((2 * NODES, lanes), F32),
        in_specs=vmem(3) + anywhere(len(after)),
        out_specs=vmem(1)[0],
        scratch_shapes=[
            pltpu.VMEM((lanes, STEP * 256), BF16),
            pltpu.VMEM((lanes, STEP * 256), BF16),
            pltpu.VMEM((lanes, 256), F32),
        ],
        name="leaf_%d" % chunk[0],
        compiler_params=SMALL,
        cost_estimate=cost(2.3 * chunk[1]),
    )(*prepared, *after)


def place(index, merged):
    code = jnp.int32(0)
    for bit in range(merged):
        code = code + ((index >> bit) & 1) * 2 ** (merged - 1 - bit)
    return (code.astype(F32) + 0.5) * (1.0 / 2.0**merged)


def node_columns(shape):
    nodes = node_table()
    row = iota(shape, 0)
    first = jnp.zeros(shape, F32)
    second = jnp.zeros(shape, F32)
    for t in range(ORDER):
        first = jnp.where(row // ORDER == t, float(nodes[t]), first)
        second = jnp.where(row % ORDER == t, float(nodes[t]), second)
    return first, second


def speeds(info_ref, klass, at):
    _, wave = turn((klass + at) * (1.0 / 32.0))
    one = (32.0 + info_ref[0].astype(F32) + info_ref[1].astype(F32) * wave) * (1.0 / 4096.0)
    two = (32.0 + info_ref[2].astype(F32) + info_ref[3].astype(F32) * wave) * (1.0 / 4096.0)
    return one, two


def root_of(speed, first, second):
    a = speed[0] * first
    b = speed[1] * second
    return jnp.sqrt(1.0 + a * a + b * b)


LEVELS = ((1, 0), (2, 0), (1, 1), (2, 1))


def exact(x):
    high = x.astype(BF16)
    mid, low = split(x - high.astype(F32))
    return jnp.concatenate([high, mid, low], axis=0)


def spread(values, out_ref, columns):
    klass = iota((TGT * 4, 512), 0)
    lane = iota((TGT * 4, 512), 1)
    pick = jnp.where(klass == (lane // 16 + 2 * (lane % 16)) % TGT + TGT * columns, 1.0, 0.0).astype(BF16)
    moved = jnp.dot(values, pick, preferred_element_type=F32)
    rows = 2 * NODES
    out_ref[...] = moved[:rows] + moved[rows : 2 * rows] + moved[2 * rows :]


def tables_body(pair, info_ref, mix_first_ref, mix_second_ref, *rest):
    gamma_refs = [rest[-5 + k] for k in range(4)] if pair == 0 else [rest[-4 + k] for k in range(4)]
    index_x = info_ref[4]
    index_y = info_ref[5]
    z_first, z_second = node_columns((NODES, 128))
    lane = iota((1, 128), 1)
    klass = (lane % TGT).astype(F32)
    which = lane // TGT
    quads = [[], [], [], [], []]
    merged = [0, 0]
    for number, (along, level) in enumerate(LEVELS):
        before = list(merged)
        merged[along - 1] += 1
        if number // 2 != pair:
            continue
        old = [place(index_x, before[0]), place(index_y, before[1])]
        new = [place(index_x, merged[0]), place(index_y, merged[1])]
        index_d = index_x if along == 1 else index_y
        bit = (index_d >> level) & 1
        for who in range(2):
            side = bit if who == 0 else 1 - bit
            child_first = index_x >> before[0]
            child_second = index_y >> before[1]
            if along == 1:
                child_first = (index_x >> merged[0]) * 2 + side
            else:
                child_second = (index_y >> merged[1]) * 2 + side
            width_first = float(N // 8 * 2 ** before[0])
            width_second = float(N // 16 * 2 ** before[1])
            quads[0].append((child_first.astype(F32) * width_first, width_first))
            quads[1].append((child_second.astype(F32) * width_second, width_second))
            quads[2].append((old[0] + 2.0 * old[1], 0.0))
            quads[3].append((new[0] + 2.0 * new[1], 0.0))
            quads[4].append(((new[0] - old[0]) * (1.0 / 2048.0), (new[1] - old[1]) * (1.0 / 1024.0)))

    def lanes(values):
        out = jnp.zeros((1, 128), F32) + values[0]
        for k in range(1, 4):
            out = jnp.where(which == k, values[k], out)
        return out

    (first_at, first_width), (second_at, second_width), (old_at, _), (new_at, _), (move_first, move_second) = [
        (lanes([q[0] for q in quad]), lanes([q[1] for q in quad])) for quad in quads
    ]
    first = first_at + first_width * z_first
    second = second_at + second_width * z_second
    moved = first * move_first + second * move_second
    phase = root_of(speeds(info_ref, klass, new_at), first, second) - root_of(speeds(info_ref, klass, old_at), first, second)
    values = exact(jnp.concatenate(turn(phase + moved), axis=0))
    for k in range(4):
        spread(values, gamma_refs[k], k)
    if pair == 0:
        mix_ref = rest[-1]
        for number, (along, level) in enumerate(LEVELS):
            index_d = index_x if along == 1 else index_y
            mix_ref[number] = (mix_first_ref if along == 1 else mix_second_ref)[(index_d >> level) & 1]


def tables(info, pair, after=()):
    shapes = [jax.ShapeDtypeStruct((2 * NODES, 512), F32)] * 4
    if pair == 0:
        shapes.append(jax.ShapeDtypeStruct((4, 128, 256), BF16))
    return pl.pallas_call(
        functools.partial(tables_body, pair),
        out_shape=tuple(shapes),
        in_specs=[pl.BlockSpec(memory_space=pltpu.SMEM)] + vmem(2) + anywhere(len(after)),
        out_specs=vmem(len(shapes)),
        name="tables_%d" % pair,
        compiler_params=SMALL,
        cost_estimate=cost(0.8),
    )(info, jnp.asarray(merge_tables(1)), jnp.asarray(merge_tables(2)), *after)


def last_body(info_ref, *rest):
    last_ref, order_ref = rest[-2:]
    index_x = info_ref[4]
    index_y = info_ref[5]
    z_first, z_second = node_columns((NODES, 128))
    width_first = float(N // 8 * 4)
    width_second = float(N // 16 * 4)
    first = (index_x >> 2).astype(F32) * width_first + width_first * z_first
    second = (index_y >> 2).astype(F32) * width_second + width_second * z_second
    new = [place(index_x, 2), place(index_y, 2)]
    lane = iota((1, 128), 1)
    v = lane % 16
    for tile in range(4):
        u = tile * 8 + lane // 16
        klass = ((u + 2 * v) % TGT).astype(F32)
        root = root_of(speeds(info_ref, klass, new[0] + 2.0 * new[1]), first, second)
        root = root - jnp.floor(root)
        at_first = first * ((u.astype(F32) + new[0]) * (1.0 / 2048.0))
        at_first = at_first - jnp.floor(at_first) + root
        for half in range(2):
            at_second = second * ((v.astype(F32) + (16.0 * half + new[1])) * (1.0 / 1024.0))
            cosine, sine = turn(at_first + at_second)
            wide = slice(tile * 256 + half * 128, tile * 256 + half * 128 + 128)
            last_ref[:NODES, wide] = cosine
            last_ref[NODES:, wide] = sine
    source = iota((256, 256), 0)
    target = iota((256, 256), 1)
    wanted = ((target // 16) % 2) * 128 + (target // 32) * 16 + target % 16
    order_ref[...] = jnp.where(source == wanted, 1.0, 0.0).astype(BF16)


def last_tables(info, after):
    return pl.pallas_call(
        last_body,
        out_shape=(jax.ShapeDtypeStruct((2 * NODES, TARGETS), F32), jax.ShapeDtypeStruct((256, 256), BF16)),
        in_specs=[pl.BlockSpec(memory_space=pltpu.SMEM)] + anywhere(len(after)),
        out_specs=vmem(2),
        name="last",
        compiler_params=SMALL,
        cost_estimate=cost(0.8),
    )(info, *after)


def combined(start, group, left, own_ref, other_ref, gamma_refs):
    gcols = slice((start + group) * 128, (start + group) * 128 + 128)
    sides = [[], []]
    for half in range(2):
        cols = slice(group * 256 + half * 128, group * 256 + half * 128 + 128)
        reals, imags = [], []
        for gamma_ref, ref in zip(gamma_refs, (own_ref, other_ref)):
            gr = gamma_ref[:NODES, gcols]
            gi = gamma_ref[NODES:, gcols]
            xr = ref[:NODES, cols]
            xi = ref[NODES:, cols]
            reals.append(split(gr * xr - gi * xi))
            imags.append(split(gr * xi + gi * xr))
        for side, parts in zip(sides, (reals, imags)):
            side.append(jnp.concatenate([parts[0][0], parts[1][0], parts[0][1], parts[1][1]], axis=0))
    out = []
    for side in sides:
        both = jnp.dot(left, jnp.concatenate(side, axis=1), preferred_element_type=F32)
        out.append(both[:NODES] + both[NODES:])
    return out


def merge_body(number, chunk, own_ref, other_ref, gamma_own_ref, gamma_other_ref, mix_ref, *rest):
    start, groups = chunk
    out_ref = rest[-1]
    left = mix_ref[number]
    for group in range(groups):
        real, imag = combined(start, group, left, own_ref, other_ref, (gamma_own_ref, gamma_other_ref))
        cols = slice(group * 256, group * 256 + 256)
        out_ref[:NODES, cols] = real
        out_ref[NODES:, cols] = imag


def merge(number, chunk, own, other, gammas, mix, after=()):
    return pl.pallas_call(
        functools.partial(merge_body, number, chunk),
        out_shape=jax.ShapeDtypeStruct((2 * NODES, 256 * chunk[1]), F32),
        in_specs=vmem(5) + anywhere(len(after)),
        out_specs=vmem(1)[0],
        name="merge_%d_%d" % (number, chunk[0]),
        compiler_params=SMALL,
        cost_estimate=cost(0.2 + 0.2 * chunk[1]),
    )(own, other, *gammas, mix, *after)


def finish_body(chunk, own_ref, other_ref, gamma_own_ref, gamma_other_ref, mix_ref, last_ref, order_ref, *rest):
    start, groups = chunk
    out_ref, wide_ref, sem = rest[-3:]
    left = mix_ref[3]
    for group in range(groups):
        real, imag = combined(start, group, left, own_ref, other_ref, (gamma_own_ref, gamma_other_ref))
        tile = start + group
        cols = slice(tile * 256, tile * 256 + 256)
        cosine = last_ref[:NODES, cols]
        sine = last_ref[NODES:, cols]
        value = jnp.concatenate([cosine * real + sine * imag, cosine * imag - sine * real], axis=0)
        moved = jnp.dot(exact(value), order_ref[...], preferred_element_type=F32)
        moved = moved[:128] + moved[128:256] + moved[256:]
        wide_ref[0, :, group * 256 : group * 256 + 256] = moved[:NODES]
        wide_ref[1, :, group * 256 : group * 256 + 256] = moved[NODES:]
    copy = pltpu.make_async_copy(wide_ref, out_ref.at[:, :, start * 256 : (start + groups) * 256], sem)
    copy.start()
    copy.wait()


def finish(chunk, own, other, gammas, mix, lasts, sofar):
    args = [own, other, *gammas, mix, *lasts]
    specs = vmem(7)
    aliases = {}
    if sofar is not None:
        aliases = {len(args): 0}
        args.append(sofar)
        specs = specs + anywhere(1)
    return pl.pallas_call(
        functools.partial(finish_body, chunk),
        out_shape=jax.ShapeDtypeStruct((2, NODES, TARGETS), F32),
        in_specs=specs,
        out_specs=anywhere(1)[0],
        scratch_shapes=[pltpu.VMEM((2, NODES, 256 * chunk[1]), F32), pltpu.SemaphoreType.DMA],
        input_output_aliases=aliases,
        name="finish_%d" % chunk[0],
        compiler_params=SMALL,
        cost_estimate=cost(0.7 + 0.3 * chunk[1]),
    )(*args)


def swap(value, along, level):
    axis = "bx" if along == 1 else "by"
    return lax.ppermute(value, axis, [(i, i ^ 1 << level) for i in range(lax.axis_size(axis))])


def on_device(point_box, point_offset, point_value, coef):
    owners = lax.axis_size("bx") * lax.axis_size("by")
    place_on = jnp.stack([lax.axis_index("bx"), lax.axis_index("by")]).astype(jnp.int32)
    info = jnp.concatenate([coef, place_on])
    sent = pack(point_box.reshape(-1, 128), point_offset, point_value)
    arrived = lax.all_to_all(sent.reshape(owners, 1, -1), ("bx", "by"), split_axis=0, concat_axis=0, tiled=True)
    *gammas, mix = tables(info, 0)
    prepared = prepare(info, arrived.reshape(owners, -1), (mix,))
    leaf_a = leaf(CHUNKS[0], prepared, ())
    other = swap(leaf_a, *LEVELS[0])
    first = merge(0, CHUNKS[0], leaf_a, other, gammas[:2], mix)
    leaf_b = leaf(CHUNKS[1], prepared, (leaf_a,))
    gammas += tables(info, 1, (leaf_b,))
    second = merge(0, CHUNKS[1], leaf_b, swap(leaf_b, *LEVELS[0]), gammas[:2], mix, (gammas[4],))
    holding = [first, second]
    lasts = last_tables(info, (second,))
    for number in (1, 2):
        pair = gammas[2 * number : 2 * number + 2]
        holding = [merge(number, c, x, swap(x, *LEVELS[number]), pair, mix) for c, x in zip(CHUNKS, holding)]
    out = None
    for c, x in zip(CHUNKS, holding):
        out = finish(c, x, swap(x, *LEVELS[3]), gammas[6:], mix, lasts, out)
    return out


def solution(mesh):
    in_specs = (P(("bx", "by"), None), P(None, ("bx", "by")), P(None, ("bx", "by")), P())
    out_specs = P(None, None, ("bx", "by"))
    return jax.shard_map(on_device, mesh=mesh, in_specs=in_specs, out_specs=out_specs, check_vma=False)
```

```python
import functools
import math

import jax
import jax.numpy as jnp
import numpy as np
from jax import lax
from jax.experimental import pallas as pl
from jax.experimental.pallas import tpu as pltpu
from jax.sharding import PartitionSpec as P

N = 16384
ORDER = 8
TGT = 32
CAP = 32
CHUNKS = ((0, 1), (1, 1), (2, 1), (3, 1))
STEP = 8
NODES = ORDER * ORDER
TARGETS = TGT * TGT
F32 = jnp.float32
BF16 = jnp.bfloat16

SIN_C = (3.1415925798055824, -5.167706866167939, 2.550031193519312, -0.5980441939121666, 0.07721838615746283)
COS_C = (0.9999999532476086, -4.934792830619651, 4.058411352862725, -1.3318765680816773, 0.21968961109948903)


def node_table():
    counting = np.arange(ORDER) * 1.0
    return 0.5 - 0.5 * np.cos(np.pi * (2.0 * counting + 1.0) / (2.0 * ORDER))


def horner(coefs, x):
    total = coefs[-1]
    for c in coefs[-2::-1]:
        total = total * x + c
    return total


def turn(phase):
    r = phase - jnp.floor(phase + 0.5)
    x = r * r
    sine = horner(SIN_C, x) * r
    cosine = horner(COS_C, x)
    twice = sine + sine
    return 1.0 - twice * sine, twice * cosine


def split(x):
    high = x.astype(BF16)
    return high, (x - high.astype(F32)).astype(BF16)


def cost(micros):
    return pl.CostEstimate(flops=0, bytes_accessed=int(micros * 3.7e6), transcendentals=0)


def vmem(count):
    return [pl.BlockSpec(memory_space=pltpu.VMEM)] * count


def anywhere(count):
    return [pl.BlockSpec(memory_space=pl.ANY)] * count


SMALL = pltpu.CompilerParams(vmem_limit_bytes=12 << 20)


def iota(shape, axis):
    return lax.broadcasted_iota(jnp.int32, shape, axis)


def nt(a, b):
    return lax.dot_general(a, b, (((1,), (1,)), ((), ())), preferred_element_type=F32)


def pack_body(box_ref, off_ref, val_ref, out_ref):
    blocks = box_ref.shape[0]
    row = iota((128, 128), 0)
    row2 = iota((128, 256), 0)
    col2 = iota((128, 256), 1)
    prefix = jnp.where((row2 < col2) | (col2 >= 128), 1.0, 0.0).astype(BF16)
    same = [row == box_ref[b : b + 1, :] for b in range(blocks)]
    ones = [jnp.where(m, 1.0, 0.0).astype(BF16) for m in same]
    counts = jnp.dot(jnp.concatenate(ones, axis=0), prefix, preferred_element_type=F32)
    slots = iota((CAP, 128), 0).astype(F32)
    carry = jnp.zeros((128, 128), F32)
    wide = []
    for b in range(blocks):
        part = counts[b * 128 : (b + 1) * 128]
        rank = jnp.sum(jnp.where(same[b], part[:, :128] + carry, 0.0), axis=0, keepdims=True)
        carry = carry + part[:, 128:]
        hit = slots == rank
        cols = slice(b * 128, (b + 1) * 128)
        values = [off_ref[0:1, cols].astype(F32), off_ref[1:2, cols].astype(F32), val_ref[0:1, cols], val_ref[1:2, cols]]
        pieces = [[], [], []]
        for v in values:
            rest = v
            for piece in pieces:
                top = rest.astype(BF16).astype(F32)
                rest = rest - top
                piece.append(jnp.where(hit, top, 0.0).astype(BF16))
        wide.append(jnp.concatenate([x for piece in pieces for x in piece], axis=0))
    total = nt(jnp.concatenate(ones, axis=1), jnp.concatenate(wide, axis=1))
    out_ref[...] = total[:, :128] + total[:, 128:256] + total[:, 256:]


def pack(box, offsets, values):
    return pl.pallas_call(
        pack_body,
        out_shape=jax.ShapeDtypeStruct((128, 4 * CAP), F32),
        in_specs=[pl.BlockSpec(memory_space=pltpu.VMEM)] * 3,
        out_specs=pl.BlockSpec(memory_space=pltpu.VMEM),
        name="pack",
        cost_estimate=cost(2.0),
    )(box, offsets, values)


def basis_rows(tau):
    nodes = node_table()
    which = iota((ORDER, 128), 0)
    total = None
    for step in range(1, ORDER):
        other = jnp.zeros((ORDER, 128), F32)
        scale = jnp.zeros((ORDER, 128), F32)
        for t in range(ORDER):
            s = (t + step) % ORDER
            other = jnp.where(which == t, float(nodes[s]), other)
            scale = jnp.where(which == t, float(1.0 / (nodes[t] - nodes[s])), scale)
        factor = (tau - other) * scale
        total = factor if total is None else total * factor
    return total


def prepare_body(rx_ref, speed_ref, *rest):
    l_ref, q_ref, z_ref, xt_ref, trig_ref = rest[-5:]
    width_first, width_second = float(N // 8), float(N // 16)
    corner_first = lax.axis_index("bx").astype(F32) * width_first
    corner_second = lax.axis_index("by").astype(F32) * width_second
    xt_ref[...] = rx_ref[...].T

    order = iota((TGT, 128), 0)
    speed_first = speed_ref[0]
    speed_second = speed_ref[1]
    lin_first = (order // 16 * 2 + 1).astype(F32) * (1.0 / 4096.0)
    lin_second = (order % 16 * 4 + 34).astype(F32) * (1.0 / 4096.0)
    power = iota((16, 128), 0).astype(F32) * (1.0 / 1024.0)

    second_all = xt_ref[CAP : 2 * CAP, :] + corner_second
    cosine, sine = turn(second_all * (1.0 / 128.0))
    trig_ref[0] = cosine
    trig_ref[1] = sine
    trig_ref[2] = 1.0 - 2.0 * sine * sine
    trig_ref[3] = 2.0 * cosine * sine

    for s in range(CAP):
        off_first = xt_ref[s : s + 1, :]
        off_second = xt_ref[CAP + s : CAP + s + 1, :]
        real_in = xt_ref[2 * CAP + s : 2 * CAP + s + 1, :]
        imag_in = xt_ref[3 * CAP + s : 3 * CAP + s + 1, :]
        wrap_real = trig_ref[2, s : s + 1, :]
        wrap_imag = trig_ref[3, s : s + 1, :]
        first = off_first + corner_first
        second = off_second + corner_second
        a = speed_first * first
        b = speed_second * second
        root = jnp.sqrt(1.0 + a * a + b * b)
        root = root - jnp.floor(root)
        lin = lin_first * first + lin_second * second
        cosine, sine = turn(root + (lin - jnp.floor(lin)))
        more_cosine = cosine * wrap_real - sine * wrap_imag
        more_sine = cosine * wrap_imag + sine * wrap_real
        for eps in range(2):
            rows = slice(eps * 16, eps * 16 + 16)
            q_ref[s, 2 * eps, :16] = cosine[rows]
            q_ref[s, 2 * eps, 16:] = more_cosine[rows]
            q_ref[s, 2 * eps + 1, :16] = sine[rows]
            q_ref[s, 2 * eps + 1, 16:] = more_sine[rows]
        cosine, sine = turn(power * (first - second))
        z_ref[s, 0] = cosine * real_in - sine * imag_in
        z_ref[s, 1] = cosine * imag_in + sine * real_in
        cols = slice(s * 128, s * 128 + 128)
        first_rows = basis_rows(off_first * (1.0 / width_first))
        second_rows = basis_rows(off_second * (1.0 / width_second))
        for part in range(2):
            scaled = second_rows * trig_ref[part, s : s + 1, :]
            for t in range(0, ORDER, 2):
                pair = jnp.concatenate([first_rows[t : t + 1] * scaled, first_rows[t + 1 : t + 2] * scaled], axis=0)
                high, low = split(pair)
                base = part * NODES + t * ORDER
                l_ref[base : base + 16, cols] = high
                l_ref[128 + base : 128 + base + 16, cols] = low


def prepare(arrived, speed):
    return pl.pallas_call(
        prepare_body,
        out_shape=(
            jax.ShapeDtypeStruct((256, CAP * 128), BF16),
            jax.ShapeDtypeStruct((CAP, 4, TGT, 128), F32),
            jax.ShapeDtypeStruct((CAP, 2, 16, 128), F32),
        ),
        in_specs=vmem(2),
        out_specs=vmem(3),
        scratch_shapes=[pltpu.VMEM((128, 128), F32), pltpu.VMEM((4, CAP, 128), F32)],
        name="prepare",
        compiler_params=SMALL,
        cost_estimate=cost(2.0),
    )(arrived, speed)


def leaf_body(chunk, l_ref, q_ref, z_ref, *rest):
    start, groups = chunk
    out_ref, ra_ref, rb_ref, acc_ref = rest[-4:]
    half = STEP * 128

    def build(step, r_ref):
        for j in range(STEP):
            s = step * STEP + j
            cols = slice(j * 128, j * 128 + 128)
            low_cols = slice(half + j * 128, half + j * 128 + 128)
            for local in range(4 * groups):
                up = start * 4 + local
                zr = z_ref[s, 0, up : up + 1, :]
                zi = z_ref[s, 1, up : up + 1, :]
                for eps in range(2):
                    qr = q_ref[s, 2 * eps, up : up + 16, :]
                    qi = q_ref[s, 2 * eps + 1, up : up + 16, :]
                    for part, value in enumerate((qr * zr - qi * zi, qr * zi + qi * zr)):
                        high, low = split(value)
                        base = (local // 4) * 256 + part * 128 + (2 * (local % 4) + eps) * 16
                        r_ref[base : base + 16, cols] = high
                        r_ref[base : base + 16, low_cols] = low

    steps = CAP // STEP
    build(0, ra_ref)
    for step in range(steps):
        now, later = (ra_ref, rb_ref) if step % 2 == 0 else (rb_ref, ra_ref)
        if step + 1 < steps:
            build(step + 1, later)
        right = l_ref[:, step * half : step * half + half]
        product = nt(now[...], jnp.concatenate([right, right], axis=1))
        if step == 0:
            acc_ref[...] = product
        else:
            acc_ref[...] += product

    for g in range(groups):
        blocks = []
        for part in range(2):
            rows = slice(g * 256 + part * 128, g * 256 + part * 128 + 128)
            blocks.append((acc_ref[rows, :128] + acc_ref[rows, 128:]).T)
        (cr, sr), (ci, si) = [(x[:NODES], x[NODES:]) for x in blocks]
        low_cols = slice(g * 256, g * 256 + 128)
        high_cols = slice(g * 256 + 128, g * 256 + 256)
        out_ref[:NODES, low_cols] = cr + si
        out_ref[NODES:, low_cols] = ci - sr
        out_ref[:NODES, high_cols] = cr - si
        out_ref[NODES:, high_cols] = ci + sr


def leaf(chunk, prepared, after):
    lanes = 256 * chunk[1]
    return pl.pallas_call(
        functools.partial(leaf_body, chunk),
        out_shape=jax.ShapeDtypeStruct((2 * NODES, lanes), F32),
        in_specs=vmem(3) + anywhere(len(after)),
        out_specs=vmem(1)[0],
        scratch_shapes=[
            pltpu.VMEM((lanes, STEP * 256), BF16),
            pltpu.VMEM((lanes, STEP * 256), BF16),
            pltpu.VMEM((lanes, 256), F32),
        ],
        name="leaf_%d" % chunk[0],
        compiler_params=SMALL,
        cost_estimate=cost(2.3 * chunk[1]),
    )(*prepared, *after)


def place(index, merged):
    code = jnp.int32(0)
    for bit in range(merged):
        code = code + ((index >> bit) & 1) * 2 ** (merged - 1 - bit)
    return (code.astype(F32) + 0.5) * (1.0 / 2.0**merged)


def node_columns(shape):
    nodes = node_table()
    row = iota(shape, 0)
    first = jnp.zeros(shape, F32)
    second = jnp.zeros(shape, F32)
    for t in range(ORDER):
        first = jnp.where(row // ORDER == t, float(nodes[t]), first)
        second = jnp.where(row % ORDER == t, float(nodes[t]), second)
    return first, second


def speeds(info_ref, klass, at):
    _, wave = turn((klass + at) * (1.0 / 32.0))
    one = (32.0 + info_ref[0].astype(F32) + info_ref[1].astype(F32) * wave) * (1.0 / 4096.0)
    two = (32.0 + info_ref[2].astype(F32) + info_ref[3].astype(F32) * wave) * (1.0 / 4096.0)
    return one, two


def root_of(speed, first, second):
    a = speed[0] * first
    b = speed[1] * second
    return jnp.sqrt(1.0 + a * a + b * b)


LEVELS = ((1, 0), (2, 0), (1, 1), (2, 1))


def exact(x):
    high = x.astype(BF16)
    mid, low = split(x - high.astype(F32))
    return jnp.concatenate([high, mid, low], axis=0)


def spread(values, out_ref, columns):
    klass = iota((TGT * 4, 512), 0)
    lane = iota((TGT * 4, 512), 1)
    pick = jnp.where(klass == (lane // 16 + 2 * (lane % 16)) % TGT + TGT * columns, 1.0, 0.0).astype(BF16)
    moved = jnp.dot(values, pick, preferred_element_type=F32)
    rows = 2 * NODES
    out_ref[...] = moved[:rows] + moved[rows : 2 * rows] + moved[2 * rows :]


def mix_of(number):
    along, level = LEVELS[number]
    bit = (lax.axis_index("bx" if along == 1 else "by") >> level) & 1
    nodes = node_table()
    lane = iota((1, 128), 1)
    who = lane // NODES
    first = lane // ORDER % ORDER
    second = lane % ORDER
    source = first if along == 1 else second
    at = jnp.zeros((1, 128), F32)
    for t in range(ORDER):
        at = jnp.where(source == t, float(nodes[t]), at)
    side = jnp.where(who == 0, bit, 1 - bit).astype(F32)
    rows = basis_rows((at + side) * 0.5)
    row = iota((ORDER, 128), 0)
    full = []
    for t in range(ORDER):
        if along == 1:
            full.append(jnp.where(row == second, rows[t : t + 1], 0.0))
        else:
            full.append(jnp.where(first == t, rows, 0.0))
    high, low = split(jnp.concatenate(full, axis=0))
    top = jnp.concatenate([high, high], axis=1)
    bottom = jnp.concatenate([low, jnp.zeros_like(low)], axis=1)
    return jnp.concatenate([top, bottom], axis=0)


def tables_body(pair, info_ref, *rest):
    gamma_refs = [rest[-6 + k] for k in range(4)] if pair == 0 else [rest[-4 + k] for k in range(4)]
    index_x = lax.axis_index("bx")
    index_y = lax.axis_index("by")
    z_first, z_second = node_columns((NODES, 128))
    lane = iota((1, 128), 1)
    klass = (lane % TGT).astype(F32)
    which = lane // TGT
    quads = [[], [], [], [], []]
    merged = [0, 0]
    for number, (along, level) in enumerate(LEVELS):
        before = list(merged)
        merged[along - 1] += 1
        if number // 2 != pair:
            continue
        old = [place(index_x, before[0]), place(index_y, before[1])]
        new = [place(index_x, merged[0]), place(index_y, merged[1])]
        index_d = index_x if along == 1 else index_y
        bit = (index_d >> level) & 1
        for who in range(2):
            side = bit if who == 0 else 1 - bit
            child_first = index_x >> before[0]
            child_second = index_y >> before[1]
            if along == 1:
                child_first = (index_x >> merged[0]) * 2 + side
            else:
                child_second = (index_y >> merged[1]) * 2 + side
            width_first = float(N // 8 * 2 ** before[0])
            width_second = float(N // 16 * 2 ** before[1])
            quads[0].append((child_first.astype(F32) * width_first, width_first))
            quads[1].append((child_second.astype(F32) * width_second, width_second))
            quads[2].append((old[0] + 2.0 * old[1], 0.0))
            quads[3].append((new[0] + 2.0 * new[1], 0.0))
            quads[4].append(((new[0] - old[0]) * (1.0 / 2048.0), (new[1] - old[1]) * (1.0 / 1024.0)))

    def lanes(values):
        out = jnp.zeros((1, 128), F32) + values[0]
        for k in range(1, 4):
            out = jnp.where(which == k, values[k], out)
        return out

    (first_at, first_width), (second_at, second_width), (old_at, _), (new_at, _), (move_first, move_second) = [
        (lanes([q[0] for q in quad]), lanes([q[1] for q in quad])) for quad in quads
    ]
    first = first_at + first_width * z_first
    second = second_at + second_width * z_second
    moved = first * move_first + second * move_second
    phase = root_of(speeds(info_ref, klass, new_at), first, second) - root_of(speeds(info_ref, klass, old_at), first, second)
    values = exact(jnp.concatenate(turn(phase + moved), axis=0))
    for k in range(4):
        spread(values, gamma_refs[k], k)
    if pair == 0:
        mix_ref, speed_ref = rest[-2:]
        order = iota((TGT, 128), 0)
        klass = (order % 16) * 2 + order // 16
        _, wave = turn((klass.astype(F32) + 1.5) * (1.0 / 32.0))
        speed_first = (32.0 + info_ref[0].astype(F32) + info_ref[1].astype(F32) * wave) * (1.0 / 4096.0)
        speed_second = (32.0 + info_ref[2].astype(F32) + info_ref[3].astype(F32) * wave) * (1.0 / 4096.0)
        speed_ref[0] = speed_first
        speed_ref[1] = speed_second
        for number in range(4):
            mix_ref[number] = mix_of(number)


def tables(info, pair, after=()):
    shapes = [jax.ShapeDtypeStruct((2 * NODES, 512), F32)] * 4
    if pair == 0:
        shapes.append(jax.ShapeDtypeStruct((4, 128, 256), BF16))
        shapes.append(jax.ShapeDtypeStruct((2, TGT, 128), F32))
    return pl.pallas_call(
        functools.partial(tables_body, pair),
        out_shape=tuple(shapes),
        in_specs=[pl.BlockSpec(memory_space=pltpu.SMEM)] + anywhere(len(after)),
        out_specs=vmem(len(shapes)),
        name="tables_%d" % pair,
        compiler_params=SMALL,
        cost_estimate=cost(0.8),
    )(info, *after)


def last_body(info_ref, *rest):
    last_ref, order_ref = rest[-2:]
    index_x = lax.axis_index("bx")
    index_y = lax.axis_index("by")
    z_first, z_second = node_columns((NODES, 128))
    width_first = float(N // 8 * 4)
    width_second = float(N // 16 * 4)
    first = (index_x >> 2).astype(F32) * width_first + width_first * z_first
    second = (index_y >> 2).astype(F32) * width_second + width_second * z_second
    new = [place(index_x, 2), place(index_y, 2)]
    lane = iota((1, 128), 1)
    v = lane % 16
    for tile in range(4):
        u = tile * 8 + lane // 16
        klass = ((u + 2 * v) % TGT).astype(F32)
        root = root_of(speeds(info_ref, klass, new[0] + 2.0 * new[1]), first, second)
        root = root - jnp.floor(root)
        at_first = first * ((u.astype(F32) + new[0]) * (1.0 / 2048.0))
        at_first = at_first - jnp.floor(at_first) + root
        for half in range(2):
            at_second = second * ((v.astype(F32) + (16.0 * half + new[1])) * (1.0 / 1024.0))
            cosine, sine = turn(at_first + at_second)
            wide = slice(tile * 256 + half * 128, tile * 256 + half * 128 + 128)
            last_ref[:NODES, wide] = cosine
            last_ref[NODES:, wide] = sine
    source = iota((256, 256), 0)
    target = iota((256, 256), 1)
    wanted = ((target // 16) % 2) * 128 + (target // 32) * 16 + target % 16
    order_ref[...] = jnp.where(source == wanted, 1.0, 0.0).astype(BF16)


def last_tables(info, after):
    return pl.pallas_call(
        last_body,
        out_shape=(jax.ShapeDtypeStruct((2 * NODES, TARGETS), F32), jax.ShapeDtypeStruct((256, 256), BF16)),
        in_specs=[pl.BlockSpec(memory_space=pltpu.SMEM)] + anywhere(len(after)),
        out_specs=vmem(2),
        name="last",
        compiler_params=SMALL,
        cost_estimate=cost(0.8),
    )(info, *after)


def combined(start, group, left, own_ref, other_ref, gamma_refs):
    gcols = slice((start + group) * 128, (start + group) * 128 + 128)
    sides = [[], []]
    for half in range(2):
        cols = slice(group * 256 + half * 128, group * 256 + half * 128 + 128)
        reals, imags = [], []
        for gamma_ref, ref in zip(gamma_refs, (own_ref, other_ref)):
            gr = gamma_ref[:NODES, gcols]
            gi = gamma_ref[NODES:, gcols]
            xr = ref[:NODES, cols]
            xi = ref[NODES:, cols]
            reals.append(split(gr * xr - gi * xi))
            imags.append(split(gr * xi + gi * xr))
        for side, parts in zip(sides, (reals, imags)):
            side.append(jnp.concatenate([parts[0][0], parts[1][0], parts[0][1], parts[1][1]], axis=0))
    out = []
    for side in sides:
        both = jnp.dot(left, jnp.concatenate(side, axis=1), preferred_element_type=F32)
        out.append(both[:NODES] + both[NODES:])
    return out


def merge_body(number, chunk, own_ref, other_ref, gamma_own_ref, gamma_other_ref, mix_ref, *rest):
    start, groups = chunk
    out_ref = rest[-1]
    left = mix_ref[number]
    for group in range(groups):
        real, imag = combined(start, group, left, own_ref, other_ref, (gamma_own_ref, gamma_other_ref))
        cols = slice(group * 256, group * 256 + 256)
        out_ref[:NODES, cols] = real
        out_ref[NODES:, cols] = imag


def merge(number, chunk, own, other, gammas, mix, after=()):
    return pl.pallas_call(
        functools.partial(merge_body, number, chunk),
        out_shape=jax.ShapeDtypeStruct((2 * NODES, 256 * chunk[1]), F32),
        in_specs=vmem(5) + anywhere(len(after)),
        out_specs=vmem(1)[0],
        name="merge_%d_%d" % (number, chunk[0]),
        compiler_params=SMALL,
        cost_estimate=cost(0.2 + 0.2 * chunk[1]),
    )(own, other, *gammas, mix, *after)


def finish_body(chunk, own_ref, other_ref, gamma_own_ref, gamma_other_ref, mix_ref, last_ref, order_ref, *rest):
    start, groups = chunk
    out_ref, wide_ref, sem = rest[-3:]
    left = mix_ref[3]
    for group in range(groups):
        real, imag = combined(start, group, left, own_ref, other_ref, (gamma_own_ref, gamma_other_ref))
        tile = start + group
        cols = slice(tile * 256, tile * 256 + 256)
        cosine = last_ref[:NODES, cols]
        sine = last_ref[NODES:, cols]
        value = jnp.concatenate([cosine * real + sine * imag, cosine * imag - sine * real], axis=0)
        moved = jnp.dot(exact(value), order_ref[...], preferred_element_type=F32)
        moved = moved[:128] + moved[128:256] + moved[256:]
        wide_ref[0, :, group * 256 : group * 256 + 256] = moved[:NODES]
        wide_ref[1, :, group * 256 : group * 256 + 256] = moved[NODES:]
    copy = pltpu.make_async_copy(wide_ref, out_ref.at[:, :, start * 256 : (start + groups) * 256], sem)
    copy.start()
    copy.wait()


def finish(chunk, own, other, gammas, mix, lasts, sofar):
    args = [own, other, *gammas, mix, *lasts]
    specs = vmem(7)
    aliases = {}
    if sofar is not None:
        aliases = {len(args): 0}
        args.append(sofar)
        specs = specs + anywhere(1)
    return pl.pallas_call(
        functools.partial(finish_body, chunk),
        out_shape=jax.ShapeDtypeStruct((2, NODES, TARGETS), F32),
        in_specs=specs,
        out_specs=anywhere(1)[0],
        scratch_shapes=[pltpu.VMEM((2, NODES, 256 * chunk[1]), F32), pltpu.SemaphoreType.DMA],
        input_output_aliases=aliases,
        name="finish_%d" % chunk[0],
        compiler_params=SMALL,
        cost_estimate=cost(0.7 + 0.3 * chunk[1]),
    )(*args)


def swap(value, along, level):
    axis = "bx" if along == 1 else "by"
    return lax.ppermute(value, axis, [(i, i ^ 1 << level) for i in range(lax.axis_size(axis))])


def on_device(point_box, point_offset, point_value, coef):
    owners = lax.axis_size("bx") * lax.axis_size("by")
    info = coef
    sent = pack(point_box.reshape(-1, 128), point_offset, point_value)
    arrived = lax.all_to_all(sent.reshape(owners, 1, -1), ("bx", "by"), split_axis=0, concat_axis=0, tiled=True)
    *gammas, mix, speed = tables(info, 0)
    prepared = prepare(arrived.reshape(owners, -1), speed)

    def exchange(number, c, x):
        return swap(x, *LEVELS[number])

    def join(number, c, x, y, after=()):
        return merge(number, c, x, y, gammas[2 * number : 2 * number + 2], mix, after)

    c0, c1, c2, c3 = CHUNKS
    leaf0 = leaf(c0, prepared, ())
    leaf1 = leaf(c1, prepared, (leaf0,))
    one0 = join(0, c0, leaf0, exchange(0, c0, leaf0))
    leaf2 = leaf(c2, prepared, (one0,))
    one1 = join(0, c1, leaf1, exchange(0, c1, leaf1))
    got0 = exchange(1, c0, one0)
    leaf3 = leaf(c3, prepared, (one1, got0))
    one2 = join(0, c2, leaf2, exchange(0, c2, leaf2))
    got1 = exchange(1, c1, one1)
    gammas += tables(info, 1, (leaf3, got1))
    one3 = join(0, c3, leaf3, exchange(0, c3, leaf3), (gammas[4],))
    ones = [one0, one1, one2, one3]
    lasts = last_tables(info, (one0,))
    swapped = [got0, got1, exchange(1, c2, one2), exchange(1, c3, one3)]

    late = [join(1, c, x, y) for c, x, y in zip(CHUNKS, ones, swapped)]
    holding = [join(2, c, x, exchange(2, c, x)) for c, x in zip(CHUNKS, late)]
    out = None
    for c, x in zip(CHUNKS, holding):
        out = finish(c, x, swap(x, *LEVELS[3]), gammas[6:], mix, lasts, out)
    return out


def solution(mesh):
    in_specs = (P(("bx", "by"), None), P(None, ("bx", "by")), P(None, ("bx", "by")), P())
    out_specs = P(None, None, ("bx", "by"))
    return jax.shard_map(on_device, mesh=mesh, in_specs=in_specs, out_specs=out_specs, check_vma=False)
```

```python
import functools
import math

import jax
import jax.numpy as jnp
import numpy as np
from jax import lax
from jax.experimental import pallas as pl
from jax.experimental.pallas import tpu as pltpu
from jax.sharding import PartitionSpec as P

N = 16384
ORDER = 8
TGT = 32
CAP = 32
CHUNKS = ((0, 1), (1, 1), (2, 1), (3, 1))
STEP = 8
NODES = ORDER * ORDER
TARGETS = TGT * TGT
F32 = jnp.float32
BF16 = jnp.bfloat16

SIN_C = (3.1415925798055824, -5.167706866167939, 2.550031193519312, -0.5980441939121666, 0.07721838615746283)
COS_C = (0.9999999532476086, -4.934792830619651, 4.058411352862725, -1.3318765680816773, 0.21968961109948903)


def node_table():
    counting = np.arange(ORDER) * 1.0
    return 0.5 - 0.5 * np.cos(np.pi * (2.0 * counting + 1.0) / (2.0 * ORDER))


def horner(coefs, x):
    total = coefs[-1]
    for c in coefs[-2::-1]:
        total = total * x + c
    return total


def turn(phase):
    r = phase - jnp.floor(phase + 0.5)
    x = r * r
    sine = horner(SIN_C, x) * r
    cosine = horner(COS_C, x)
    twice = sine + sine
    return 1.0 - twice * sine, twice * cosine


def split(x):
    high = x.astype(BF16)
    return high, (x - high.astype(F32)).astype(BF16)


def cost(micros):
    return pl.CostEstimate(flops=0, bytes_accessed=int(micros * 3.7e6), transcendentals=0)


def vmem(count):
    return [pl.BlockSpec(memory_space=pltpu.VMEM)] * count


def anywhere(count):
    return [pl.BlockSpec(memory_space=pl.ANY)] * count


SMALL = pltpu.CompilerParams(vmem_limit_bytes=12 << 20)


def iota(shape, axis):
    return lax.broadcasted_iota(jnp.int32, shape, axis)


def nt(a, b):
    return lax.dot_general(a, b, (((1,), (1,)), ((), ())), preferred_element_type=F32)


def pack_body(box_ref, off_ref, val_ref, out_ref):
    blocks = box_ref.shape[0]
    row = iota((128, 128), 0)
    row2 = iota((128, 256), 0)
    col2 = iota((128, 256), 1)
    prefix = jnp.where((row2 < col2) | (col2 >= 128), 1.0, 0.0).astype(BF16)
    same = [row == box_ref[b : b + 1, :] for b in range(blocks)]
    ones = [jnp.where(m, 1.0, 0.0).astype(BF16) for m in same]
    counts = jnp.dot(jnp.concatenate(ones, axis=0), prefix, preferred_element_type=F32)
    slots = iota((CAP, 128), 0).astype(F32)
    carry = jnp.zeros((128, 128), F32)
    wide = []
    for b in range(blocks):
        part = counts[b * 128 : (b + 1) * 128]
        rank = jnp.sum(jnp.where(same[b], part[:, :128] + carry, 0.0), axis=0, keepdims=True)
        carry = carry + part[:, 128:]
        hit = slots == rank
        cols = slice(b * 128, (b + 1) * 128)
        values = [off_ref[0:1, cols].astype(F32), off_ref[1:2, cols].astype(F32), val_ref[0:1, cols], val_ref[1:2, cols]]
        pieces = [[], [], []]
        for v in values:
            rest = v
            for piece in pieces:
                top = rest.astype(BF16).astype(F32)
                rest = rest - top
                piece.append(jnp.where(hit, top, 0.0).astype(BF16))
        wide.append(jnp.concatenate([x for piece in pieces for x in piece], axis=0))
    total = nt(jnp.concatenate(ones, axis=1), jnp.concatenate(wide, axis=1))
    out_ref[...] = total[:, :128] + total[:, 128:256] + total[:, 256:]


def pack(box, offsets, values):
    return pl.pallas_call(
        pack_body,
        out_shape=jax.ShapeDtypeStruct((128, 4 * CAP), F32),
        in_specs=[pl.BlockSpec(memory_space=pltpu.VMEM)] * 3,
        out_specs=pl.BlockSpec(memory_space=pltpu.VMEM),
        name="pack",
        cost_estimate=cost(2.0),
    )(box, offsets, values)


def basis_rows(tau):
    nodes = node_table()
    which = iota((ORDER, 128), 0)
    total = None
    for step in range(1, ORDER):
        other = jnp.zeros((ORDER, 128), F32)
        scale = jnp.zeros((ORDER, 128), F32)
        for t in range(ORDER):
            s = (t + step) % ORDER
            other = jnp.where(which == t, float(nodes[s]), other)
            scale = jnp.where(which == t, float(1.0 / (nodes[t] - nodes[s])), scale)
        factor = (tau - other) * scale
        total = factor if total is None else total * factor
    return total


def prepare_body(rx_ref, speed_ref, *rest):
    l_ref, q_ref, z_ref, xt_ref, trig_ref = rest[-5:]
    width_first, width_second = float(N // 8), float(N // 16)
    corner_first = lax.axis_index("bx").astype(F32) * width_first
    corner_second = lax.axis_index("by").astype(F32) * width_second
    xt_ref[...] = rx_ref[...].T

    order = iota((TGT, 128), 0)
    speed_first = speed_ref[0]
    speed_second = speed_ref[1]
    lin_first = (order // 16 * 2 + 1).astype(F32) * (1.0 / 4096.0)
    lin_second = (order % 16 * 4 + 34).astype(F32) * (1.0 / 4096.0)
    power = iota((16, 128), 0).astype(F32) * (1.0 / 1024.0)

    second_all = xt_ref[CAP : 2 * CAP, :] + corner_second
    cosine, sine = turn(second_all * (1.0 / 128.0))
    trig_ref[0] = cosine
    trig_ref[1] = sine
    trig_ref[2] = 1.0 - 2.0 * sine * sine
    trig_ref[3] = 2.0 * cosine * sine

    for s in range(CAP):
        off_first = xt_ref[s : s + 1, :]
        off_second = xt_ref[CAP + s : CAP + s + 1, :]
        real_in = xt_ref[2 * CAP + s : 2 * CAP + s + 1, :]
        imag_in = xt_ref[3 * CAP + s : 3 * CAP + s + 1, :]
        wrap_real = trig_ref[2, s : s + 1, :]
        wrap_imag = trig_ref[3, s : s + 1, :]
        first = off_first + corner_first
        second = off_second + corner_second
        a = speed_first * first
        b = speed_second * second
        root = jnp.sqrt(1.0 + a * a + b * b)
        root = root - jnp.floor(root)
        lin = lin_first * first + lin_second * second
        cosine, sine = turn(root + (lin - jnp.floor(lin)))
        more_cosine = cosine * wrap_real - sine * wrap_imag
        more_sine = cosine * wrap_imag + sine * wrap_real
        for eps in range(2):
            rows = slice(eps * 16, eps * 16 + 16)
            q_ref[s, 2 * eps, :16] = cosine[rows]
            q_ref[s, 2 * eps, 16:] = more_cosine[rows]
            q_ref[s, 2 * eps + 1, :16] = sine[rows]
            q_ref[s, 2 * eps + 1, 16:] = more_sine[rows]
        cosine, sine = turn(power * (first - second))
        z_ref[s, 0] = cosine * real_in - sine * imag_in
        z_ref[s, 1] = cosine * imag_in + sine * real_in
        cols = slice(s * 128, s * 128 + 128)
        first_rows = basis_rows(off_first * (1.0 / width_first))
        second_rows = basis_rows(off_second * (1.0 / width_second))
        for part in range(2):
            scaled = second_rows * trig_ref[part, s : s + 1, :]
            for t in range(0, ORDER, 2):
                pair = jnp.concatenate([first_rows[t : t + 1] * scaled, first_rows[t + 1 : t + 2] * scaled], axis=0)
                high, low = split(pair)
                base = part * NODES + t * ORDER
                l_ref[base : base + 16, cols] = high
                l_ref[128 + base : 128 + base + 16, cols] = low


def prepare(arrived, speed):
    return pl.pallas_call(
        prepare_body,
        out_shape=(
            jax.ShapeDtypeStruct((256, CAP * 128), BF16),
            jax.ShapeDtypeStruct((CAP, 4, TGT, 128), F32),
            jax.ShapeDtypeStruct((CAP, 2, 16, 128), F32),
        ),
        in_specs=vmem(2),
        out_specs=vmem(3),
        scratch_shapes=[pltpu.VMEM((128, 128), F32), pltpu.VMEM((4, CAP, 128), F32)],
        name="prepare",
        compiler_params=SMALL,
        cost_estimate=cost(2.0),
    )(arrived, speed)


def leaf_body(chunk, l_ref, q_ref, z_ref, *rest):
    start, groups = chunk
    out_ref, ra_ref, rb_ref, acc_ref = rest[-4:]
    half = STEP * 128

    def build(step, r_ref):
        for j in range(STEP):
            s = step * STEP + j
            cols = slice(j * 128, j * 128 + 128)
            low_cols = slice(half + j * 128, half + j * 128 + 128)
            for local in range(4 * groups):
                up = start * 4 + local
                zr = z_ref[s, 0, up : up + 1, :]
                zi = z_ref[s, 1, up : up + 1, :]
                for eps in range(2):
                    qr = q_ref[s, 2 * eps, up : up + 16, :]
                    qi = q_ref[s, 2 * eps + 1, up : up + 16, :]
                    for part, value in enumerate((qr * zr - qi * zi, qr * zi + qi * zr)):
                        high, low = split(value)
                        base = (local // 4) * 256 + part * 128 + (2 * (local % 4) + eps) * 16
                        r_ref[base : base + 16, cols] = high
                        r_ref[base : base + 16, low_cols] = low

    steps = CAP // STEP
    build(0, ra_ref)
    for step in range(steps):
        now, later = (ra_ref, rb_ref) if step % 2 == 0 else (rb_ref, ra_ref)
        if step + 1 < steps:
            build(step + 1, later)
        right = l_ref[:, step * half : step * half + half]
        product = nt(now[...], jnp.concatenate([right, right], axis=1))
        if step == 0:
            acc_ref[...] = product
        else:
            acc_ref[...] += product

    for g in range(groups):
        blocks = []
        for part in range(2):
            rows = slice(g * 256 + part * 128, g * 256 + part * 128 + 128)
            blocks.append((acc_ref[rows, :128] + acc_ref[rows, 128:]).T)
        (cr, sr), (ci, si) = [(x[:NODES], x[NODES:]) for x in blocks]
        low_cols = slice(g * 256, g * 256 + 128)
        high_cols = slice(g * 256 + 128, g * 256 + 256)
        out_ref[:NODES, low_cols] = cr + si
        out_ref[NODES:, low_cols] = ci - sr
        out_ref[:NODES, high_cols] = cr - si
        out_ref[NODES:, high_cols] = ci + sr


def leaf(chunk, prepared, after):
    lanes = 256 * chunk[1]
    return pl.pallas_call(
        functools.partial(leaf_body, chunk),
        out_shape=jax.ShapeDtypeStruct((2 * NODES, lanes), F32),
        in_specs=vmem(3) + anywhere(len(after)),
        out_specs=vmem(1)[0],
        scratch_shapes=[
            pltpu.VMEM((lanes, STEP * 256), BF16),
            pltpu.VMEM((lanes, STEP * 256), BF16),
            pltpu.VMEM((lanes, 256), F32),
        ],
        name="leaf_%d" % chunk[0],
        compiler_params=SMALL,
        cost_estimate=cost(2.3 * chunk[1]),
    )(*prepared, *after)


def place(index, merged):
    code = jnp.int32(0)
    for bit in range(merged):
        code = code + ((index >> bit) & 1) * 2 ** (merged - 1 - bit)
    return (code.astype(F32) + 0.5) * (1.0 / 2.0**merged)


def node_columns(shape):
    nodes = node_table()
    row = iota(shape, 0)
    first = jnp.zeros(shape, F32)
    second = jnp.zeros(shape, F32)
    for t in range(ORDER):
        first = jnp.where(row // ORDER == t, float(nodes[t]), first)
        second = jnp.where(row % ORDER == t, float(nodes[t]), second)
    return first, second


def speeds(info_ref, klass, at):
    _, wave = turn((klass + at) * (1.0 / 32.0))
    one = (32.0 + info_ref[0].astype(F32) + info_ref[1].astype(F32) * wave) * (1.0 / 4096.0)
    two = (32.0 + info_ref[2].astype(F32) + info_ref[3].astype(F32) * wave) * (1.0 / 4096.0)
    return one, two


def root_of(speed, first, second):
    a = speed[0] * first
    b = speed[1] * second
    return jnp.sqrt(1.0 + a * a + b * b)


LEVELS = ((1, 0), (2, 0), (1, 1), (2, 1))


def exact(x):
    high = x.astype(BF16)
    mid, low = split(x - high.astype(F32))
    return jnp.concatenate([high, mid, low], axis=0)


def spread(values, out_ref, columns):
    klass = iota((TGT * 4, 512), 0)
    lane = iota((TGT * 4, 512), 1)
    pick = jnp.where(klass == (lane // 16 + 2 * (lane % 16)) % TGT + TGT * columns, 1.0, 0.0).astype(BF16)
    moved = jnp.dot(values, pick, preferred_element_type=F32)
    rows = 2 * NODES
    out_ref[...] = moved[:rows] + moved[rows : 2 * rows] + moved[2 * rows :]


def mix_of(number):
    along, level = LEVELS[number]
    bit = (lax.axis_index("bx" if along == 1 else "by") >> level) & 1
    nodes = node_table()
    lane = iota((1, 128), 1)
    who = lane // NODES
    first = lane // ORDER % ORDER
    second = lane % ORDER
    source = first if along == 1 else second
    at = jnp.zeros((1, 128), F32)
    for t in range(ORDER):
        at = jnp.where(source == t, float(nodes[t]), at)
    side = jnp.where(who == 0, bit, 1 - bit).astype(F32)
    rows = basis_rows((at + side) * 0.5)
    row = iota((ORDER, 128), 0)
    full = []
    for t in range(ORDER):
        if along == 1:
            full.append(jnp.where(row == second, rows[t : t + 1], 0.0))
        else:
            full.append(jnp.where(first == t, rows, 0.0))
    high, low = split(jnp.concatenate(full, axis=0))
    top = jnp.concatenate([high, high], axis=1)
    bottom = jnp.concatenate([low, jnp.zeros_like(low)], axis=1)
    return jnp.concatenate([top, bottom], axis=0)


def tables_body(pair, info_ref, *rest):
    gamma_refs = [rest[-6 + k] for k in range(4)] if pair == 0 else [rest[-4 + k] for k in range(4)]
    index_x = lax.axis_index("bx")
    index_y = lax.axis_index("by")
    z_first, z_second = node_columns((NODES, 128))
    lane = iota((1, 128), 1)
    klass = (lane % TGT).astype(F32)
    which = lane // TGT
    quads = [[], [], [], [], []]
    merged = [0, 0]
    for number, (along, level) in enumerate(LEVELS):
        before = list(merged)
        merged[along - 1] += 1
        if number // 2 != pair:
            continue
        old = [place(index_x, before[0]), place(index_y, before[1])]
        new = [place(index_x, merged[0]), place(index_y, merged[1])]
        index_d = index_x if along == 1 else index_y
        bit = (index_d >> level) & 1
        for who in range(2):
            side = bit if who == 0 else 1 - bit
            child_first = index_x >> before[0]
            child_second = index_y >> before[1]
            if along == 1:
                child_first = (index_x >> merged[0]) * 2 + side
            else:
                child_second = (index_y >> merged[1]) * 2 + side
            width_first = float(N // 8 * 2 ** before[0])
            width_second = float(N // 16 * 2 ** before[1])
            quads[0].append((child_first.astype(F32) * width_first, width_first))
            quads[1].append((child_second.astype(F32) * width_second, width_second))
            quads[2].append((old[0] + 2.0 * old[1], 0.0))
            quads[3].append((new[0] + 2.0 * new[1], 0.0))
            quads[4].append(((new[0] - old[0]) * (1.0 / 2048.0), (new[1] - old[1]) * (1.0 / 1024.0)))

    def lanes(values):
        out = jnp.zeros((1, 128), F32) + values[0]
        for k in range(1, 4):
            out = jnp.where(which == k, values[k], out)
        return out

    (first_at, first_width), (second_at, second_width), (old_at, _), (new_at, _), (move_first, move_second) = [
        (lanes([q[0] for q in quad]), lanes([q[1] for q in quad])) for quad in quads
    ]
    first = first_at + first_width * z_first
    second = second_at + second_width * z_second
    moved = first * move_first + second * move_second
    phase = root_of(speeds(info_ref, klass, new_at), first, second) - root_of(speeds(info_ref, klass, old_at), first, second)
    values = exact(jnp.concatenate(turn(phase + moved), axis=0))
    for k in range(4):
        spread(values, gamma_refs[k], k)
    if pair == 0:
        mix_ref, speed_ref = rest[-2:]
        order = iota((TGT, 128), 0)
        klass = (order % 16) * 2 + order // 16
        _, wave = turn((klass.astype(F32) + 1.5) * (1.0 / 32.0))
        speed_first = (32.0 + info_ref[0].astype(F32) + info_ref[1].astype(F32) * wave) * (1.0 / 4096.0)
        speed_second = (32.0 + info_ref[2].astype(F32) + info_ref[3].astype(F32) * wave) * (1.0 / 4096.0)
        speed_ref[0] = speed_first
        speed_ref[1] = speed_second
        for number in range(4):
            mix_ref[number] = mix_of(number)


def tables(info, pair, after=()):
    shapes = [jax.ShapeDtypeStruct((2 * NODES, 512), F32)] * 4
    if pair == 0:
        shapes.append(jax.ShapeDtypeStruct((4, 128, 256), BF16))
        shapes.append(jax.ShapeDtypeStruct((2, TGT, 128), F32))
    return pl.pallas_call(
        functools.partial(tables_body, pair),
        out_shape=tuple(shapes),
        in_specs=[pl.BlockSpec(memory_space=pltpu.SMEM)] + anywhere(len(after)),
        out_specs=vmem(len(shapes)),
        name="tables_%d" % pair,
        compiler_params=SMALL,
        cost_estimate=cost(0.8),
    )(info, *after)


def last_body(info_ref, *rest):
    last_ref, order_ref = rest[-2:]
    index_x = lax.axis_index("bx")
    index_y = lax.axis_index("by")
    z_first, z_second = node_columns((NODES, 128))
    width_first = float(N // 8 * 4)
    width_second = float(N // 16 * 4)
    first = (index_x >> 2).astype(F32) * width_first + width_first * z_first
    second = (index_y >> 2).astype(F32) * width_second + width_second * z_second
    new = [place(index_x, 2), place(index_y, 2)]
    lane = iota((1, 128), 1)
    v = lane % 16
    for tile in range(4):
        u = tile * 8 + lane // 16
        klass = ((u + 2 * v) % TGT).astype(F32)
        root = root_of(speeds(info_ref, klass, new[0] + 2.0 * new[1]), first, second)
        root = root - jnp.floor(root)
        at_first = first * ((u.astype(F32) + new[0]) * (1.0 / 2048.0))
        at_first = at_first - jnp.floor(at_first) + root
        for half in range(2):
            at_second = second * ((v.astype(F32) + (16.0 * half + new[1])) * (1.0 / 1024.0))
            cosine, sine = turn(at_first + at_second)
            wide = slice(tile * 256 + half * 128, tile * 256 + half * 128 + 128)
            last_ref[:NODES, wide] = cosine
            last_ref[NODES:, wide] = sine
    source = iota((256, 256), 0)
    target = iota((256, 256), 1)
    wanted = ((target // 16) % 2) * 128 + (target // 32) * 16 + target % 16
    order_ref[...] = jnp.where(source == wanted, 1.0, 0.0).astype(BF16)


def last_tables(info, after):
    return pl.pallas_call(
        last_body,
        out_shape=(jax.ShapeDtypeStruct((2 * NODES, TARGETS), F32), jax.ShapeDtypeStruct((256, 256), BF16)),
        in_specs=[pl.BlockSpec(memory_space=pltpu.SMEM)] + anywhere(len(after)),
        out_specs=vmem(2),
        name="last",
        compiler_params=SMALL,
        cost_estimate=cost(0.8),
    )(info, *after)


def combined(start, group, left, own_ref, other_ref, gamma_refs):
    gcols = slice((start + group) * 128, (start + group) * 128 + 128)
    sides = [[], []]
    for half in range(2):
        cols = slice(group * 256 + half * 128, group * 256 + half * 128 + 128)
        reals, imags = [], []
        for gamma_ref, ref in zip(gamma_refs, (own_ref, other_ref)):
            gr = gamma_ref[:NODES, gcols]
            gi = gamma_ref[NODES:, gcols]
            xr = ref[:NODES, cols]
            xi = ref[NODES:, cols]
            reals.append(split(gr * xr - gi * xi))
            imags.append(split(gr * xi + gi * xr))
        for side, parts in zip(sides, (reals, imags)):
            side.append(jnp.concatenate([parts[0][0], parts[1][0], parts[0][1], parts[1][1]], axis=0))
    out = []
    for side in sides:
        both = jnp.dot(left, jnp.concatenate(side, axis=1), preferred_element_type=F32)
        out.append(both[:NODES] + both[NODES:])
    return out


def merge_body(number, chunk, own_ref, other_ref, gamma_own_ref, gamma_other_ref, mix_ref, *rest):
    start, groups = chunk
    out_ref = rest[-1]
    left = mix_ref[number]
    for group in range(groups):
        real, imag = combined(start, group, left, own_ref, other_ref, (gamma_own_ref, gamma_other_ref))
        cols = slice(group * 256, group * 256 + 256)
        out_ref[:NODES, cols] = real
        out_ref[NODES:, cols] = imag


def merge(number, chunk, own, other, gammas, mix, after=()):
    return pl.pallas_call(
        functools.partial(merge_body, number, chunk),
        out_shape=jax.ShapeDtypeStruct((2 * NODES, 256 * chunk[1]), F32),
        in_specs=vmem(5) + anywhere(len(after)),
        out_specs=vmem(1)[0],
        name="merge_%d_%d" % (number, chunk[0]),
        compiler_params=SMALL,
        cost_estimate=cost(0.2 + 0.2 * chunk[1]),
    )(own, other, *gammas, mix, *after)


def finish_body(chunk, own_ref, other_ref, gamma_own_ref, gamma_other_ref, mix_ref, last_ref, order_ref, *rest):
    start, groups = chunk
    out_ref, wide_ref, sem = rest[-3:]
    left = mix_ref[3]
    for group in range(groups):
        real, imag = combined(start, group, left, own_ref, other_ref, (gamma_own_ref, gamma_other_ref))
        tile = start + group
        cols = slice(tile * 256, tile * 256 + 256)
        cosine = last_ref[:NODES, cols]
        sine = last_ref[NODES:, cols]
        value = jnp.concatenate([cosine * real + sine * imag, cosine * imag - sine * real], axis=0)
        moved = jnp.dot(exact(value), order_ref[...], preferred_element_type=F32)
        moved = moved[:128] + moved[128:256] + moved[256:]
        wide_ref[0, :, group * 256 : group * 256 + 256] = moved[:NODES]
        wide_ref[1, :, group * 256 : group * 256 + 256] = moved[NODES:]
    copy = pltpu.make_async_copy(wide_ref, out_ref.at[:, :, start * 256 : (start + groups) * 256], sem)
    copy.start()
    copy.wait()


def finish(chunk, own, other, gammas, mix, lasts, sofar):
    args = [own, other, *gammas, mix, *lasts]
    specs = vmem(7)
    aliases = {}
    if sofar is not None:
        aliases = {len(args): 0}
        args.append(sofar)
        specs = specs + anywhere(1)
    return pl.pallas_call(
        functools.partial(finish_body, chunk),
        out_shape=jax.ShapeDtypeStruct((2, NODES, TARGETS), F32),
        in_specs=specs,
        out_specs=anywhere(1)[0],
        scratch_shapes=[pltpu.VMEM((2, NODES, 256 * chunk[1]), F32), pltpu.SemaphoreType.DMA],
        input_output_aliases=aliases,
        name="finish_%d" % chunk[0],
        compiler_params=SMALL,
        cost_estimate=cost(0.7 + 0.3 * chunk[1]),
    )(*args)


def swap(value, along, level):
    axis = "bx" if along == 1 else "by"
    return lax.ppermute(value, axis, [(i, i ^ 1 << level) for i in range(lax.axis_size(axis))])


def on_device(point_box, point_offset, point_value, coef):
    owners = lax.axis_size("bx") * lax.axis_size("by")
    info = coef
    sent = pack(point_box.reshape(-1, 128), point_offset, point_value)
    arrived = lax.all_to_all(sent.reshape(owners, 1, -1), ("bx", "by"), split_axis=0, concat_axis=0, tiled=True)
    *gammas, mix, speed = tables(info, 0)
    prepared = prepare(arrived.reshape(owners, -1), speed)

    def exchange(number, c, x):
        return swap(x, *LEVELS[number])

    def join(number, c, x, y, after=()):
        return merge(number, c, x, y, gammas[2 * number : 2 * number + 2], mix, after)

    c0, c1, c2, c3 = CHUNKS
    leaf0 = leaf(c0, prepared, ())
    leaf1 = leaf(c1, prepared, (leaf0,))
    one0 = join(0, c0, leaf0, exchange(0, c0, leaf0))
    leaf2 = leaf(c2, prepared, (one0,))
    one1 = join(0, c1, leaf1, exchange(0, c1, leaf1))
    got0 = exchange(1, c0, one0)
    two0 = join(1, c0, one0, got0)
    leaf3 = leaf(c3, prepared, (one1, got0))
    one2 = join(0, c2, leaf2, exchange(0, c2, leaf2))
    one3 = join(0, c3, leaf3, exchange(0, c3, leaf3), (two0, one2))
    two1 = join(1, c1, one1, exchange(1, c1, one1))
    gammas += tables(info, 1, (one3, two1))
    y0 = exchange(2, c0, two0)
    y1 = exchange(2, c1, two1)
    three0 = join(2, c0, two0, y0)
    x0 = exchange(3, c0, three0)
    two2 = join(1, c2, one2, exchange(1, c2, one2), (three0,))
    three1 = join(2, c1, two1, y1)
    x1 = exchange(3, c1, three1)
    two3 = join(1, c3, one3, exchange(1, c3, one3), (three1,))
    three2 = join(2, c2, two2, exchange(2, c2, two2), (x0,))
    x2 = exchange(3, c2, three2)
    three3 = join(2, c3, two3, exchange(2, c3, two3), (x0, x1))
    lasts = last_tables(info, (one0,))
    out = None
    for c, x, y in zip(CHUNKS, (three0, three1, three2, three3), (x0, x1, x2, exchange(3, c3, three3))):
        out = finish(c, x, y, gammas[6:], mix, lasts, out)
    return out


def solution(mesh):
    in_specs = (P(("bx", "by"), None), P(None, ("bx", "by")), P(None, ("bx", "by")), P())
    out_specs = P(None, None, ("bx", "by"))
    return jax.shard_map(on_device, mesh=mesh, in_specs=in_specs, out_specs=out_specs, check_vma=False)
```

```python
import functools
import math

import jax
import jax.numpy as jnp
import numpy as np
from jax import lax
from jax.experimental import pallas as pl
from jax.experimental.pallas import tpu as pltpu
from jax.sharding import PartitionSpec as P

N = 16384
ORDER = 8
TGT = 32
CAP = 32
CHUNKS = ((0, 1), (1, 1), (2, 1), (3, 1))
STEP = 1
NODES = ORDER * ORDER
TARGETS = TGT * TGT
F32 = jnp.float32
BF16 = jnp.bfloat16

SIN_C = (3.1415925798055824, -5.167706866167939, 2.550031193519312, -0.5980441939121666, 0.07721838615746283)
COS_C = (0.9999999532476086, -4.934792830619651, 4.058411352862725, -1.3318765680816773, 0.21968961109948903)


def node_table():
    counting = np.arange(ORDER) * 1.0
    return 0.5 - 0.5 * np.cos(np.pi * (2.0 * counting + 1.0) / (2.0 * ORDER))


def horner(coefs, x):
    total = coefs[-1]
    for c in coefs[-2::-1]:
        total = total * x + c
    return total


def turn(phase):
    r = phase - jnp.floor(phase + 0.5)
    x = r * r
    sine = horner(SIN_C, x) * r
    cosine = horner(COS_C, x)
    twice = sine + sine
    return 1.0 - twice * sine, twice * cosine


def split(x):
    high = x.astype(BF16)
    return high, (x - high.astype(F32)).astype(BF16)


def cost(micros):
    return pl.CostEstimate(flops=0, bytes_accessed=int(micros * 3.7e6), transcendentals=0)


def vmem(count):
    return [pl.BlockSpec(memory_space=pltpu.VMEM)] * count


def anywhere(count):
    return [pl.BlockSpec(memory_space=pl.ANY)] * count


SMALL = pltpu.CompilerParams(vmem_limit_bytes=12 << 20)


def iota(shape, axis):
    return lax.broadcasted_iota(jnp.int32, shape, axis)


def nt(a, b):
    return lax.dot_general(a, b, (((1,), (1,)), ((), ())), preferred_element_type=F32)


def pack_body(box_ref, off_ref, val_ref, out_ref):
    blocks = box_ref.shape[0]
    row = iota((128, 128), 0)
    row2 = iota((128, 256), 0)
    col2 = iota((128, 256), 1)
    prefix = jnp.where((row2 < col2) | (col2 >= 128), 1.0, 0.0).astype(BF16)
    same = [row == box_ref[b : b + 1, :] for b in range(blocks)]
    ones = [jnp.where(m, 1.0, 0.0).astype(BF16) for m in same]
    counts = jnp.dot(jnp.concatenate(ones, axis=0), prefix, preferred_element_type=F32)
    slots = iota((CAP, 128), 0).astype(F32)
    carry = jnp.zeros((128, 128), F32)
    wide = []
    for b in range(blocks):
        part = counts[b * 128 : (b + 1) * 128]
        rank = jnp.sum(jnp.where(same[b], part[:, :128] + carry, 0.0), axis=0, keepdims=True)
        carry = carry + part[:, 128:]
        hit = slots == rank
        cols = slice(b * 128, (b + 1) * 128)
        values = [off_ref[0:1, cols].astype(F32), off_ref[1:2, cols].astype(F32), val_ref[0:1, cols], val_ref[1:2, cols]]
        pieces = [[], [], []]
        for v in values:
            rest = v
            for piece in pieces:
                top = rest.astype(BF16).astype(F32)
                rest = rest - top
                piece.append(jnp.where(hit, top, 0.0).astype(BF16))
        wide.append(jnp.concatenate([x for piece in pieces for x in piece], axis=0))
    total = nt(jnp.concatenate(ones, axis=1), jnp.concatenate(wide, axis=1))
    out_ref[...] = total[:, :128] + total[:, 128:256] + total[:, 256:]


def pack(box, offsets, values):
    return pl.pallas_call(
        pack_body,
        out_shape=jax.ShapeDtypeStruct((128, 4 * CAP), F32),
        in_specs=[pl.BlockSpec(memory_space=pltpu.VMEM)] * 3,
        out_specs=pl.BlockSpec(memory_space=pltpu.VMEM),
        name="pack",
        cost_estimate=cost(2.0),
    )(box, offsets, values)


def basis_rows(tau):
    nodes = node_table()
    which = iota((ORDER, 128), 0)
    total = None
    for step in range(1, ORDER):
        other = jnp.zeros((ORDER, 128), F32)
        scale = jnp.zeros((ORDER, 128), F32)
        for t in range(ORDER):
            s = (t + step) % ORDER
            other = jnp.where(which == t, float(nodes[s]), other)
            scale = jnp.where(which == t, float(1.0 / (nodes[t] - nodes[s])), scale)
        factor = (tau - other) * scale
        total = factor if total is None else total * factor
    return total


def prepare_body(rx_ref, speed_ref, *rest):
    l_ref, q_ref, z_ref, xt_ref, trig_ref = rest[-5:]
    width_first, width_second = float(N // 8), float(N // 16)
    corner_first = lax.axis_index("bx").astype(F32) * width_first
    corner_second = lax.axis_index("by").astype(F32) * width_second
    xt_ref[...] = rx_ref[...].T

    order = iota((TGT, 128), 0)
    speed_first = speed_ref[0]
    speed_second = speed_ref[1]
    lin_first = (order // 16 * 2 + 1).astype(F32) * (1.0 / 4096.0)
    lin_second = (order % 16 * 4 + 34).astype(F32) * (1.0 / 4096.0)
    power = iota((16, 128), 0).astype(F32) * (1.0 / 1024.0)

    second_all = xt_ref[CAP : 2 * CAP, :] + corner_second
    cosine, sine = turn(second_all * (1.0 / 128.0))
    trig_ref[0] = cosine
    trig_ref[1] = sine
    trig_ref[2] = 1.0 - 2.0 * sine * sine
    trig_ref[3] = 2.0 * cosine * sine

    for s in range(CAP):
        off_first = xt_ref[s : s + 1, :]
        off_second = xt_ref[CAP + s : CAP + s + 1, :]
        real_in = xt_ref[2 * CAP + s : 2 * CAP + s + 1, :]
        imag_in = xt_ref[3 * CAP + s : 3 * CAP + s + 1, :]
        wrap_real = trig_ref[2, s : s + 1, :]
        wrap_imag = trig_ref[3, s : s + 1, :]
        first = off_first + corner_first
        second = off_second + corner_second
        a = speed_first * first
        b = speed_second * second
        root = jnp.sqrt(1.0 + a * a + b * b)
        root = root - jnp.floor(root)
        lin = lin_first * first + lin_second * second
        cosine, sine = turn(root + (lin - jnp.floor(lin)))
        more_cosine = cosine * wrap_real - sine * wrap_imag
        more_sine = cosine * wrap_imag + sine * wrap_real
        for eps in range(2):
            rows = slice(eps * 16, eps * 16 + 16)
            q_ref[s, 2 * eps, :16] = cosine[rows]
            q_ref[s, 2 * eps, 16:] = more_cosine[rows]
            q_ref[s, 2 * eps + 1, :16] = sine[rows]
            q_ref[s, 2 * eps + 1, 16:] = more_sine[rows]
        cosine, sine = turn(power * (first - second))
        z_ref[s, 0] = cosine * real_in - sine * imag_in
        z_ref[s, 1] = cosine * imag_in + sine * real_in
        cols = slice(s * 128, s * 128 + 128)
        first_rows = basis_rows(off_first * (1.0 / width_first))
        second_rows = basis_rows(off_second * (1.0 / width_second))
        for part in range(2):
            scaled = second_rows * trig_ref[part, s : s + 1, :]
            for t in range(0, ORDER, 2):
                pair = jnp.concatenate([first_rows[t : t + 1] * scaled, first_rows[t + 1 : t + 2] * scaled], axis=0)
                high, low = split(pair)
                base = part * NODES + t * ORDER
                l_ref[base : base + 16, cols] = high
                l_ref[128 + base : 128 + base + 16, cols] = low


def prepare(arrived, speed):
    return pl.pallas_call(
        prepare_body,
        out_shape=(
            jax.ShapeDtypeStruct((256, CAP * 128), BF16),
            jax.ShapeDtypeStruct((CAP, 4, TGT, 128), F32),
            jax.ShapeDtypeStruct((CAP, 2, 16, 128), F32),
        ),
        in_specs=vmem(2),
        out_specs=vmem(3),
        scratch_shapes=[pltpu.VMEM((128, 128), F32), pltpu.VMEM((4, CAP, 128), F32)],
        name="prepare",
        compiler_params=SMALL,
        cost_estimate=cost(2.0),
    )(arrived, speed)


def leaf_body(chunk, l_ref, q_ref, z_ref, *rest):
    start, groups = chunk
    out_ref, ra_ref, rb_ref, acc_ref = rest[-4:]
    half = STEP * 128

    def build(step, r_ref):
        for j in range(STEP):
            s = step * STEP + j
            cols = slice(j * 128, j * 128 + 128)
            low_cols = slice(half + j * 128, half + j * 128 + 128)
            for local in range(4 * groups):
                up = start * 4 + local
                zr = z_ref[s, 0, up : up + 1, :]
                zi = z_ref[s, 1, up : up + 1, :]
                for eps in range(2):
                    qr = q_ref[s, 2 * eps, up : up + 16, :]
                    qi = q_ref[s, 2 * eps + 1, up : up + 16, :]
                    for part, value in enumerate((qr * zr - qi * zi, qr * zi + qi * zr)):
                        high, low = split(value)
                        base = (local // 4) * 256 + part * 128 + (2 * (local % 4) + eps) * 16
                        r_ref[base : base + 16, cols] = high
                        r_ref[base : base + 16, low_cols] = low

    steps = CAP // STEP
    build(0, ra_ref)
    for step in range(steps):
        now, later = (ra_ref, rb_ref) if step % 2 == 0 else (rb_ref, ra_ref)
        if step + 1 < steps:
            build(step + 1, later)
        right = l_ref[:, step * half : step * half + half]
        product = nt(now[...], jnp.concatenate([right, right], axis=1))
        if step == 0:
            acc_ref[...] = product
        else:
            acc_ref[...] += product

    for g in range(groups):
        blocks = []
        for part in range(2):
            rows = slice(g * 256 + part * 128, g * 256 + part * 128 + 128)
            blocks.append((acc_ref[rows, :128] + acc_ref[rows, 128:]).T)
        (cr, sr), (ci, si) = [(x[:NODES], x[NODES:]) for x in blocks]
        low_cols = slice(g * 256, g * 256 + 128)
        high_cols = slice(g * 256 + 128, g * 256 + 256)
        out_ref[:NODES, low_cols] = cr + si
        out_ref[NODES:, low_cols] = ci - sr
        out_ref[:NODES, high_cols] = cr - si
        out_ref[NODES:, high_cols] = ci + sr


def leaf(chunk, prepared, after):
    lanes = 256 * chunk[1]
    return pl.pallas_call(
        functools.partial(leaf_body, chunk),
        out_shape=jax.ShapeDtypeStruct((2 * NODES, lanes), F32),
        in_specs=vmem(3) + anywhere(len(after)),
        out_specs=vmem(1)[0],
        scratch_shapes=[
            pltpu.VMEM((lanes, STEP * 256), BF16),
            pltpu.VMEM((lanes, STEP * 256), BF16),
            pltpu.VMEM((lanes, 256), F32),
        ],
        name="leaf_%d" % chunk[0],
        compiler_params=SMALL,
        cost_estimate=cost(2.3 * chunk[1]),
    )(*prepared, *after)


def place(index, merged):
    code = jnp.int32(0)
    for bit in range(merged):
        code = code + ((index >> bit) & 1) * 2 ** (merged - 1 - bit)
    return (code.astype(F32) + 0.5) * (1.0 / 2.0**merged)


def node_columns(shape):
    nodes = node_table()
    row = iota(shape, 0)
    first = jnp.zeros(shape, F32)
    second = jnp.zeros(shape, F32)
    for t in range(ORDER):
        first = jnp.where(row // ORDER == t, float(nodes[t]), first)
        second = jnp.where(row % ORDER == t, float(nodes[t]), second)
    return first, second


def speeds(info_ref, klass, at):
    _, wave = turn((klass + at) * (1.0 / 32.0))
    one = (32.0 + info_ref[0].astype(F32) + info_ref[1].astype(F32) * wave) * (1.0 / 4096.0)
    two = (32.0 + info_ref[2].astype(F32) + info_ref[3].astype(F32) * wave) * (1.0 / 4096.0)
    return one, two


def root_of(speed, first, second):
    a = speed[0] * first
    b = speed[1] * second
    return jnp.sqrt(1.0 + a * a + b * b)


LEVELS = ((1, 0), (2, 0), (1, 1), (2, 1))


def exact(x):
    high = x.astype(BF16)
    mid, low = split(x - high.astype(F32))
    return jnp.concatenate([high, mid, low], axis=0)


def spread(values, out_ref, columns):
    klass = iota((TGT * 4, 512), 0)
    lane = iota((TGT * 4, 512), 1)
    pick = jnp.where(klass == (lane // 16 + 2 * (lane % 16)) % TGT + TGT * columns, 1.0, 0.0).astype(BF16)
    moved = jnp.dot(values, pick, preferred_element_type=F32)
    rows = 2 * NODES
    out_ref[...] = moved[:rows] + moved[rows : 2 * rows] + moved[2 * rows :]


def mix_of(number):
    along, level = LEVELS[number]
    bit = (lax.axis_index("bx" if along == 1 else "by") >> level) & 1
    nodes = node_table()
    lane = iota((1, 128), 1)
    who = lane // NODES
    first = lane // ORDER % ORDER
    second = lane % ORDER
    source = first if along == 1 else second
    at = jnp.zeros((1, 128), F32)
    for t in range(ORDER):
        at = jnp.where(source == t, float(nodes[t]), at)
    side = jnp.where(who == 0, bit, 1 - bit).astype(F32)
    rows = basis_rows((at + side) * 0.5)
    row = iota((ORDER, 128), 0)
    full = []
    for t in range(ORDER):
        if along == 1:
            full.append(jnp.where(row == second, rows[t : t + 1], 0.0))
        else:
            full.append(jnp.where(first == t, rows, 0.0))
    high, low = split(jnp.concatenate(full, axis=0))
    top = jnp.concatenate([high, high], axis=1)
    bottom = jnp.concatenate([low, jnp.zeros_like(low)], axis=1)
    return jnp.concatenate([top, bottom], axis=0)


def tables_body(pair, info_ref, *rest):
    gamma_refs = [rest[-6 + k] for k in range(4)] if pair == 0 else [rest[-4 + k] for k in range(4)]
    index_x = lax.axis_index("bx")
    index_y = lax.axis_index("by")
    z_first, z_second = node_columns((NODES, 128))
    lane = iota((1, 128), 1)
    klass = (lane % TGT).astype(F32)
    which = lane // TGT
    quads = [[], [], [], [], []]
    merged = [0, 0]
    for number, (along, level) in enumerate(LEVELS):
        before = list(merged)
        merged[along - 1] += 1
        if number // 2 != pair:
            continue
        old = [place(index_x, before[0]), place(index_y, before[1])]
        new = [place(index_x, merged[0]), place(index_y, merged[1])]
        index_d = index_x if along == 1 else index_y
        bit = (index_d >> level) & 1
        for who in range(2):
            side = bit if who == 0 else 1 - bit
            child_first = index_x >> before[0]
            child_second = index_y >> before[1]
            if along == 1:
                child_first = (index_x >> merged[0]) * 2 + side
            else:
                child_second = (index_y >> merged[1]) * 2 + side
            width_first = float(N // 8 * 2 ** before[0])
            width_second = float(N // 16 * 2 ** before[1])
            quads[0].append((child_first.astype(F32) * width_first, width_first))
            quads[1].append((child_second.astype(F32) * width_second, width_second))
            quads[2].append((old[0] + 2.0 * old[1], 0.0))
            quads[3].append((new[0] + 2.0 * new[1], 0.0))
            quads[4].append(((new[0] - old[0]) * (1.0 / 2048.0), (new[1] - old[1]) * (1.0 / 1024.0)))

    def lanes(values):
        out = jnp.zeros((1, 128), F32) + values[0]
        for k in range(1, 4):
            out = jnp.where(which == k, values[k], out)
        return out

    (first_at, first_width), (second_at, second_width), (old_at, _), (new_at, _), (move_first, move_second) = [
        (lanes([q[0] for q in quad]), lanes([q[1] for q in quad])) for quad in quads
    ]
    first = first_at + first_width * z_first
    second = second_at + second_width * z_second
    moved = first * move_first + second * move_second
    phase = root_of(speeds(info_ref, klass, new_at), first, second) - root_of(speeds(info_ref, klass, old_at), first, second)
    values = exact(jnp.concatenate(turn(phase + moved), axis=0))
    for k in range(4):
        spread(values, gamma_refs[k], k)
    if pair == 0:
        mix_ref, speed_ref = rest[-2:]
        order = iota((TGT, 128), 0)
        klass = (order % 16) * 2 + order // 16
        _, wave = turn((klass.astype(F32) + 1.5) * (1.0 / 32.0))
        speed_first = (32.0 + info_ref[0].astype(F32) + info_ref[1].astype(F32) * wave) * (1.0 / 4096.0)
        speed_second = (32.0 + info_ref[2].astype(F32) + info_ref[3].astype(F32) * wave) * (1.0 / 4096.0)
        speed_ref[0] = speed_first
        speed_ref[1] = speed_second
        for number in range(4):
            mix_ref[number] = mix_of(number)


def tables(info, pair, after=()):
    shapes = [jax.ShapeDtypeStruct((2 * NODES, 512), F32)] * 4
    if pair == 0:
        shapes.append(jax.ShapeDtypeStruct((4, 128, 256), BF16))
        shapes.append(jax.ShapeDtypeStruct((2, TGT, 128), F32))
    return pl.pallas_call(
        functools.partial(tables_body, pair),
        out_shape=tuple(shapes),
        in_specs=[pl.BlockSpec(memory_space=pltpu.SMEM)] + anywhere(len(after)),
        out_specs=vmem(len(shapes)),
        name="tables_%d" % pair,
        compiler_params=SMALL,
        cost_estimate=cost(0.8),
    )(info, *after)


def last_body(info_ref, *rest):
    last_ref, order_ref = rest[-2:]
    index_x = lax.axis_index("bx")
    index_y = lax.axis_index("by")
    z_first, z_second = node_columns((NODES, 128))
    width_first = float(N // 8 * 4)
    width_second = float(N // 16 * 4)
    first = (index_x >> 2).astype(F32) * width_first + width_first * z_first
    second = (index_y >> 2).astype(F32) * width_second + width_second * z_second
    new = [place(index_x, 2), place(index_y, 2)]
    lane = iota((1, 128), 1)
    v = lane % 16
    for tile in range(4):
        u = tile * 8 + lane // 16
        klass = ((u + 2 * v) % TGT).astype(F32)
        root = root_of(speeds(info_ref, klass, new[0] + 2.0 * new[1]), first, second)
        root = root - jnp.floor(root)
        at_first = first * ((u.astype(F32) + new[0]) * (1.0 / 2048.0))
        at_first = at_first - jnp.floor(at_first) + root
        for half in range(2):
            at_second = second * ((v.astype(F32) + (16.0 * half + new[1])) * (1.0 / 1024.0))
            cosine, sine = turn(at_first + at_second)
            wide = slice(tile * 256 + half * 128, tile * 256 + half * 128 + 128)
            last_ref[:NODES, wide] = cosine
            last_ref[NODES:, wide] = sine
    source = iota((256, 256), 0)
    target = iota((256, 256), 1)
    wanted = ((target // 16) % 2) * 128 + (target // 32) * 16 + target % 16
    order_ref[...] = jnp.where(source == wanted, 1.0, 0.0).astype(BF16)


def last_tables(info, after):
    return pl.pallas_call(
        last_body,
        out_shape=(jax.ShapeDtypeStruct((2 * NODES, TARGETS), F32), jax.ShapeDtypeStruct((256, 256), BF16)),
        in_specs=[pl.BlockSpec(memory_space=pltpu.SMEM)] + anywhere(len(after)),
        out_specs=vmem(2),
        name="last",
        compiler_params=SMALL,
        cost_estimate=cost(0.8),
    )(info, *after)


def combined(start, group, left, own_ref, other_ref, gamma_refs):
    gcols = slice((start + group) * 128, (start + group) * 128 + 128)
    sides = [[], []]
    for half in range(2):
        cols = slice(group * 256 + half * 128, group * 256 + half * 128 + 128)
        reals, imags = [], []
        for gamma_ref, ref in zip(gamma_refs, (own_ref, other_ref)):
            gr = gamma_ref[:NODES, gcols]
            gi = gamma_ref[NODES:, gcols]
            xr = ref[:NODES, cols]
            xi = ref[NODES:, cols]
            reals.append(split(gr * xr - gi * xi))
            imags.append(split(gr * xi + gi * xr))
        for side, parts in zip(sides, (reals, imags)):
            side.append(jnp.concatenate([parts[0][0], parts[1][0], parts[0][1], parts[1][1]], axis=0))
    out = []
    for side in sides:
        both = jnp.dot(left, jnp.concatenate(side, axis=1), preferred_element_type=F32)
        out.append(both[:NODES] + both[NODES:])
    return out


def merge_body(number, chunk, own_ref, other_ref, gamma_own_ref, gamma_other_ref, mix_ref, *rest):
    start, groups = chunk
    out_ref = rest[-1]
    left = mix_ref[number]
    for group in range(groups):
        real, imag = combined(start, group, left, own_ref, other_ref, (gamma_own_ref, gamma_other_ref))
        cols = slice(group * 256, group * 256 + 256)
        out_ref[:NODES, cols] = real
        out_ref[NODES:, cols] = imag


def merge(number, chunk, own, other, gammas, mix, after=()):
    return pl.pallas_call(
        functools.partial(merge_body, number, chunk),
        out_shape=jax.ShapeDtypeStruct((2 * NODES, 256 * chunk[1]), F32),
        in_specs=vmem(5) + anywhere(len(after)),
        out_specs=vmem(1)[0],
        name="merge_%d_%d" % (number, chunk[0]),
        compiler_params=SMALL,
        cost_estimate=cost(0.2 + 0.2 * chunk[1]),
    )(own, other, *gammas, mix, *after)


def finish_body(chunk, own_ref, other_ref, gamma_own_ref, gamma_other_ref, mix_ref, last_ref, order_ref, *rest):
    start, groups = chunk
    out_ref, wide_ref, sem = rest[-3:]
    left = mix_ref[3]
    for group in range(groups):
        real, imag = combined(start, group, left, own_ref, other_ref, (gamma_own_ref, gamma_other_ref))
        tile = start + group
        cols = slice(tile * 256, tile * 256 + 256)
        cosine = last_ref[:NODES, cols]
        sine = last_ref[NODES:, cols]
        value = jnp.concatenate([cosine * real + sine * imag, cosine * imag - sine * real], axis=0)
        moved = jnp.dot(exact(value), order_ref[...], preferred_element_type=F32)
        moved = moved[:128] + moved[128:256] + moved[256:]
        wide_ref[0, :, group * 256 : group * 256 + 256] = moved[:NODES]
        wide_ref[1, :, group * 256 : group * 256 + 256] = moved[NODES:]
    copy = pltpu.make_async_copy(wide_ref, out_ref.at[:, :, start * 256 : (start + groups) * 256], sem)
    copy.start()
    copy.wait()


def finish(chunk, own, other, gammas, mix, lasts, sofar):
    args = [own, other, *gammas, mix, *lasts]
    specs = vmem(7)
    aliases = {}
    if sofar is not None:
        aliases = {len(args): 0}
        args.append(sofar)
        specs = specs + anywhere(1)
    return pl.pallas_call(
        functools.partial(finish_body, chunk),
        out_shape=jax.ShapeDtypeStruct((2, NODES, TARGETS), F32),
        in_specs=specs,
        out_specs=anywhere(1)[0],
        scratch_shapes=[pltpu.VMEM((2, NODES, 256 * chunk[1]), F32), pltpu.SemaphoreType.DMA],
        input_output_aliases=aliases,
        name="finish_%d" % chunk[0],
        compiler_params=SMALL,
        cost_estimate=cost(0.7 + 0.3 * chunk[1]),
    )(*args)


def swap(value, along, level):
    axis = "bx" if along == 1 else "by"
    return lax.ppermute(value, axis, [(i, i ^ 1 << level) for i in range(lax.axis_size(axis))])


def on_device(point_box, point_offset, point_value, coef):
    owners = lax.axis_size("bx") * lax.axis_size("by")
    info = coef
    sent = pack(point_box.reshape(-1, 128), point_offset, point_value)
    arrived = lax.all_to_all(sent.reshape(owners, 1, -1), ("bx", "by"), split_axis=0, concat_axis=0, tiled=True)
    *gammas, mix, speed = tables(info, 0)
    prepared = prepare(arrived.reshape(owners, -1), speed)

    def exchange(number, c, x):
        return swap(x, *LEVELS[number])

    def join(number, c, x, y, after=()):
        return merge(number, c, x, y, gammas[2 * number : 2 * number + 2], mix, after)

    c0, c1, c2, c3 = CHUNKS
    leaf0 = leaf(c0, prepared, ())
    leaf1 = leaf(c1, prepared, (leaf0,))
    one0 = join(0, c0, leaf0, exchange(0, c0, leaf0))
    leaf2 = leaf(c2, prepared, (one0,))
    one1 = join(0, c1, leaf1, exchange(0, c1, leaf1))
    got0 = exchange(1, c0, one0)
    two0 = join(1, c0, one0, got0)
    leaf3 = leaf(c3, prepared, (one1,))
    one2 = join(0, c2, leaf2, exchange(0, c2, leaf2))
    one3 = join(0, c3, leaf3, exchange(0, c3, leaf3), (two0, one2))
    two1 = join(1, c1, one1, exchange(1, c1, one1))
    gammas += tables(info, 1, (one3, two1))
    y0 = exchange(2, c0, two0)
    y1 = exchange(2, c1, two1)
    three0 = join(2, c0, two0, y0)
    x0 = exchange(3, c0, three0)
    two2 = join(1, c2, one2, exchange(1, c2, one2), (three0,))
    three1 = join(2, c1, two1, y1)
    x1 = exchange(3, c1, three1)
    two3 = join(1, c3, one3, exchange(1, c3, one3), (three1,))
    three2 = join(2, c2, two2, exchange(2, c2, two2), (x0,))
    x2 = exchange(3, c2, three2)
    three3 = join(2, c3, two3, exchange(2, c3, two3), (x0, x1))
    lasts = last_tables(info, (one0,))
    out = None
    for c, x, y in zip(CHUNKS, (three0, three1, three2, three3), (x0, x1, x2, exchange(3, c3, three3))):
        out = finish(c, x, y, gammas[6:], mix, lasts, out)
    return out


def solution(mesh):
    in_specs = (P(("bx", "by"), None), P(None, ("bx", "by")), P(None, ("bx", "by")), P())
    out_specs = P(None, None, ("bx", "by"))
    return jax.shard_map(on_device, mesh=mesh, in_specs=in_specs, out_specs=out_specs, check_vma=False)
```

```python
import functools
import math

import jax
import jax.numpy as jnp
import numpy as np
from jax import lax
from jax.experimental import pallas as pl
from jax.experimental.pallas import tpu as pltpu
from jax.sharding import PartitionSpec as P

N = 16384
ORDER = 8
TGT = 32
CAP = 32
CHUNKS = ((0, 1), (1, 1), (2, 1), (3, 1))
STEP = 1
NODES = ORDER * ORDER
TARGETS = TGT * TGT
F32 = jnp.float32
BF16 = jnp.bfloat16

SIN_C = (3.1415925798055824, -5.167706866167939, 2.550031193519312, -0.5980441939121666, 0.07721838615746283)
COS_C = (0.9999999532476086, -4.934792830619651, 4.058411352862725, -1.3318765680816773, 0.21968961109948903)


def node_table():
    counting = np.arange(ORDER) * 1.0
    return 0.5 - 0.5 * np.cos(np.pi * (2.0 * counting + 1.0) / (2.0 * ORDER))


def horner(coefs, x):
    total = coefs[-1]
    for c in coefs[-2::-1]:
        total = total * x + c
    return total


def turn(phase):
    r = phase - jnp.floor(phase + 0.5)
    x = r * r
    sine = horner(SIN_C, x) * r
    cosine = horner(COS_C, x)
    twice = sine + sine
    return 1.0 - twice * sine, twice * cosine


def split(x):
    high = x.astype(BF16)
    return high, (x - high.astype(F32)).astype(BF16)


def cost(micros):
    return pl.CostEstimate(flops=0, bytes_accessed=int(micros * 3.7e6), transcendentals=0)


def vmem(count):
    return [pl.BlockSpec(memory_space=pltpu.VMEM)] * count


def anywhere(count):
    return [pl.BlockSpec(memory_space=pl.ANY)] * count


SMALL = pltpu.CompilerParams(vmem_limit_bytes=12 << 20)


def iota(shape, axis):
    return lax.broadcasted_iota(jnp.int32, shape, axis)


def nt(a, b):
    return lax.dot_general(a, b, (((1,), (1,)), ((), ())), preferred_element_type=F32)


def pack_body(box_ref, off_ref, val_ref, out_ref):
    blocks = box_ref.shape[0]
    row = iota((128, 128), 0)
    row2 = iota((128, 256), 0)
    col2 = iota((128, 256), 1)
    prefix = jnp.where((row2 < col2) | (col2 >= 128), 1.0, 0.0).astype(BF16)
    same = [row == box_ref[b : b + 1, :] for b in range(blocks)]
    ones = [jnp.where(m, 1.0, 0.0).astype(BF16) for m in same]
    counts = jnp.dot(jnp.concatenate(ones, axis=0), prefix, preferred_element_type=F32)
    slots = iota((CAP, 128), 0).astype(F32)
    carry = jnp.zeros((128, 128), F32)
    wide = []
    for b in range(blocks):
        part = counts[b * 128 : (b + 1) * 128]
        rank = jnp.sum(jnp.where(same[b], part[:, :128] + carry, 0.0), axis=0, keepdims=True)
        carry = carry + part[:, 128:]
        hit = slots == rank
        cols = slice(b * 128, (b + 1) * 128)
        values = [off_ref[0:1, cols].astype(F32), off_ref[1:2, cols].astype(F32), val_ref[0:1, cols], val_ref[1:2, cols]]
        pieces = [[], [], []]
        for v in values:
            rest = v
            for piece in pieces:
                top = rest.astype(BF16).astype(F32)
                rest = rest - top
                piece.append(jnp.where(hit, top, 0.0).astype(BF16))
        wide.append(jnp.concatenate([x for piece in pieces for x in piece], axis=0))
    total = nt(jnp.concatenate(ones, axis=1), jnp.concatenate(wide, axis=1))
    out_ref[...] = total[:, :128] + total[:, 128:256] + total[:, 256:]


def pack(box, offsets, values):
    return pl.pallas_call(
        pack_body,
        out_shape=jax.ShapeDtypeStruct((128, 4 * CAP), F32),
        in_specs=[pl.BlockSpec(memory_space=pltpu.VMEM)] * 3,
        out_specs=pl.BlockSpec(memory_space=pltpu.VMEM),
        name="pack",
        cost_estimate=cost(2.0),
    )(box, offsets, values)


def basis_rows(tau):
    nodes = node_table()
    which = iota((ORDER, 128), 0)
    total = None
    for step in range(1, ORDER):
        other = jnp.zeros((ORDER, 128), F32)
        scale = jnp.zeros((ORDER, 128), F32)
        for t in range(ORDER):
            s = (t + step) % ORDER
            other = jnp.where(which == t, float(nodes[s]), other)
            scale = jnp.where(which == t, float(1.0 / (nodes[t] - nodes[s])), scale)
        factor = (tau - other) * scale
        total = factor if total is None else total * factor
    return total


def prepare_body(rx_ref, speed_ref, *rest):
    l_ref, q_ref, z_ref, xt_ref, trig_ref = rest[-5:]
    width_first, width_second = float(N // 8), float(N // 16)
    corner_first = lax.axis_index("bx").astype(F32) * width_first
    corner_second = lax.axis_index("by").astype(F32) * width_second
    xt_ref[...] = rx_ref[...].T

    order = iota((TGT, 128), 0)
    speed_first = speed_ref[0]
    speed_second = speed_ref[1]
    lin_first = (order // 16 * 2 + 1).astype(F32) * (1.0 / 4096.0)
    lin_second = (order % 16 * 4 + 34).astype(F32) * (1.0 / 4096.0)
    power = iota((16, 128), 0).astype(F32) * (1.0 / 1024.0)

    second_all = xt_ref[CAP : 2 * CAP, :] + corner_second
    cosine, sine = turn(second_all * (1.0 / 128.0))
    trig_ref[0] = cosine
    trig_ref[1] = sine
    trig_ref[2] = 1.0 - 2.0 * sine * sine
    trig_ref[3] = 2.0 * cosine * sine

    for s in range(CAP):
        off_first = xt_ref[s : s + 1, :]
        off_second = xt_ref[CAP + s : CAP + s + 1, :]
        real_in = xt_ref[2 * CAP + s : 2 * CAP + s + 1, :]
        imag_in = xt_ref[3 * CAP + s : 3 * CAP + s + 1, :]
        wrap_real = trig_ref[2, s : s + 1, :]
        wrap_imag = trig_ref[3, s : s + 1, :]
        first = off_first + corner_first
        second = off_second + corner_second
        a = speed_first * first
        b = speed_second * second
        root = jnp.sqrt(1.0 + a * a + b * b)
        root = root - jnp.floor(root)
        lin = lin_first * first + lin_second * second
        cosine, sine = turn(root + (lin - jnp.floor(lin)))
        more_cosine = cosine * wrap_real - sine * wrap_imag
        more_sine = cosine * wrap_imag + sine * wrap_real
        for eps in range(2):
            rows = slice(eps * 16, eps * 16 + 16)
            q_ref[s, 2 * eps, :16] = cosine[rows]
            q_ref[s, 2 * eps, 16:] = more_cosine[rows]
            q_ref[s, 2 * eps + 1, :16] = sine[rows]
            q_ref[s, 2 * eps + 1, 16:] = more_sine[rows]
        cosine, sine = turn(power * (first - second))
        z_ref[s, 0] = cosine * real_in - sine * imag_in
        z_ref[s, 1] = cosine * imag_in + sine * real_in
        cols = slice(s * 128, s * 128 + 128)
        first_rows = basis_rows(off_first * (1.0 / width_first))
        second_rows = basis_rows(off_second * (1.0 / width_second))
        for part in range(2):
            scaled = second_rows * trig_ref[part, s : s + 1, :]
            for t in range(0, ORDER, 2):
                pair = jnp.concatenate([first_rows[t : t + 1] * scaled, first_rows[t + 1 : t + 2] * scaled], axis=0)
                high, low = split(pair)
                base = part * NODES + t * ORDER
                l_ref[base : base + 16, cols] = high
                l_ref[128 + base : 128 + base + 16, cols] = low


def prepare(arrived, speed):
    return pl.pallas_call(
        prepare_body,
        out_shape=(
            jax.ShapeDtypeStruct((256, CAP * 128), BF16),
            jax.ShapeDtypeStruct((CAP, 4, TGT, 128), F32),
            jax.ShapeDtypeStruct((CAP, 2, 16, 128), F32),
        ),
        in_specs=vmem(2),
        out_specs=vmem(3),
        scratch_shapes=[pltpu.VMEM((128, 128), F32), pltpu.VMEM((4, CAP, 128), F32)],
        name="prepare",
        compiler_params=SMALL,
        cost_estimate=cost(2.0),
    )(arrived, speed)


def leaf_body(chunk, l_ref, q_ref, z_ref, *rest):
    start, groups = chunk
    out_ref, ra_ref, rb_ref, acc_ref = rest[-4:]
    half = STEP * 128

    def build(step, r_ref):
        for j in range(STEP):
            s = step * STEP + j
            cols = slice(j * 128, j * 128 + 128)
            low_cols = slice(half + j * 128, half + j * 128 + 128)
            for local in range(4 * groups):
                up = start * 4 + local
                zr = z_ref[s, 0, up : up + 1, :]
                zi = z_ref[s, 1, up : up + 1, :]
                for eps in range(2):
                    qr = q_ref[s, 2 * eps, up : up + 16, :]
                    qi = q_ref[s, 2 * eps + 1, up : up + 16, :]
                    for part, value in enumerate((qr * zr - qi * zi, qr * zi + qi * zr)):
                        high, low = split(value)
                        base = (local // 4) * 256 + part * 128 + (2 * (local % 4) + eps) * 16
                        r_ref[base : base + 16, cols] = high
                        r_ref[base : base + 16, low_cols] = low

    steps = CAP // STEP
    build(0, ra_ref)
    for step in range(steps):
        now, later = (ra_ref, rb_ref) if step % 2 == 0 else (rb_ref, ra_ref)
        if step + 1 < steps:
            build(step + 1, later)
        right = l_ref[:, step * half : step * half + half]
        product = nt(now[...], jnp.concatenate([right, right], axis=1))
        if step == 0:
            acc_ref[...] = product
        else:
            acc_ref[...] += product

    for g in range(groups):
        blocks = []
        for part in range(2):
            rows = slice(g * 256 + part * 128, g * 256 + part * 128 + 128)
            blocks.append((acc_ref[rows, :128] + acc_ref[rows, 128:]).T)
        (cr, sr), (ci, si) = [(x[:NODES], x[NODES:]) for x in blocks]
        low_cols = slice(g * 256, g * 256 + 128)
        high_cols = slice(g * 256 + 128, g * 256 + 256)
        out_ref[:NODES, low_cols] = cr + si
        out_ref[NODES:, low_cols] = ci - sr
        out_ref[:NODES, high_cols] = cr - si
        out_ref[NODES:, high_cols] = ci + sr


def leaf(chunk, prepared, after):
    lanes = 256 * chunk[1]
    return pl.pallas_call(
        functools.partial(leaf_body, chunk),
        out_shape=jax.ShapeDtypeStruct((2 * NODES, lanes), F32),
        in_specs=vmem(3) + anywhere(len(after)),
        out_specs=vmem(1)[0],
        scratch_shapes=[
            pltpu.VMEM((lanes, STEP * 256), BF16),
            pltpu.VMEM((lanes, STEP * 256), BF16),
            pltpu.VMEM((lanes, 256), F32),
        ],
        name="leaf_%d" % chunk[0],
        compiler_params=SMALL,
        cost_estimate=cost(2.3 * chunk[1]),
    )(*prepared, *after)


def place(index, merged):
    code = jnp.int32(0)
    for bit in range(merged):
        code = code + ((index >> bit) & 1) * 2 ** (merged - 1 - bit)
    return (code.astype(F32) + 0.5) * (1.0 / 2.0**merged)


def node_columns(shape):
    nodes = node_table()
    row = iota(shape, 0)
    first = jnp.zeros(shape, F32)
    second = jnp.zeros(shape, F32)
    for t in range(ORDER):
        first = jnp.where(row // ORDER == t, float(nodes[t]), first)
        second = jnp.where(row % ORDER == t, float(nodes[t]), second)
    return first, second


def speeds(coefs, klass, at):
    _, wave = turn((klass + at) * (1.0 / 32.0))
    one = (32.0 + coefs[0] + coefs[1] * wave) * (1.0 / 4096.0)
    two = (32.0 + coefs[2] + coefs[3] * wave) * (1.0 / 4096.0)
    return one, two


def root_of(speed, first, second):
    a = speed[0] * first
    b = speed[1] * second
    return jnp.sqrt(1.0 + a * a + b * b)


LEVELS = ((1, 0), (2, 0), (1, 1), (2, 1))


def exact(x):
    high = x.astype(BF16)
    mid, low = split(x - high.astype(F32))
    return jnp.concatenate([high, mid, low], axis=0)


def spread(values, out_ref, columns):
    klass = iota((TGT * 4, 512), 0)
    lane = iota((TGT * 4, 512), 1)
    pick = jnp.where(klass == (lane // 16 + 2 * (lane % 16)) % TGT + TGT * columns, 1.0, 0.0).astype(BF16)
    moved = jnp.dot(values, pick, preferred_element_type=F32)
    rows = 2 * NODES
    out_ref[...] = moved[:rows] + moved[rows : 2 * rows] + moved[2 * rows :]


def mix_of(number):
    along, level = LEVELS[number]
    bit = (lax.axis_index("bx" if along == 1 else "by") >> level) & 1
    nodes = node_table()
    lane = iota((1, 128), 1)
    who = lane // NODES
    first = lane // ORDER % ORDER
    second = lane % ORDER
    source = first if along == 1 else second
    at = jnp.zeros((1, 128), F32)
    for t in range(ORDER):
        at = jnp.where(source == t, float(nodes[t]), at)
    side = jnp.where(who == 0, bit, 1 - bit).astype(F32)
    rows = basis_rows((at + side) * 0.5)
    row = iota((ORDER, 128), 0)
    full = []
    for t in range(ORDER):
        if along == 1:
            full.append(jnp.where(row == second, rows[t : t + 1], 0.0))
        else:
            full.append(jnp.where(first == t, rows, 0.0))
    high, low = split(jnp.concatenate(full, axis=0))
    top = jnp.concatenate([high, high], axis=1)
    bottom = jnp.concatenate([low, jnp.zeros_like(low)], axis=1)
    return jnp.concatenate([top, bottom], axis=0)


def tables_body(pair, coef_ref, *rest):
    gamma_refs = [rest[-7 + k] for k in range(4)] if pair == 0 else [rest[-4 + k] for k in range(4)]
    coefs = [coef_ref[k].astype(F32) for k in range(4)] if pair == 0 else [coef_ref[k : k + 1] for k in range(4)]
    index_x = lax.axis_index("bx")
    index_y = lax.axis_index("by")
    z_first, z_second = node_columns((NODES, 128))
    lane = iota((1, 128), 1)
    klass = (lane % TGT).astype(F32)
    which = lane // TGT
    quads = [[], [], [], [], []]
    merged = [0, 0]
    for number, (along, level) in enumerate(LEVELS):
        before = list(merged)
        merged[along - 1] += 1
        if number // 2 != pair:
            continue
        old = [place(index_x, before[0]), place(index_y, before[1])]
        new = [place(index_x, merged[0]), place(index_y, merged[1])]
        index_d = index_x if along == 1 else index_y
        bit = (index_d >> level) & 1
        for who in range(2):
            side = bit if who == 0 else 1 - bit
            child_first = index_x >> before[0]
            child_second = index_y >> before[1]
            if along == 1:
                child_first = (index_x >> merged[0]) * 2 + side
            else:
                child_second = (index_y >> merged[1]) * 2 + side
            width_first = float(N // 8 * 2 ** before[0])
            width_second = float(N // 16 * 2 ** before[1])
            quads[0].append((child_first.astype(F32) * width_first, width_first))
            quads[1].append((child_second.astype(F32) * width_second, width_second))
            quads[2].append((old[0] + 2.0 * old[1], 0.0))
            quads[3].append((new[0] + 2.0 * new[1], 0.0))
            quads[4].append(((new[0] - old[0]) * (1.0 / 2048.0), (new[1] - old[1]) * (1.0 / 1024.0)))

    def lanes(values):
        out = jnp.zeros((1, 128), F32) + values[0]
        for k in range(1, 4):
            out = jnp.where(which == k, values[k], out)
        return out

    (first_at, first_width), (second_at, second_width), (old_at, _), (new_at, _), (move_first, move_second) = [
        (lanes([q[0] for q in quad]), lanes([q[1] for q in quad])) for quad in quads
    ]
    first = first_at + first_width * z_first
    second = second_at + second_width * z_second
    moved = first * move_first + second * move_second
    phase = root_of(speeds(coefs, klass, new_at), first, second) - root_of(speeds(coefs, klass, old_at), first, second)
    values = exact(jnp.concatenate(turn(phase + moved), axis=0))
    for k in range(4):
        spread(values, gamma_refs[k], k)
    if pair == 0:
        mix_ref, speed_ref, copied_ref = rest[-3:]
        for k in range(4):
            copied_ref[k : k + 1] = jnp.zeros((1, 128), F32) + coefs[k]
        copied_ref[4:] = jnp.zeros((4, 128), F32)
        order = iota((TGT, 128), 0)
        klass = (order % 16) * 2 + order // 16
        _, wave = turn((klass.astype(F32) + 1.5) * (1.0 / 32.0))
        speed_first = (32.0 + coefs[0] + coefs[1] * wave) * (1.0 / 4096.0)
        speed_second = (32.0 + coefs[2] + coefs[3] * wave) * (1.0 / 4096.0)
        speed_ref[0] = speed_first
        speed_ref[1] = speed_second
        for number in range(4):
            mix_ref[number] = mix_of(number)


def tables(info, pair, after=()):
    shapes = [jax.ShapeDtypeStruct((2 * NODES, 512), F32)] * 4
    if pair == 0:
        shapes.append(jax.ShapeDtypeStruct((4, 128, 256), BF16))
        shapes.append(jax.ShapeDtypeStruct((2, TGT, 128), F32))
        shapes.append(jax.ShapeDtypeStruct((ORDER, 128), F32))
    return pl.pallas_call(
        functools.partial(tables_body, pair),
        out_shape=tuple(shapes),
        in_specs=[pl.BlockSpec(memory_space=pltpu.SMEM) if pair == 0 else vmem(1)[0]] + anywhere(len(after)),
        out_specs=vmem(len(shapes)),
        name="tables_%d" % pair,
        compiler_params=SMALL,
        cost_estimate=cost(0.8),
    )(info, *after)


def last_body(coef_ref, *rest):
    last_ref, order_ref = rest[-2:]
    coefs = [coef_ref[k : k + 1] for k in range(4)]
    index_x = lax.axis_index("bx")
    index_y = lax.axis_index("by")
    z_first, z_second = node_columns((NODES, 128))
    width_first = float(N // 8 * 4)
    width_second = float(N // 16 * 4)
    first = (index_x >> 2).astype(F32) * width_first + width_first * z_first
    second = (index_y >> 2).astype(F32) * width_second + width_second * z_second
    new = [place(index_x, 2), place(index_y, 2)]
    lane = iota((1, 128), 1)
    v = lane % 16
    for tile in range(4):
        u = tile * 8 + lane // 16
        klass = ((u + 2 * v) % TGT).astype(F32)
        root = root_of(speeds(coefs, klass, new[0] + 2.0 * new[1]), first, second)
        root = root - jnp.floor(root)
        at_first = first * ((u.astype(F32) + new[0]) * (1.0 / 2048.0))
        at_first = at_first - jnp.floor(at_first) + root
        for half in range(2):
            at_second = second * ((v.astype(F32) + (16.0 * half + new[1])) * (1.0 / 1024.0))
            cosine, sine = turn(at_first + at_second)
            wide = slice(tile * 256 + half * 128, tile * 256 + half * 128 + 128)
            last_ref[:NODES, wide] = cosine
            last_ref[NODES:, wide] = sine
    source = iota((256, 256), 0)
    target = iota((256, 256), 1)
    wanted = ((target // 16) % 2) * 128 + (target // 32) * 16 + target % 16
    order_ref[...] = jnp.where(source == wanted, 1.0, 0.0).astype(BF16)


def last_tables(info, after):
    return pl.pallas_call(
        last_body,
        out_shape=(jax.ShapeDtypeStruct((2 * NODES, TARGETS), F32), jax.ShapeDtypeStruct((256, 256), BF16)),
        in_specs=vmem(1) + anywhere(len(after)),
        out_specs=vmem(2),
        name="last",
        compiler_params=SMALL,
        cost_estimate=cost(0.8),
    )(info, *after)


def combined(start, group, left, own_ref, other_ref, gamma_refs):
    gcols = slice((start + group) * 128, (start + group) * 128 + 128)
    sides = [[], []]
    for half in range(2):
        cols = slice(group * 256 + half * 128, group * 256 + half * 128 + 128)
        reals, imags = [], []
        for gamma_ref, ref in zip(gamma_refs, (own_ref, other_ref)):
            gr = gamma_ref[:NODES, gcols]
            gi = gamma_ref[NODES:, gcols]
            xr = ref[:NODES, cols]
            xi = ref[NODES:, cols]
            reals.append(split(gr * xr - gi * xi))
            imags.append(split(gr * xi + gi * xr))
        for side, parts in zip(sides, (reals, imags)):
            side.append(jnp.concatenate([parts[0][0], parts[1][0], parts[0][1], parts[1][1]], axis=0))
    out = []
    for side in sides:
        both = jnp.dot(left, jnp.concatenate(side, axis=1), preferred_element_type=F32)
        out.append(both[:NODES] + both[NODES:])
    return out


def merge_body(number, chunk, own_ref, other_ref, gamma_own_ref, gamma_other_ref, mix_ref, *rest):
    start, groups = chunk
    out_ref = rest[-1]
    left = mix_ref[number]
    for group in range(groups):
        real, imag = combined(start, group, left, own_ref, other_ref, (gamma_own_ref, gamma_other_ref))
        cols = slice(group * 256, group * 256 + 256)
        out_ref[:NODES, cols] = real
        out_ref[NODES:, cols] = imag


def merge(number, chunk, own, other, gammas, mix, after=()):
    return pl.pallas_call(
        functools.partial(merge_body, number, chunk),
        out_shape=jax.ShapeDtypeStruct((2 * NODES, 256 * chunk[1]), F32),
        in_specs=vmem(5) + anywhere(len(after)),
        out_specs=vmem(1)[0],
        name="merge_%d_%d" % (number, chunk[0]),
        compiler_params=SMALL,
        cost_estimate=cost(0.2 + 0.2 * chunk[1]),
    )(own, other, *gammas, mix, *after)


def finish_body(chunk, own_ref, other_ref, gamma_own_ref, gamma_other_ref, mix_ref, last_ref, order_ref, *rest):
    start, groups = chunk
    out_ref, wide_ref, sem = rest[-3:]
    left = mix_ref[3]
    for group in range(groups):
        real, imag = combined(start, group, left, own_ref, other_ref, (gamma_own_ref, gamma_other_ref))
        tile = start + group
        cols = slice(tile * 256, tile * 256 + 256)
        cosine = last_ref[:NODES, cols]
        sine = last_ref[NODES:, cols]
        value = jnp.concatenate([cosine * real + sine * imag, cosine * imag - sine * real], axis=0)
        moved = jnp.dot(exact(value), order_ref[...], preferred_element_type=F32)
        moved = moved[:128] + moved[128:256] + moved[256:]
        wide_ref[0, :, group * 256 : group * 256 + 256] = moved[:NODES]
        wide_ref[1, :, group * 256 : group * 256 + 256] = moved[NODES:]
    copy = pltpu.make_async_copy(wide_ref, out_ref.at[:, :, start * 256 : (start + groups) * 256], sem)
    copy.start()
    copy.wait()


def finish(chunk, own, other, gammas, mix, lasts, sofar):
    args = [own, other, *gammas, mix, *lasts]
    specs = vmem(7)
    aliases = {}
    if sofar is not None:
        aliases = {len(args): 0}
        args.append(sofar)
        specs = specs + anywhere(1)
    return pl.pallas_call(
        functools.partial(finish_body, chunk),
        out_shape=jax.ShapeDtypeStruct((2, NODES, TARGETS), F32),
        in_specs=specs,
        out_specs=anywhere(1)[0],
        scratch_shapes=[pltpu.VMEM((2, NODES, 256 * chunk[1]), F32), pltpu.SemaphoreType.DMA],
        input_output_aliases=aliases,
        name="finish_%d" % chunk[0],
        compiler_params=SMALL,
        cost_estimate=cost(0.7 + 0.3 * chunk[1]),
    )(*args)


def swap(value, along, level):
    axis = "bx" if along == 1 else "by"
    return lax.ppermute(value, axis, [(i, i ^ 1 << level) for i in range(lax.axis_size(axis))])


def on_device(point_box, point_offset, point_value, coef):
    owners = lax.axis_size("bx") * lax.axis_size("by")
    info = coef
    sent = pack(point_box.reshape(-1, 128), point_offset, point_value)
    arrived = lax.all_to_all(sent.reshape(owners, 1, -1), ("bx", "by"), split_axis=0, concat_axis=0, tiled=True)
    *gammas, mix, speed, copied = tables(info, 0)
    prepared = prepare(arrived.reshape(owners, -1), speed)

    def exchange(number, c, x):
        return swap(x, *LEVELS[number])

    def join(number, c, x, y, after=()):
        return merge(number, c, x, y, gammas[2 * number : 2 * number + 2], mix, after)

    c0, c1, c2, c3 = CHUNKS
    leaf0 = leaf(c0, prepared, ())
    leaf1 = leaf(c1, prepared, (leaf0,))
    one0 = join(0, c0, leaf0, exchange(0, c0, leaf0))
    leaf2 = leaf(c2, prepared, (one0,))
    one1 = join(0, c1, leaf1, exchange(0, c1, leaf1))
    got0 = exchange(1, c0, one0)
    two0 = join(1, c0, one0, got0)
    leaf3 = leaf(c3, prepared, (one1,))
    one2 = join(0, c2, leaf2, exchange(0, c2, leaf2))
    one3 = join(0, c3, leaf3, exchange(0, c3, leaf3), (two0, one2))
    two1 = join(1, c1, one1, exchange(1, c1, one1))
    gammas += tables(copied, 1, (one3, two1))
    y0 = exchange(2, c0, two0)
    y1 = exchange(2, c1, two1)
    three0 = join(2, c0, two0, y0)
    x0 = exchange(3, c0, three0)
    two2 = join(1, c2, one2, exchange(1, c2, one2), (three0,))
    three1 = join(2, c1, two1, y1)
    x1 = exchange(3, c1, three1)
    two3 = join(1, c3, one3, exchange(1, c3, one3), (three1,))
    three2 = join(2, c2, two2, exchange(2, c2, two2), (x0,))
    x2 = exchange(3, c2, three2)
    three3 = join(2, c3, two3, exchange(2, c3, two3), (x0, x1))
    lasts = last_tables(copied, (one0,))
    out = None
    for c, x, y in zip(CHUNKS, (three0, three1, three2, three3), (x0, x1, x2, exchange(3, c3, three3))):
        out = finish(c, x, y, gammas[6:], mix, lasts, out)
    return out


def solution(mesh):
    in_specs = (P(("bx", "by"), None), P(None, ("bx", "by")), P(None, ("bx", "by")), P())
    out_specs = P(None, None, ("bx", "by"))
    return jax.shard_map(on_device, mesh=mesh, in_specs=in_specs, out_specs=out_specs, check_vma=False)
```

```python
import functools
import math

import jax
import jax.numpy as jnp
import numpy as np
from jax import lax
from jax.experimental import pallas as pl
from jax.experimental.pallas import tpu as pltpu
from jax.sharding import PartitionSpec as P

N = 16384
ORDER = 8
TGT = 32
CAP = 32
CHUNKS = ((0, 1), (1, 1), (2, 1), (3, 1))
STEP = 1
NODES = ORDER * ORDER
TARGETS = TGT * TGT
F32 = jnp.float32
BF16 = jnp.bfloat16

SIN_C = (3.1415925798055824, -5.167706866167939, 2.550031193519312, -0.5980441939121666, 0.07721838615746283)
COS_C = (0.9999999532476086, -4.934792830619651, 4.058411352862725, -1.3318765680816773, 0.21968961109948903)


def node_table():
    counting = np.arange(ORDER) * 1.0
    return 0.5 - 0.5 * np.cos(np.pi * (2.0 * counting + 1.0) / (2.0 * ORDER))


def horner(coefs, x):
    total = coefs[-1]
    for c in coefs[-2::-1]:
        total = total * x + c
    return total


def turn(phase):
    r = phase - jnp.floor(phase + 0.5)
    x = r * r
    sine = horner(SIN_C, x) * r
    cosine = horner(COS_C, x)
    twice = sine + sine
    return 1.0 - twice * sine, twice * cosine


def split(x):
    high = x.astype(BF16)
    return high, (x - high.astype(F32)).astype(BF16)


def cost(micros):
    return pl.CostEstimate(flops=0, bytes_accessed=int(micros * 3.7e6), transcendentals=0)


def vmem(count):
    return [pl.BlockSpec(memory_space=pltpu.VMEM)] * count


def anywhere(count):
    return [pl.BlockSpec(memory_space=pl.ANY)] * count


SMALL = pltpu.CompilerParams(vmem_limit_bytes=12 << 20)


def iota(shape, axis):
    return lax.broadcasted_iota(jnp.int32, shape, axis)


def nt(a, b):
    return lax.dot_general(a, b, (((1,), (1,)), ((), ())), preferred_element_type=F32)


def pack_body(box_ref, off_ref, val_ref, out_ref):
    blocks = box_ref.shape[0]
    row = iota((128, 128), 0)
    row2 = iota((128, 256), 0)
    col2 = iota((128, 256), 1)
    prefix = jnp.where((row2 < col2) | (col2 >= 128), 1.0, 0.0).astype(BF16)
    same = [row == box_ref[b : b + 1, :] for b in range(blocks)]
    ones = [jnp.where(m, 1.0, 0.0).astype(BF16) for m in same]
    counts = jnp.dot(jnp.concatenate(ones, axis=0), prefix, preferred_element_type=F32)
    slots = iota((CAP, 128), 0).astype(F32)
    carry = jnp.zeros((128, 128), F32)
    wide = []
    for b in range(blocks):
        part = counts[b * 128 : (b + 1) * 128]
        rank = jnp.sum(jnp.where(same[b], part[:, :128] + carry, 0.0), axis=0, keepdims=True)
        carry = carry + part[:, 128:]
        hit = slots == rank
        cols = slice(b * 128, (b + 1) * 128)
        values = [off_ref[0:1, cols].astype(F32), off_ref[1:2, cols].astype(F32), val_ref[0:1, cols], val_ref[1:2, cols]]
        pieces = [[], [], []]
        for index, v in enumerate(values):
            rest = v
            for piece in pieces if index > 1 else pieces[:2]:
                top = rest.astype(BF16).astype(F32)
                rest = rest - top
                piece.append(jnp.where(hit, top, 0.0).astype(BF16))
        wide.append(jnp.concatenate([x for piece in pieces for x in piece], axis=0))
    total = nt(jnp.concatenate(ones, axis=1), jnp.concatenate(wide, axis=1))
    out_ref[:, :64] = total[:, :64] + total[:, 128:192]
    out_ref[:, 64:] = total[:, 64:128] + total[:, 192:256] + total[:, 256:]


def pack(box, offsets, values):
    return pl.pallas_call(
        pack_body,
        out_shape=jax.ShapeDtypeStruct((128, 4 * CAP), F32),
        in_specs=[pl.BlockSpec(memory_space=pltpu.VMEM)] * 3,
        out_specs=pl.BlockSpec(memory_space=pltpu.VMEM),
        name="pack",
        cost_estimate=cost(2.0),
    )(box, offsets, values)


def basis_rows(tau):
    nodes = node_table()
    which = iota((ORDER, 128), 0)
    total = None
    for step in range(1, ORDER):
        other = jnp.zeros((ORDER, 128), F32)
        scale = jnp.zeros((ORDER, 128), F32)
        for t in range(ORDER):
            s = (t + step) % ORDER
            other = jnp.where(which == t, float(nodes[s]), other)
            scale = jnp.where(which == t, float(1.0 / (nodes[t] - nodes[s])), scale)
        factor = (tau - other) * scale
        total = factor if total is None else total * factor
    return total


def prepare_body(rx_ref, speed_ref, *rest):
    l_ref, q_ref, z_ref, xt_ref, trig_ref = rest[-5:]
    width_first, width_second = float(N // 8), float(N // 16)
    corner_first = lax.axis_index("bx").astype(F32) * width_first
    corner_second = lax.axis_index("by").astype(F32) * width_second
    xt_ref[...] = rx_ref[...].T

    order = iota((TGT, 128), 0)
    speed_first = speed_ref[0]
    speed_second = speed_ref[1]
    lin_first = (order // 16 * 2 + 1).astype(F32) * (1.0 / 4096.0)
    lin_second = (order % 16 * 4 + 34).astype(F32) * (1.0 / 4096.0)
    power = iota((16, 128), 0).astype(F32) * (1.0 / 1024.0)

    second_all = xt_ref[CAP : 2 * CAP, :] + corner_second
    cosine, sine = turn(second_all * (1.0 / 128.0))
    trig_ref[0] = cosine
    trig_ref[1] = sine
    trig_ref[2] = 1.0 - 2.0 * sine * sine
    trig_ref[3] = 2.0 * cosine * sine

    for s in range(CAP):
        off_first = xt_ref[s : s + 1, :]
        off_second = xt_ref[CAP + s : CAP + s + 1, :]
        real_in = xt_ref[2 * CAP + s : 2 * CAP + s + 1, :]
        imag_in = xt_ref[3 * CAP + s : 3 * CAP + s + 1, :]
        wrap_real = trig_ref[2, s : s + 1, :]
        wrap_imag = trig_ref[3, s : s + 1, :]
        first = off_first + corner_first
        second = off_second + corner_second
        a = speed_first * first
        b = speed_second * second
        root = jnp.sqrt(1.0 + a * a + b * b)
        root = root - jnp.floor(root)
        lin = lin_first * first + lin_second * second
        cosine, sine = turn(root + (lin - jnp.floor(lin)))
        more_cosine = cosine * wrap_real - sine * wrap_imag
        more_sine = cosine * wrap_imag + sine * wrap_real
        for eps in range(2):
            rows = slice(eps * 16, eps * 16 + 16)
            q_ref[s, 2 * eps, :16] = cosine[rows]
            q_ref[s, 2 * eps, 16:] = more_cosine[rows]
            q_ref[s, 2 * eps + 1, :16] = sine[rows]
            q_ref[s, 2 * eps + 1, 16:] = more_sine[rows]
        cosine, sine = turn(power * (first - second))
        z_ref[s, 0] = cosine * real_in - sine * imag_in
        z_ref[s, 1] = cosine * imag_in + sine * real_in
        cols = slice(s * 128, s * 128 + 128)
        first_rows = basis_rows(off_first * (1.0 / width_first))
        second_rows = basis_rows(off_second * (1.0 / width_second))
        for part in range(2):
            scaled = second_rows * trig_ref[part, s : s + 1, :]
            for t in range(0, ORDER, 2):
                pair = jnp.concatenate([first_rows[t : t + 1] * scaled, first_rows[t + 1 : t + 2] * scaled], axis=0)
                high, low = split(pair)
                base = part * NODES + t * ORDER
                l_ref[base : base + 16, cols] = high
                l_ref[128 + base : 128 + base + 16, cols] = low


def prepare(arrived, speed):
    return pl.pallas_call(
        prepare_body,
        out_shape=(
            jax.ShapeDtypeStruct((256, CAP * 128), BF16),
            jax.ShapeDtypeStruct((CAP, 4, TGT, 128), F32),
            jax.ShapeDtypeStruct((CAP, 2, 16, 128), F32),
        ),
        in_specs=vmem(2),
        out_specs=vmem(3),
        scratch_shapes=[pltpu.VMEM((128, 128), F32), pltpu.VMEM((4, CAP, 128), F32)],
        name="prepare",
        compiler_params=SMALL,
        cost_estimate=cost(2.0),
    )(arrived, speed)


def leaf_body(chunk, l_ref, q_ref, z_ref, *rest):
    start, groups = chunk
    out_ref, ra_ref, rb_ref, acc_ref = rest[-4:]
    half = STEP * 128

    def build(step, r_ref):
        for j in range(STEP):
            s = step * STEP + j
            cols = slice(j * 128, j * 128 + 128)
            low_cols = slice(half + j * 128, half + j * 128 + 128)
            for local in range(4 * groups):
                up = start * 4 + local
                zr = z_ref[s, 0, up : up + 1, :]
                zi = z_ref[s, 1, up : up + 1, :]
                for eps in range(2):
                    qr = q_ref[s, 2 * eps, up : up + 16, :]
                    qi = q_ref[s, 2 * eps + 1, up : up + 16, :]
                    for part, value in enumerate((qr * zr - qi * zi, qr * zi + qi * zr)):
                        high, low = split(value)
                        base = (local // 4) * 256 + part * 128 + (2 * (local % 4) + eps) * 16
                        r_ref[base : base + 16, cols] = high
                        r_ref[base : base + 16, low_cols] = low

    steps = CAP // STEP
    build(0, ra_ref)
    for step in range(steps):
        now, later = (ra_ref, rb_ref) if step % 2 == 0 else (rb_ref, ra_ref)
        if step + 1 < steps:
            build(step + 1, later)
        right = l_ref[:, step * half : step * half + half]
        product = nt(now[...], jnp.concatenate([right, right], axis=1))
        if step == 0:
            acc_ref[...] = product
        else:
            acc_ref[...] += product

    for g in range(groups):
        blocks = []
        for part in range(2):
            rows = slice(g * 256 + part * 128, g * 256 + part * 128 + 128)
            blocks.append((acc_ref[rows, :128] + acc_ref[rows, 128:]).T)
        (cr, sr), (ci, si) = [(x[:NODES], x[NODES:]) for x in blocks]
        low_cols = slice(g * 256, g * 256 + 128)
        high_cols = slice(g * 256 + 128, g * 256 + 256)
        out_ref[:NODES, low_cols] = cr + si
        out_ref[NODES:, low_cols] = ci - sr
        out_ref[:NODES, high_cols] = cr - si
        out_ref[NODES:, high_cols] = ci + sr


def leaf(chunk, prepared, after):
    lanes = 256 * chunk[1]
    return pl.pallas_call(
        functools.partial(leaf_body, chunk),
        out_shape=jax.ShapeDtypeStruct((2 * NODES, lanes), F32),
        in_specs=vmem(3) + anywhere(len(after)),
        out_specs=vmem(1)[0],
        scratch_shapes=[
            pltpu.VMEM((lanes, STEP * 256), BF16),
            pltpu.VMEM((lanes, STEP * 256), BF16),
            pltpu.VMEM((lanes, 256), F32),
        ],
        name="leaf_%d" % chunk[0],
        compiler_params=SMALL,
        cost_estimate=cost(2.3 * chunk[1]),
    )(*prepared, *after)


def place(index, merged):
    code = jnp.int32(0)
    for bit in range(merged):
        code = code + ((index >> bit) & 1) * 2 ** (merged - 1 - bit)
    return (code.astype(F32) + 0.5) * (1.0 / 2.0**merged)


def node_columns(shape):
    nodes = node_table()
    row = iota(shape, 0)
    first = jnp.zeros(shape, F32)
    second = jnp.zeros(shape, F32)
    for t in range(ORDER):
        first = jnp.where(row // ORDER == t, float(nodes[t]), first)
        second = jnp.where(row % ORDER == t, float(nodes[t]), second)
    return first, second


def speeds(coefs, klass, at):
    _, wave = turn((klass + at) * (1.0 / 32.0))
    one = (32.0 + coefs[0] + coefs[1] * wave) * (1.0 / 4096.0)
    two = (32.0 + coefs[2] + coefs[3] * wave) * (1.0 / 4096.0)
    return one, two


def root_of(speed, first, second):
    a = speed[0] * first
    b = speed[1] * second
    return jnp.sqrt(1.0 + a * a + b * b)


LEVELS = ((1, 0), (2, 0), (1, 1), (2, 1))


def exact(x):
    high = x.astype(BF16)
    mid, low = split(x - high.astype(F32))
    return jnp.concatenate([high, mid, low], axis=0)


def spread(values, out_ref, columns):
    klass = iota((TGT * 4, 512), 0)
    lane = iota((TGT * 4, 512), 1)
    pick = jnp.where(klass == (lane // 16 + 2 * (lane % 16)) % TGT + TGT * columns, 1.0, 0.0).astype(BF16)
    moved = jnp.dot(values, pick, preferred_element_type=F32)
    rows = 2 * NODES
    out_ref[...] = moved[:rows] + moved[rows : 2 * rows] + moved[2 * rows :]


def mix_of(number):
    along, level = LEVELS[number]
    bit = (lax.axis_index("bx" if along == 1 else "by") >> level) & 1
    nodes = node_table()
    lane = iota((1, 128), 1)
    who = lane // NODES
    first = lane // ORDER % ORDER
    second = lane % ORDER
    source = first if along == 1 else second
    at = jnp.zeros((1, 128), F32)
    for t in range(ORDER):
        at = jnp.where(source == t, float(nodes[t]), at)
    side = jnp.where(who == 0, bit, 1 - bit).astype(F32)
    rows = basis_rows((at + side) * 0.5)
    row = iota((ORDER, 128), 0)
    full = []
    for t in range(ORDER):
        if along == 1:
            full.append(jnp.where(row == second, rows[t : t + 1], 0.0))
        else:
            full.append(jnp.where(first == t, rows, 0.0))
    high, low = split(jnp.concatenate(full, axis=0))
    top = jnp.concatenate([high, high], axis=1)
    bottom = jnp.concatenate([low, jnp.zeros_like(low)], axis=1)
    return jnp.concatenate([top, bottom], axis=0)


def tables_body(pair, coef_ref, *rest):
    gamma_refs = [rest[-7 + k] for k in range(4)] if pair == 0 else [rest[-4 + k] for k in range(4)]
    coefs = [coef_ref[k].astype(F32) for k in range(4)] if pair == 0 else [coef_ref[k : k + 1] for k in range(4)]
    index_x = lax.axis_index("bx")
    index_y = lax.axis_index("by")
    z_first, z_second = node_columns((NODES, 128))
    lane = iota((1, 128), 1)
    klass = (lane % TGT).astype(F32)
    which = lane // TGT
    quads = [[], [], [], [], []]
    merged = [0, 0]
    for number, (along, level) in enumerate(LEVELS):
        before = list(merged)
        merged[along - 1] += 1
        if number // 2 != pair:
            continue
        old = [place(index_x, before[0]), place(index_y, before[1])]
        new = [place(index_x, merged[0]), place(index_y, merged[1])]
        index_d = index_x if along == 1 else index_y
        bit = (index_d >> level) & 1
        for who in range(2):
            side = bit if who == 0 else 1 - bit
            child_first = index_x >> before[0]
            child_second = index_y >> before[1]
            if along == 1:
                child_first = (index_x >> merged[0]) * 2 + side
            else:
                child_second = (index_y >> merged[1]) * 2 + side
            width_first = float(N // 8 * 2 ** before[0])
            width_second = float(N // 16 * 2 ** before[1])
            quads[0].append((child_first.astype(F32) * width_first, width_first))
            quads[1].append((child_second.astype(F32) * width_second, width_second))
            quads[2].append((old[0] + 2.0 * old[1], 0.0))
            quads[3].append((new[0] + 2.0 * new[1], 0.0))
            quads[4].append(((new[0] - old[0]) * (1.0 / 2048.0), (new[1] - old[1]) * (1.0 / 1024.0)))

    def lanes(values):
        out = jnp.zeros((1, 128), F32) + values[0]
        for k in range(1, 4):
            out = jnp.where(which == k, values[k], out)
        return out

    (first_at, first_width), (second_at, second_width), (old_at, _), (new_at, _), (move_first, move_second) = [
        (lanes([q[0] for q in quad]), lanes([q[1] for q in quad])) for quad in quads
    ]
    first = first_at + first_width * z_first
    second = second_at + second_width * z_second
    moved = first * move_first + second * move_second
    phase = root_of(speeds(coefs, klass, new_at), first, second) - root_of(speeds(coefs, klass, old_at), first, second)
    values = exact(jnp.concatenate(turn(phase + moved), axis=0))
    for k in range(4):
        spread(values, gamma_refs[k], k)
    if pair == 0:
        mix_ref, speed_ref, copied_ref = rest[-3:]
        for k in range(4):
            copied_ref[k : k + 1] = jnp.zeros((1, 128), F32) + coefs[k]
        copied_ref[4:] = jnp.zeros((4, 128), F32)
        order = iota((TGT, 128), 0)
        klass = (order % 16) * 2 + order // 16
        _, wave = turn((klass.astype(F32) + 1.5) * (1.0 / 32.0))
        speed_first = (32.0 + coefs[0] + coefs[1] * wave) * (1.0 / 4096.0)
        speed_second = (32.0 + coefs[2] + coefs[3] * wave) * (1.0 / 4096.0)
        speed_ref[0] = speed_first
        speed_ref[1] = speed_second
        for number in range(4):
            mix_ref[number] = mix_of(number)


def tables(info, pair, after=()):
    shapes = [jax.ShapeDtypeStruct((2 * NODES, 512), F32)] * 4
    if pair == 0:
        shapes.append(jax.ShapeDtypeStruct((4, 128, 256), BF16))
        shapes.append(jax.ShapeDtypeStruct((2, TGT, 128), F32))
        shapes.append(jax.ShapeDtypeStruct((ORDER, 128), F32))
    return pl.pallas_call(
        functools.partial(tables_body, pair),
        out_shape=tuple(shapes),
        in_specs=[pl.BlockSpec(memory_space=pltpu.SMEM) if pair == 0 else vmem(1)[0]] + anywhere(len(after)),
        out_specs=vmem(len(shapes)),
        name="tables_%d" % pair,
        compiler_params=SMALL,
        cost_estimate=cost(0.8),
    )(info, *after)


def last_body(coef_ref, *rest):
    last_ref, order_ref = rest[-2:]
    coefs = [coef_ref[k : k + 1] for k in range(4)]
    index_x = lax.axis_index("bx")
    index_y = lax.axis_index("by")
    z_first, z_second = node_columns((NODES, 128))
    width_first = float(N // 8 * 4)
    width_second = float(N // 16 * 4)
    first = (index_x >> 2).astype(F32) * width_first + width_first * z_first
    second = (index_y >> 2).astype(F32) * width_second + width_second * z_second
    new = [place(index_x, 2), place(index_y, 2)]
    lane = iota((1, 128), 1)
    v = lane % 16
    for tile in range(4):
        u = tile * 8 + lane // 16
        klass = ((u + 2 * v) % TGT).astype(F32)
        root = root_of(speeds(coefs, klass, new[0] + 2.0 * new[1]), first, second)
        root = root - jnp.floor(root)
        at_first = first * ((u.astype(F32) + new[0]) * (1.0 / 2048.0))
        at_first = at_first - jnp.floor(at_first) + root
        for half in range(2):
            at_second = second * ((v.astype(F32) + (16.0 * half + new[1])) * (1.0 / 1024.0))
            cosine, sine = turn(at_first + at_second)
            wide = slice(tile * 256 + half * 128, tile * 256 + half * 128 + 128)
            last_ref[:NODES, wide] = cosine
            last_ref[NODES:, wide] = sine
    source = iota((256, 256), 0)
    target = iota((256, 256), 1)
    wanted = ((target // 16) % 2) * 128 + (target // 32) * 16 + target % 16
    order_ref[...] = jnp.where(source == wanted, 1.0, 0.0).astype(BF16)


def last_tables(info, after):
    return pl.pallas_call(
        last_body,
        out_shape=(jax.ShapeDtypeStruct((2 * NODES, TARGETS), F32), jax.ShapeDtypeStruct((256, 256), BF16)),
        in_specs=vmem(1) + anywhere(len(after)),
        out_specs=vmem(2),
        name="last",
        compiler_params=SMALL,
        cost_estimate=cost(0.8),
    )(info, *after)


def combined(start, group, left, own_ref, other_ref, gamma_refs):
    gcols = slice((start + group) * 128, (start + group) * 128 + 128)
    sides = [[], []]
    for half in range(2):
        cols = slice(group * 256 + half * 128, group * 256 + half * 128 + 128)
        reals, imags = [], []
        for gamma_ref, ref in zip(gamma_refs, (own_ref, other_ref)):
            gr = gamma_ref[:NODES, gcols]
            gi = gamma_ref[NODES:, gcols]
            xr = ref[:NODES, cols]
            xi = ref[NODES:, cols]
            reals.append(split(gr * xr - gi * xi))
            imags.append(split(gr * xi + gi * xr))
        for side, parts in zip(sides, (reals, imags)):
            side.append(jnp.concatenate([parts[0][0], parts[1][0], parts[0][1], parts[1][1]], axis=0))
    out = []
    for side in sides:
        both = jnp.dot(left, jnp.concatenate(side, axis=1), preferred_element_type=F32)
        out.append(both[:NODES] + both[NODES:])
    return out


def merge_body(number, chunk, own_ref, other_ref, gamma_own_ref, gamma_other_ref, mix_ref, *rest):
    start, groups = chunk
    out_ref = rest[-1]
    left = mix_ref[number]
    for group in range(groups):
        real, imag = combined(start, group, left, own_ref, other_ref, (gamma_own_ref, gamma_other_ref))
        cols = slice(group * 256, group * 256 + 256)
        out_ref[:NODES, cols] = real
        out_ref[NODES:, cols] = imag


def merge(number, chunk, own, other, gammas, mix, after=()):
    return pl.pallas_call(
        functools.partial(merge_body, number, chunk),
        out_shape=jax.ShapeDtypeStruct((2 * NODES, 256 * chunk[1]), F32),
        in_specs=vmem(5) + anywhere(len(after)),
        out_specs=vmem(1)[0],
        name="merge_%d_%d" % (number, chunk[0]),
        compiler_params=SMALL,
        cost_estimate=cost(0.2 + 0.2 * chunk[1]),
    )(own, other, *gammas, mix, *after)


def finish_body(chunk, own_ref, other_ref, gamma_own_ref, gamma_other_ref, mix_ref, last_ref, order_ref, *rest):
    start, groups = chunk
    out_ref, wide_ref, sem = rest[-3:]
    left = mix_ref[3]
    for group in range(groups):
        real, imag = combined(start, group, left, own_ref, other_ref, (gamma_own_ref, gamma_other_ref))
        tile = start + group
        cols = slice(tile * 256, tile * 256 + 256)
        cosine = last_ref[:NODES, cols]
        sine = last_ref[NODES:, cols]
        value = jnp.concatenate([cosine * real + sine * imag, cosine * imag - sine * real], axis=0)
        moved = jnp.dot(exact(value), order_ref[...], preferred_element_type=F32)
        moved = moved[:128] + moved[128:256] + moved[256:]
        wide_ref[0, :, group * 256 : group * 256 + 256] = moved[:NODES]
        wide_ref[1, :, group * 256 : group * 256 + 256] = moved[NODES:]
    copy = pltpu.make_async_copy(wide_ref, out_ref.at[:, :, start * 256 : (start + groups) * 256], sem)
    copy.start()
    copy.wait()


def finish(chunk, own, other, gammas, mix, lasts, sofar):
    args = [own, other, *gammas, mix, *lasts]
    specs = vmem(7)
    aliases = {}
    if sofar is not None:
        aliases = {len(args): 0}
        args.append(sofar)
        specs = specs + anywhere(1)
    return pl.pallas_call(
        functools.partial(finish_body, chunk),
        out_shape=jax.ShapeDtypeStruct((2, NODES, TARGETS), F32),
        in_specs=specs,
        out_specs=anywhere(1)[0],
        scratch_shapes=[pltpu.VMEM((2, NODES, 256 * chunk[1]), F32), pltpu.SemaphoreType.DMA],
        input_output_aliases=aliases,
        name="finish_%d" % chunk[0],
        compiler_params=SMALL,
        cost_estimate=cost(0.7 + 0.3 * chunk[1]),
    )(*args)


def swap(value, along, level):
    axis = "bx" if along == 1 else "by"
    return lax.ppermute(value, axis, [(i, i ^ 1 << level) for i in range(lax.axis_size(axis))])


def on_device(point_box, point_offset, point_value, coef):
    owners = lax.axis_size("bx") * lax.axis_size("by")
    info = coef
    sent = pack(point_box.reshape(-1, 128), point_offset, point_value)
    arrived = lax.all_to_all(sent.reshape(owners, 1, -1), ("bx", "by"), split_axis=0, concat_axis=0, tiled=True)
    *gammas, mix, speed, copied = tables(info, 0)
    prepared = prepare(arrived.reshape(owners, -1), speed)

    def exchange(number, c, x):
        return swap(x, *LEVELS[number])

    def join(number, c, x, y, after=()):
        return merge(number, c, x, y, gammas[2 * number : 2 * number + 2], mix, after)

    c0, c1, c2, c3 = CHUNKS
    leaf0 = leaf(c0, prepared, ())
    leaf1 = leaf(c1, prepared, (leaf0,))
    one0 = join(0, c0, leaf0, exchange(0, c0, leaf0))
    leaf2 = leaf(c2, prepared, (one0,))
    one1 = join(0, c1, leaf1, exchange(0, c1, leaf1))
    got0 = exchange(1, c0, one0)
    two0 = join(1, c0, one0, got0)
    leaf3 = leaf(c3, prepared, (one1,))
    one2 = join(0, c2, leaf2, exchange(0, c2, leaf2))
    one3 = join(0, c3, leaf3, exchange(0, c3, leaf3), (two0, one2))
    two1 = join(1, c1, one1, exchange(1, c1, one1))
    gammas += tables(copied, 1, (one3, two1))
    y0 = exchange(2, c0, two0)
    y1 = exchange(2, c1, two1)
    three0 = join(2, c0, two0, y0)
    x0 = exchange(3, c0, three0)
    two2 = join(1, c2, one2, exchange(1, c2, one2), (three0,))
    three1 = join(2, c1, two1, y1)
    x1 = exchange(3, c1, three1)
    two3 = join(1, c3, one3, exchange(1, c3, one3), (three1,))
    three2 = join(2, c2, two2, exchange(2, c2, two2), (x0,))
    x2 = exchange(3, c2, three2)
    three3 = join(2, c3, two3, exchange(2, c3, two3), (x0, x1))
    lasts = last_tables(copied, (one0,))
    out = None
    for c, x, y in zip(CHUNKS, (three0, three1, three2, three3), (x0, x1, x2, exchange(3, c3, three3))):
        out = finish(c, x, y, gammas[6:], mix, lasts, out)
    return out


def solution(mesh):
    in_specs = (P(("bx", "by"), None), P(None, ("bx", "by")), P(None, ("bx", "by")), P())
    out_specs = P(None, None, ("bx", "by"))
    return jax.shard_map(on_device, mesh=mesh, in_specs=in_specs, out_specs=out_specs, check_vma=False)
```
